256 devices in a mesh: row: 8 (over x, y_lo), col: 32 (over y_hi, z, core).
Axes of the slice: x: 4, y: 4 (y_hi: 2, y_lo: 2; y = y_hi * 2 + y_lo), z: 8, core: 2. Of those that a mesh axis runs over, the one named last changes fastest.
Arguments:
- features: bfloat16 [65536, 128], P(('row', 'col')), may hold values from -6 to 6
- degrees: int32 [65536], P(('row', 'col')), may hold values from 32 to 159
- adj_tiles: bfloat16 [8, 32, 256, 4096], P('row', 'col'), may hold values from 0 to 0.22472483, as said below
- tile_rows: int32 [8, 32, 256], P('row', 'col'), may hold values from 0 to 127
- tile_cols: int32 [8, 32, 256], P('row', 'col'), may hold values from 0 to 31
- tile_counts: int32 [8, 32], P('row', 'col'), may hold values from 64 to 256, as said below
Outputs:
- propagated: bfloat16 [65536, 128], P(('row', 'col'))
The draws below stay inside these ranges and needn't reach their ends.
Inputs may be any that keep to these rules, and one draw needn't show every extreme that they name: Each block holds at most 256 live tiles, in its first tile_counts slots; some block holds exactly 256. `adj_tiles`: edge weights are zero or positive.
All inputs are finite; a program needn't handle non-finite values.
Results may differ from the reference program's by a relative error of at most 0.0054.
Values may be sent and summed in bfloat16 or wider, within the bound.
A program may use at most 128 MiB of HBM per device.

```python
import jax
import jax.numpy as jnp
from jax import lax

FEAT = 128
TILE = 64
KNN = 32
STEPS = 2
NODES_DEV = 256
TILE_MAX = 256
NODES = 65536
N_ROW = 8
N_COL = 32


def draw_tile_counts(key, part):
    base = jax.random.fold_in(key, 11)
    first_key, second_key = jax.random.split(base)
    drawn = jax.random.randint(first_key, (N_ROW * N_COL,), TILE_MAX // 4, TILE_MAX + 1)
    chosen = jax.random.randint(second_key, (), 0, N_ROW * N_COL)
    drawn = jnp.where(jnp.arange(N_ROW * N_COL) == chosen, TILE_MAX, drawn)
    return drawn.reshape(N_ROW, N_COL).astype(jnp.int32)


def draw_adj_tiles(key, part):
    base = jax.random.fold_in(key, 23)
    mask_key, value_key = jax.random.split(base)
    shape = (N_ROW, N_COL, TILE_MAX, TILE * TILE)
    present = jax.random.uniform(mask_key, shape, jnp.float32) < 1.0 / 32.0
    weight_scale = (NODES_DEV / (TILE_MAX * TILE * TILE / 32.0 * 0.625)) ** 0.5
    values = jax.random.uniform(value_key, shape, jnp.float32, 0.5, 1.5)
    return jnp.where(present, values * weight_scale, 0.0).astype(jnp.bfloat16)


def place_ends(result, own_key, smallest, high):
    longest = result.shape.index(max(result.shape))
    spots = []
    for shift in (0, 1):
        where = [jax.random.randint(jax.random.fold_in(own_key, axis), (), 0, length) for axis, length in enumerate(result.shape)]
        where[longest] = (where[longest] + shift) % result.shape[longest]
        spots.append(tuple(where))
    return result.at[spots[0]].set(smallest).at[spots[1]].set(high)


def levels(own_key, extent, pieces, smallest, largest):
    factor_of = 1.0
    for axis_at, blocks in pieces:
        heights = jax.random.uniform(jax.random.fold_in(jax.random.fold_in(own_key, 6), axis_at), (blocks,), jnp.float32, smallest / len(pieces), largest / len(pieces))
        factor_of = factor_of * jnp.repeat(jnp.exp(heights), extent[axis_at] // blocks).reshape((-1,) + (1,) * (len(extent) - 1 - axis_at))
    return factor_of


def centred(rng, extent, scale, bound, cuts=(), kind=jnp.bfloat16):
    result = scale * jax.random.normal(rng, extent, jnp.float32)
    if cuts:
        result = result * levels(rng, extent, cuts, -0.22, 0.18)
    return jnp.clip(result, -bound, bound).astype(kind)


def setup_inputs(seed: int = 0) -> dict:
    key_list = jax.random.split(jax.random.key(seed), 7)
    features = centred(key_list[0], (NODES, FEAT), 1.0, 6.0, ((0, 256),))
    degrees = place_ends(jax.random.randint(key_list[1], (NODES,), KNN, 5 * KNN), jax.random.fold_in(key_list[1], 1), KNN, (5 * KNN) - 1).astype(jnp.int32)
    adj_tiles = draw_adj_tiles(jax.random.fold_in(key_list[6], 71), 0)
    tile_rows = place_ends(jax.random.randint(key_list[3], (N_ROW, N_COL, TILE_MAX), 0, NODES_DEV * N_COL // TILE), jax.random.fold_in(key_list[3], 1), 0, (NODES_DEV * N_COL // TILE) - 1).astype(jnp.int32)
    tile_cols = place_ends(jax.random.randint(key_list[4], (N_ROW, N_COL, TILE_MAX), 0, NODES_DEV * N_ROW // TILE), jax.random.fold_in(key_list[4], 1), 0, (NODES_DEV * N_ROW // TILE) - 1).astype(jnp.int32)
    tile_counts = draw_tile_counts(jax.random.fold_in(key_list[6], 71), 0)
    return dict(features=features, degrees=degrees, adj_tiles=adj_tiles, tile_rows=tile_rows, tile_cols=tile_cols, tile_counts=tile_counts)


ALPHA = 0.1

def reference(features, degrees, adj_tiles, tile_rows, tile_cols, tile_counts):
    norm_scale = jnp.sqrt(KNN / degrees.astype(jnp.float32))[:, None]
    teleport = ALPHA * features.astype(jnp.float32)
    current = features.astype(jnp.float32)
    row_tiles = NODES_DEV * N_COL // TILE
    panel_rows = NODES_DEV * N_COL
    block_len = min(256, TILE_MAX)
    num_turns = TILE_MAX // block_len
    for repeat in range(STEPS):
        source = (norm_scale * current).astype(jnp.bfloat16)
        panels = source.reshape(N_ROW, N_COL, NODES_DEV, FEAT).transpose(1, 0, 2, 3)
        panels = panels.reshape(N_COL, N_ROW * NODES_DEV // TILE, TILE, FEAT)

        def per_device(summed, flat_index):
            row_index = (flat_index // N_COL).astype(jnp.int32)
            col_index = (flat_index % N_COL).astype(jnp.int32)
            col_panel = panels[col_index].astype(jnp.float32)
            dev_tiles = adj_tiles[row_index, col_index].reshape(TILE_MAX, TILE, TILE)
            row_ids_all = tile_rows[row_index, col_index]
            col_ids_all = tile_cols[row_index, col_index]
            live_count = tile_counts[row_index, col_index]

            def add_block(totals, turn_index):
                first_tile = (turn_index * block_len).astype(jnp.int32)
                tile_block = lax.dynamic_slice_in_dim(dev_tiles, first_tile, block_len, 0).astype(jnp.float32)
                row_ids = lax.dynamic_slice_in_dim(row_ids_all, first_tile, block_len, 0)
                col_ids = lax.dynamic_slice_in_dim(col_ids_all, first_tile, block_len, 0)
                live_mask = first_tile + jnp.arange(block_len, dtype=jnp.int32) < live_count
                inputs = col_panel[col_ids]
                products = jnp.einsum('tab,tbf->taf', tile_block, inputs)
                products = jnp.where(live_mask[:, None, None], products, jnp.zeros_like(products))
                return (totals.at[row_ids].add(products), None)
            start_tot = jnp.zeros((row_tiles, TILE, FEAT), jnp.float32)
            totals, _ = lax.scan(add_block, start_tot, jnp.arange(num_turns, dtype=jnp.int32))
            offset = row_index * panel_rows
            old_rows = lax.dynamic_slice_in_dim(summed, offset, panel_rows, 0)
            summed = lax.dynamic_update_slice_in_dim(summed, old_rows + totals.reshape(panel_rows, FEAT), offset, 0)
            return (summed, None)
        summed, _ = lax.scan(per_device, jnp.zeros((NODES, FEAT), jnp.float32), jnp.arange(N_ROW * N_COL, dtype=jnp.int32))
        current = (1.0 - ALPHA) * norm_scale * summed + teleport
    return current.astype(jnp.bfloat16)
```

```python
import jax
import jax.numpy as jnp
from jax import lax
from jax.sharding import PartitionSpec as P

TILE = 64
KNN = 32
STEPS = 2


ALPHA = 0.1


def shards(features, degrees, adj_tiles, tile_rows, tile_cols, tile_counts):
    col_count = lax.axis_size("col")
    nodes_dev = features.shape[0]
    feat_width = features.shape[1]
    tile_slots = adj_tiles.shape[2]
    dev_tiles = adj_tiles.reshape(tile_slots, TILE, TILE)
    row_ids_all = tile_rows.reshape(tile_slots)
    col_ids_all = tile_cols.reshape(tile_slots)
    live_count = tile_counts.reshape(())
    block_len = min(256, tile_slots)
    num_turns = tile_slots // block_len
    row_tiles = nodes_dev * col_count // TILE
    norm_scale = jnp.sqrt(KNN / degrees.astype(jnp.float32))[:, None]
    teleport = ALPHA * features.astype(jnp.float32)
    current = features.astype(jnp.float32)
    for repeat in range(STEPS):
        source = (norm_scale * current).astype(jnp.bfloat16)
        col_panel = lax.all_gather(source, "row", axis=0, tiled=True).reshape(-1, TILE, feat_width)

        def add_block(turn_index, totals):
            first_tile = turn_index * block_len
            live_mask = first_tile + jnp.arange(block_len, dtype=jnp.int32) < live_count
            inputs = col_panel[col_ids_all]
            products = jnp.einsum(
                "tab,tbf->taf", dev_tiles, inputs, preferred_element_type=jnp.float32
            )
            products = jnp.where(live_mask[:, None, None], products, jnp.zeros_like(products))
            return totals.at[row_ids_all].add(products)

        start_tot = jnp.zeros((row_tiles, TILE, feat_width), jnp.float32)
        totals = lax.fori_loop(0, num_turns, add_block, start_tot)
        partial_rows = totals.reshape(row_tiles * TILE, feat_width)
        own_rows = lax.psum_scatter(partial_rows, "col", scatter_dimension=0, tiled=True)
        current = (1.0 - ALPHA) * norm_scale * own_rows + teleport
    return current.astype(jnp.bfloat16)


def solution(mesh):
    return jax.shard_map(
        shards,
        mesh=mesh,
        in_specs=(
            P(("row", "col"), None),
            P(("row", "col")),
            P("row", "col", None, None),
            P("row", "col", None),
            P("row", "col", None),
            P("row", "col"),
        ),
        out_specs=P(("row", "col"), None),
        check_vma=False,
    )
```

```python
import functools

import jax
import jax.numpy as jnp
from jax import lax
from jax.experimental import pallas as pl
from jax.experimental.pallas import tpu as pltpu
from jax.sharding import PartitionSpec as P

TILE = 64
KNN = 32
STEPS = 2

MESH = pl.DeviceIdType.MESH

ALPHA = 0.1


def reduce_scatter_kernel(n, part_ref, own_ref, out_ref, recv, send_sem, recv_sem):
    me = lax.axis_index("col")
    row = lax.axis_index("row")

    barrier = pltpu.get_barrier_semaphore()

    def greet(k, carry):
        peer = lax.rem(me + k, n)
        pl.semaphore_signal(barrier, inc=1, device_id=(row, peer), device_id_type=MESH)
        return carry

    lax.fori_loop(1, n, greet, 0)
    pl.semaphore_wait(barrier, n - 1)

    def send(peer):
        return pltpu.make_async_remote_copy(
            src_ref=part_ref.at[peer],
            dst_ref=recv.at[me],
            send_sem=send_sem.at[peer],
            recv_sem=recv_sem.at[me],
            device_id=(row, peer),
            device_id_type=MESH,
        )

    def arrival(sender):
        return pltpu.make_async_remote_copy(
            src_ref=part_ref.at[sender],
            dst_ref=recv.at[sender],
            send_sem=send_sem.at[sender],
            recv_sem=recv_sem.at[sender],
            device_id=(row, sender),
            device_id_type=MESH,
        )

    def start(k, carry):
        send(lax.rem(me + k, n)).start()
        return carry

    lax.fori_loop(1, n, start, 0)

    out_ref[...] = own_ref[...]

    def finish(k, carry):
        sender = lax.rem(me + n - k, n)
        arrival(sender).wait_recv()
        out_ref[...] += recv[sender].astype(jnp.float32)
        return carry

    lax.fori_loop(1, n, finish, 0)

    def drain(k, carry):
        send(lax.rem(me + k, n)).wait_send()
        return carry

    lax.fori_loop(1, n, drain, 0)


def col_reduce_scatter(partial_rows, nodes_dev):
    n = lax.axis_size("col")
    feat_width = partial_rows.shape[1]
    me = lax.axis_index("col")
    own = lax.dynamic_slice_in_dim(partial_rows, me * nodes_dev, nodes_dev, 0)
    pieces = partial_rows.reshape(n, nodes_dev, feat_width).astype(jnp.bfloat16)
    return pl.pallas_call(
        functools.partial(reduce_scatter_kernel, n),
        out_shape=jax.ShapeDtypeStruct((nodes_dev, feat_width), jnp.float32),
        in_specs=[pl.BlockSpec(memory_space=pltpu.VMEM)] * 2,
        out_specs=pl.BlockSpec(memory_space=pltpu.VMEM),
        scratch_shapes=[
            pltpu.VMEM((n, nodes_dev, feat_width), jnp.bfloat16),
            pltpu.SemaphoreType.DMA((n,)),
            pltpu.SemaphoreType.DMA((n,)),
        ],
        compiler_params=pltpu.CompilerParams(collective_id=0, has_side_effects=True),
    )(pieces, own)


def shards(features, degrees, adj_tiles, tile_rows, tile_cols, tile_counts):
    col_count = lax.axis_size("col")
    nodes_dev = features.shape[0]
    feat_width = features.shape[1]
    tile_slots = adj_tiles.shape[2]
    dev_tiles = adj_tiles.reshape(tile_slots, TILE, TILE)
    row_ids_all = tile_rows.reshape(tile_slots)
    col_ids_all = tile_cols.reshape(tile_slots)
    live_count = tile_counts.reshape(())
    block_len = min(256, tile_slots)
    num_turns = tile_slots // block_len
    row_tiles = nodes_dev * col_count // TILE
    norm_scale = jnp.sqrt(KNN / degrees.astype(jnp.float32))[:, None]
    teleport = ALPHA * features.astype(jnp.float32)
    current = features.astype(jnp.float32)
    for repeat in range(STEPS):
        source = (norm_scale * current).astype(jnp.bfloat16)
        col_panel = lax.all_gather(source, "row", axis=0, tiled=True).reshape(-1, TILE, feat_width)

        def add_block(turn_index, totals):
            first_tile = turn_index * block_len
            live_mask = first_tile + jnp.arange(block_len, dtype=jnp.int32) < live_count
            inputs = col_panel[col_ids_all]
            products = jnp.einsum(
                "tab,tbf->taf", dev_tiles, inputs, preferred_element_type=jnp.float32
            )
            products = jnp.where(live_mask[:, None, None], products, jnp.zeros_like(products))
            return totals.at[row_ids_all].add(products)

        start_tot = jnp.zeros((row_tiles, TILE, feat_width), jnp.float32)
        totals = lax.fori_loop(0, num_turns, add_block, start_tot)
        partial_rows = totals.reshape(row_tiles * TILE, feat_width)
        own_rows = col_reduce_scatter(partial_rows, nodes_dev)
        current = (1.0 - ALPHA) * norm_scale * own_rows + teleport
    return current.astype(jnp.bfloat16)


def solution(mesh):
    return jax.shard_map(
        shards,
        mesh=mesh,
        in_specs=(
            P(("row", "col"), None),
            P(("row", "col")),
            P("row", "col", None, None),
            P("row", "col", None),
            P("row", "col", None),
            P("row", "col"),
        ),
        out_specs=P(("row", "col"), None),
        check_vma=False,
    )
```

```python
import functools

import jax
import jax.numpy as jnp
from jax import lax
from jax.experimental import pallas as pl
from jax.experimental.pallas import tpu as pltpu
from jax.sharding import PartitionSpec as P

TILE = 64
KNN = 32
STEPS = 2

MESH = pl.DeviceIdType.MESH

ALPHA = 0.1


def reduce_scatter_kernel(n, part_ref, own_ref, out_ref, recv, send_sem, recv_sem):
    me = lax.axis_index("col")
    row = lax.axis_index("row")

    barrier = pltpu.get_barrier_semaphore()

    def greet(k, carry):
        peer = lax.rem(me + k, n)
        pl.semaphore_signal(barrier, inc=1, device_id=(row, peer), device_id_type=MESH)
        return carry

    lax.fori_loop(1, n, greet, 0)
    pl.semaphore_wait(barrier, n - 1)

    def send(peer):
        return pltpu.make_async_remote_copy(
            src_ref=part_ref.at[peer],
            dst_ref=recv.at[me],
            send_sem=send_sem.at[peer],
            recv_sem=recv_sem.at[me],
            device_id=(row, peer),
            device_id_type=MESH,
        )

    def arrival(sender):
        return pltpu.make_async_remote_copy(
            src_ref=part_ref.at[sender],
            dst_ref=recv.at[sender],
            send_sem=send_sem.at[sender],
            recv_sem=recv_sem.at[sender],
            device_id=(row, sender),
            device_id_type=MESH,
        )

    def start(k, carry):
        send(lax.rem(me + k, n)).start()
        return carry

    lax.fori_loop(1, n, start, 0)

    out_ref[...] = own_ref[...]

    def finish(k, carry):
        sender = lax.rem(me + n - k, n)
        arrival(sender).wait_recv()
        out_ref[...] += recv[sender].astype(jnp.float32)
        return carry

    lax.fori_loop(1, n, finish, 0)

    def drain(k, carry):
        send(lax.rem(me + k, n)).wait_send()
        return carry

    lax.fori_loop(1, n, drain, 0)


def col_reduce_scatter(pieces, own):
    n, nodes_dev, feat_width = pieces.shape
    return pl.pallas_call(
        functools.partial(reduce_scatter_kernel, n),
        out_shape=jax.ShapeDtypeStruct((nodes_dev, feat_width), jnp.float32),
        in_specs=[pl.BlockSpec(memory_space=pltpu.VMEM)] * 2,
        out_specs=pl.BlockSpec(memory_space=pltpu.VMEM),
        scratch_shapes=[
            pltpu.VMEM((n, nodes_dev, feat_width), jnp.bfloat16),
            pltpu.SemaphoreType.DMA((n,)),
            pltpu.SemaphoreType.DMA((n,)),
        ],
        compiler_params=pltpu.CompilerParams(collective_id=0, has_side_effects=True),
    )(pieces, own)


def block_product_kernel(group, rows_ref, cols_ref, count_ref, adj_ref, panel_ref,
                         pieces_ref, own_ref, acc_ref):
    acc_ref[...] = jnp.zeros_like(acc_ref)
    count = count_ref[0]
    slots = adj_ref.shape[0]

    def body(g, carry):
        base = g * group
        prods = []
        for i in range(group):
            t = base + i
            p = jnp.dot(adj_ref[t], panel_ref[cols_ref[t]], preferred_element_type=jnp.float32)
            prods.append(jnp.where(t < count, p, jnp.zeros_like(p)))
        for i in range(group):
            r = rows_ref[base + i]
            acc_ref[r] += prods[i]
        return carry

    lax.fori_loop(0, slots // group, body, 0)
    pieces_ref[...] = acc_ref[...].astype(pieces_ref.dtype)
    per_piece = own_ref.shape[0]
    me = lax.axis_index("col")
    own_ref[...] = acc_ref[pl.ds(me * per_piece, per_piece)]


def block_product(row_ids, col_ids, count, dev_tiles, col_panel, row_tiles, nodes_dev):
    slots = dev_tiles.shape[0]
    feat_width = col_panel.shape[2]
    per_piece = nodes_dev // TILE
    group = 4 if slots % 4 == 0 else 1
    smem = pl.BlockSpec(memory_space=pltpu.SMEM)
    vmem = pl.BlockSpec(memory_space=pltpu.VMEM)
    return pl.pallas_call(
        functools.partial(block_product_kernel, group),
        out_shape=(
            jax.ShapeDtypeStruct((row_tiles, TILE, feat_width), jnp.bfloat16),
            jax.ShapeDtypeStruct((per_piece, TILE, feat_width), jnp.float32),
        ),
        in_specs=[smem, smem, smem, vmem, vmem],
        out_specs=(vmem, vmem),
        scratch_shapes=[pltpu.VMEM((row_tiles, TILE, feat_width), jnp.float32)],
        cost_estimate=pl.CostEstimate(
            flops=2 * slots * TILE * TILE * feat_width,
            bytes_accessed=slots * TILE * TILE * 2 + row_tiles * TILE * feat_width * 2,
            transcendentals=0,
        ),
    )(row_ids, col_ids, count, dev_tiles, col_panel)


def shards(features, degrees, adj_tiles, tile_rows, tile_cols, tile_counts):
    col_count = lax.axis_size("col")
    nodes_dev = features.shape[0]
    feat_width = features.shape[1]
    tile_slots = adj_tiles.shape[2]
    dev_tiles = adj_tiles.reshape(tile_slots, TILE, TILE)
    row_ids_all = tile_rows.reshape(tile_slots)
    col_ids_all = tile_cols.reshape(tile_slots)
    live_count = tile_counts.reshape(1)
    row_tiles = nodes_dev * col_count // TILE
    norm_scale = jnp.sqrt(KNN / degrees.astype(jnp.float32))[:, None]
    teleport = ALPHA * features.astype(jnp.float32)
    current = features.astype(jnp.float32)
    for repeat in range(STEPS):
        source = (norm_scale * current).astype(jnp.bfloat16)
        col_panel = lax.all_gather(source, "row", axis=0, tiled=True).reshape(-1, TILE, feat_width)
        pieces, own = block_product(
            row_ids_all, col_ids_all, live_count, dev_tiles, col_panel, row_tiles, nodes_dev
        )
        own_rows = col_reduce_scatter(
            pieces.reshape(col_count, nodes_dev, feat_width), own.reshape(nodes_dev, feat_width)
        )
        current = (1.0 - ALPHA) * norm_scale * own_rows + teleport
    return current.astype(jnp.bfloat16)


def solution(mesh):
    return jax.shard_map(
        shards,
        mesh=mesh,
        in_specs=(
            P(("row", "col"), None),
            P(("row", "col")),
            P("row", "col", None, None),
            P("row", "col", None),
            P("row", "col", None),
            P("row", "col"),
        ),
        out_specs=P(("row", "col"), None),
        check_vma=False,
    )
```

```python
import functools

import jax
import jax.numpy as jnp
from jax import lax
from jax.experimental import pallas as pl
from jax.experimental.pallas import tpu as pltpu
from jax.sharding import PartitionSpec as P

TILE = 64
KNN = 32
STEPS = 2

MESH = pl.DeviceIdType.MESH

ALPHA = 0.1


def reduce_scatter_kernel(n, part_ref, own_ref, out_ref, recv, send_sem, recv_sem):
    me = lax.axis_index("col")
    row = lax.axis_index("row")

    barrier = pltpu.get_barrier_semaphore()

    def greet(k, carry):
        peer = lax.rem(me + k, n)
        pl.semaphore_signal(barrier, inc=1, device_id=(row, peer), device_id_type=MESH)
        return carry

    lax.fori_loop(1, n, greet, 0)
    pl.semaphore_wait(barrier, n - 1)

    def send(peer):
        return pltpu.make_async_remote_copy(
            src_ref=part_ref.at[peer],
            dst_ref=recv.at[me],
            send_sem=send_sem.at[peer],
            recv_sem=recv_sem.at[me],
            device_id=(row, peer),
            device_id_type=MESH,
        )

    def arrival(sender):
        return pltpu.make_async_remote_copy(
            src_ref=part_ref.at[sender],
            dst_ref=recv.at[sender],
            send_sem=send_sem.at[sender],
            recv_sem=recv_sem.at[sender],
            device_id=(row, sender),
            device_id_type=MESH,
        )

    def start(k, carry):
        send(lax.rem(me + k, n)).start()
        return carry

    lax.fori_loop(1, n, start, 0)

    out_ref[...] = own_ref[...]

    def finish(k, carry):
        sender = lax.rem(me + n - k, n)
        arrival(sender).wait_recv()
        out_ref[...] += recv[sender].astype(jnp.float32)
        return carry

    lax.fori_loop(1, n, finish, 0)

    def drain(k, carry):
        send(lax.rem(me + k, n)).wait_send()
        return carry

    lax.fori_loop(1, n, drain, 0)


def col_reduce_scatter(pieces, own):
    n, nodes_dev, feat_width = pieces.shape
    return pl.pallas_call(
        functools.partial(reduce_scatter_kernel, n),
        out_shape=jax.ShapeDtypeStruct((nodes_dev, feat_width), jnp.float32),
        in_specs=[pl.BlockSpec(memory_space=pltpu.VMEM)] * 2,
        out_specs=pl.BlockSpec(memory_space=pltpu.VMEM),
        scratch_shapes=[
            pltpu.VMEM((n, nodes_dev, feat_width), jnp.bfloat16),
            pltpu.SemaphoreType.DMA((n,)),
            pltpu.SemaphoreType.DMA((n,)),
        ],
        compiler_params=pltpu.CompilerParams(collective_id=0, has_side_effects=True),
    )(pieces, own)


def all_gather_kernel(n, src_ref, out_ref, send_sem, recv_sem):
    me = lax.axis_index("row")
    col = lax.axis_index("col")

    barrier = pltpu.get_barrier_semaphore()

    def greet(k, carry):
        peer = lax.rem(me + k, n)
        pl.semaphore_signal(barrier, inc=1, device_id=(peer, col), device_id_type=MESH)
        return carry

    lax.fori_loop(1, n, greet, 0)
    pl.semaphore_wait(barrier, n - 1)

    def copy(peer, slot):
        return pltpu.make_async_remote_copy(
            src_ref=src_ref,
            dst_ref=out_ref.at[slot],
            send_sem=send_sem.at[peer],
            recv_sem=recv_sem.at[slot],
            device_id=(peer, col),
            device_id_type=MESH,
        )

    def start(k, carry):
        copy(lax.rem(me + k, n), me).start()
        return carry

    lax.fori_loop(1, n, start, 0)
    out_ref[me] = src_ref[...]

    def finish(k, carry):
        sender = lax.rem(me + n - k, n)
        copy(sender, sender).wait_recv()
        copy(lax.rem(me + k, n), me).wait_send()
        return carry

    lax.fori_loop(1, n, finish, 0)


def row_all_gather(source):
    n = lax.axis_size("row")
    nodes_dev, feat_width = source.shape
    vmem = pl.BlockSpec(memory_space=pltpu.VMEM)
    return pl.pallas_call(
        functools.partial(all_gather_kernel, n),
        out_shape=jax.ShapeDtypeStruct((n, nodes_dev, feat_width), source.dtype),
        in_specs=[vmem],
        out_specs=vmem,
        scratch_shapes=[pltpu.SemaphoreType.DMA((n,)), pltpu.SemaphoreType.DMA((n,))],
        compiler_params=pltpu.CompilerParams(collective_id=1, has_side_effects=True),
    )(source)


def block_product_kernel(group, rows_ref, cols_ref, count_ref, adj_ref, panel_ref,
                         pieces_ref, own_ref, acc_ref):
    acc_ref[...] = jnp.zeros_like(acc_ref)
    count = count_ref[0]
    slots = adj_ref.shape[0]

    def body(g, carry):
        base = g * group
        prods = []
        for i in range(group):
            t = base + i
            p = jnp.dot(adj_ref[t], panel_ref[cols_ref[t]], preferred_element_type=jnp.float32)
            prods.append(jnp.where(t < count, p, jnp.zeros_like(p)))
        for i in range(group):
            r = rows_ref[base + i]
            acc_ref[r] += prods[i]
        return carry

    lax.fori_loop(0, slots // group, body, 0)
    pieces_ref[...] = acc_ref[...].astype(pieces_ref.dtype)
    per_piece = own_ref.shape[0]
    me = lax.axis_index("col")
    own_ref[...] = acc_ref[pl.ds(me * per_piece, per_piece)]


def block_product(row_ids, col_ids, count, dev_tiles, col_panel, row_tiles, nodes_dev):
    slots = dev_tiles.shape[0]
    feat_width = col_panel.shape[2]
    per_piece = nodes_dev // TILE
    group = 4 if slots % 4 == 0 else 1
    smem = pl.BlockSpec(memory_space=pltpu.SMEM)
    vmem = pl.BlockSpec(memory_space=pltpu.VMEM)
    return pl.pallas_call(
        functools.partial(block_product_kernel, group),
        out_shape=(
            jax.ShapeDtypeStruct((row_tiles, TILE, feat_width), jnp.bfloat16),
            jax.ShapeDtypeStruct((per_piece, TILE, feat_width), jnp.float32),
        ),
        in_specs=[smem, smem, smem, vmem, vmem],
        out_specs=(vmem, vmem),
        scratch_shapes=[pltpu.VMEM((row_tiles, TILE, feat_width), jnp.float32)],
        cost_estimate=pl.CostEstimate(
            flops=2 * slots * TILE * TILE * feat_width,
            bytes_accessed=slots * TILE * TILE * 2 + row_tiles * TILE * feat_width * 2,
            transcendentals=0,
        ),
    )(row_ids, col_ids, count, dev_tiles, col_panel)


def shards(features, degrees, adj_tiles, tile_rows, tile_cols, tile_counts):
    col_count = lax.axis_size("col")
    nodes_dev = features.shape[0]
    feat_width = features.shape[1]
    tile_slots = adj_tiles.shape[2]
    dev_tiles = adj_tiles.reshape(tile_slots, TILE, TILE)
    row_ids_all = tile_rows.reshape(tile_slots)
    col_ids_all = tile_cols.reshape(tile_slots)
    live_count = tile_counts.reshape(1)
    row_tiles = nodes_dev * col_count // TILE
    norm_scale = jnp.sqrt(KNN / degrees.astype(jnp.float32))[:, None]
    teleport = ALPHA * features.astype(jnp.float32)
    current = features.astype(jnp.float32)
    for repeat in range(STEPS):
        source = (norm_scale * current).astype(jnp.bfloat16)
        col_panel = row_all_gather(source).reshape(-1, TILE, feat_width)
        pieces, own = block_product(
            row_ids_all, col_ids_all, live_count, dev_tiles, col_panel, row_tiles, nodes_dev
        )
        own_rows = col_reduce_scatter(
            pieces.reshape(col_count, nodes_dev, feat_width), own.reshape(nodes_dev, feat_width)
        )
        current = (1.0 - ALPHA) * norm_scale * own_rows + teleport
    return current.astype(jnp.bfloat16)


def solution(mesh):
    return jax.shard_map(
        shards,
        mesh=mesh,
        in_specs=(
            P(("row", "col"), None),
            P(("row", "col")),
            P("row", "col", None, None),
            P("row", "col", None),
            P("row", "col", None),
            P("row", "col"),
        ),
        out_specs=P(("row", "col"), None),
        check_vma=False,
    )
```

```python
import functools

import jax
import jax.numpy as jnp
from jax import lax
from jax.experimental import pallas as pl
from jax.experimental.pallas import tpu as pltpu
from jax.sharding import PartitionSpec as P

TILE = 64
KNN = 32
STEPS = 2

MESH = pl.DeviceIdType.MESH

ALPHA = 0.1


CORES = 2
Z_RING = 8


def reduce_scatter_kernel(n_z, x_ref, out_ref, ra, sa, cw_recv, ccw_recv, cw_send, ccw_send,
                          fin, y_recv, a_sems, cw_sems, ccw_sems, y_sems):
    c = lax.axis_index("col")
    row = lax.axis_index("row")
    core = lax.rem(c, CORES)
    z = lax.rem(c // CORES, n_z)
    yh = c // (CORES * n_z)

    def dev(yh_, z_, core_):
        return (row, (yh_ * n_z + z_) * CORES + core_)

    partner = dev(yh, z, 1 - core)
    right = dev(yh, lax.rem(z + 1, n_z), core)
    left = dev(yh, lax.rem(z + n_z - 1, n_z), core)
    y_partner = dev(1 - yh, z, core)

    barrier = pltpu.get_barrier_semaphore()
    for peer in (partner, right, left, y_partner):
        pl.semaphore_signal(barrier, inc=1, device_id=peer, device_id_type=MESH)
    pl.semaphore_wait(barrier, 4)

    def rcopy(src, dst, sems, k, peer):
        return pltpu.make_async_remote_copy(
            src_ref=src, dst_ref=dst, send_sem=sems.at[0, k], recv_sem=sems.at[1, k],
            device_id=peer, device_id_type=MESH,
        )

    copy_a = rcopy(x_ref.at[1 - core], ra, a_sems, 0, partner)
    copy_a.start()
    copy_a.wait_recv()
    sa[...] = x_ref[core] + ra[...]

    sends = [copy_a]
    for s in range(n_z - 1):
        g_cw = lax.rem(z + (n_z - s - 1), n_z)
        g_ccw = lax.rem(z + s + 1, n_z)
        src_cw = sa.at[g_cw, 0] if s == 0 else cw_send.at[s - 1]
        src_ccw = sa.at[g_ccw, 1] if s == 0 else ccw_send.at[s - 1]
        copy_cw = rcopy(src_cw, cw_recv.at[s], cw_sems, s, right)
        copy_ccw = rcopy(src_ccw, ccw_recv.at[s], ccw_sems, s, left)
        copy_cw.start()
        copy_ccw.start()
        sends += [copy_cw, copy_ccw]
        got_cw = lax.rem(z + (2 * n_z - s - 2), n_z)
        got_ccw = lax.rem(z + s + 2, n_z)
        copy_cw.wait_recv()
        if s < n_z - 2:
            cw_send[s] = cw_recv[s] + sa[got_cw, 0]
        else:
            fin[0] = cw_recv[s] + sa[got_cw, 0]
        copy_ccw.wait_recv()
        if s < n_z - 2:
            ccw_send[s] = ccw_recv[s] + sa[got_ccw, 1]
        else:
            fin[1] = ccw_recv[s] + sa[got_ccw, 1]

    copy_y = rcopy(fin.at[1 - yh], y_recv, y_sems, 0, y_partner)
    copy_y.start()
    sends.append(copy_y)
    copy_y.wait_recv()
    out_ref[...] = fin[yh] + y_recv[...]
    for cp in sends:
        cp.wait_send()


def col_reduce_scatter(pieces):
    cores, n_z, n_y, nodes_dev, feat_width = pieces.shape
    piece = (nodes_dev, feat_width)
    vmem = pl.BlockSpec(memory_space=pltpu.VMEM)
    return pl.pallas_call(
        functools.partial(reduce_scatter_kernel, n_z),
        out_shape=jax.ShapeDtypeStruct(piece, jnp.float32),
        in_specs=[vmem],
        out_specs=vmem,
        scratch_shapes=[
            pltpu.VMEM((n_z, n_y) + piece, jnp.float32),
            pltpu.VMEM((n_z, n_y) + piece, jnp.float32),
            pltpu.VMEM((n_z - 1,) + piece, jnp.float32),
            pltpu.VMEM((n_z - 1,) + piece, jnp.float32),
            pltpu.VMEM((n_z - 1,) + piece, jnp.float32),
            pltpu.VMEM((n_z - 1,) + piece, jnp.float32),
            pltpu.VMEM((n_y,) + piece, jnp.float32),
            pltpu.VMEM(piece, jnp.float32),
            pltpu.SemaphoreType.DMA((2, 1)),
            pltpu.SemaphoreType.DMA((2, n_z - 1)),
            pltpu.SemaphoreType.DMA((2, n_z - 1)),
            pltpu.SemaphoreType.DMA((2, 1)),
        ],
        compiler_params=pltpu.CompilerParams(collective_id=0, has_side_effects=True),
    )(pieces)


def all_gather_kernel(n, src_ref, out_ref, send_sem, recv_sem):
    me = lax.axis_index("row")
    col = lax.axis_index("col")

    barrier = pltpu.get_barrier_semaphore()

    def greet(k, carry):
        peer = lax.rem(me + k, n)
        pl.semaphore_signal(barrier, inc=1, device_id=(peer, col), device_id_type=MESH)
        return carry

    lax.fori_loop(1, n, greet, 0)
    pl.semaphore_wait(barrier, n - 1)

    def copy(peer, slot):
        return pltpu.make_async_remote_copy(
            src_ref=src_ref,
            dst_ref=out_ref.at[slot],
            send_sem=send_sem.at[peer],
            recv_sem=recv_sem.at[slot],
            device_id=(peer, col),
            device_id_type=MESH,
        )

    def start(k, carry):
        copy(lax.rem(me + k, n), me).start()
        return carry

    lax.fori_loop(1, n, start, 0)
    out_ref[me] = src_ref[...]

    def finish(k, carry):
        sender = lax.rem(me + n - k, n)
        copy(sender, sender).wait_recv()
        copy(lax.rem(me + k, n), me).wait_send()
        return carry

    lax.fori_loop(1, n, finish, 0)


def row_all_gather(source):
    n = lax.axis_size("row")
    nodes_dev, feat_width = source.shape
    vmem = pl.BlockSpec(memory_space=pltpu.VMEM)
    return pl.pallas_call(
        functools.partial(all_gather_kernel, n),
        out_shape=jax.ShapeDtypeStruct((n, nodes_dev, feat_width), source.dtype),
        in_specs=[vmem],
        out_specs=vmem,
        scratch_shapes=[pltpu.SemaphoreType.DMA((n,)), pltpu.SemaphoreType.DMA((n,))],
        compiler_params=pltpu.CompilerParams(collective_id=1, has_side_effects=True),
    )(source)


def block_product_kernel(group, rows_ref, cols_ref, count_ref, adj_ref, panel_ref,
                         pieces_ref, acc_ref):
    acc_ref[...] = jnp.zeros_like(acc_ref)
    count = count_ref[0]
    slots = adj_ref.shape[0]

    def body(g, carry):
        base = g * group
        prods = []
        for i in range(group):
            t = base + i
            p = jnp.dot(adj_ref[t], panel_ref[cols_ref[t]], preferred_element_type=jnp.float32)
            prods.append(jnp.where(t < count, p, jnp.zeros_like(p)))
        for i in range(group):
            r = rows_ref[base + i]
            acc_ref[r] += prods[i]
        return carry

    lax.fori_loop(0, slots // group, body, 0)
    cores, n_z, n_y, per_piece = pieces_ref.shape[:4]
    for j in range(cores * n_z * n_y):
        core_j, z_j, yh_j = j % cores, (j // cores) % n_z, j // (cores * n_z)
        pieces_ref[core_j, z_j, yh_j] = acc_ref[j * per_piece:(j + 1) * per_piece]


def block_product(row_ids, col_ids, count, dev_tiles, col_panel, row_tiles, nodes_dev):
    slots = dev_tiles.shape[0]
    feat_width = col_panel.shape[2]
    per_piece = nodes_dev // TILE
    group = 4 if slots % 4 == 0 else 1
    smem = pl.BlockSpec(memory_space=pltpu.SMEM)
    vmem = pl.BlockSpec(memory_space=pltpu.VMEM)
    return pl.pallas_call(
        functools.partial(block_product_kernel, group),
        out_shape=jax.ShapeDtypeStruct(
            (CORES, Z_RING, row_tiles // (per_piece * CORES * Z_RING), per_piece, TILE, feat_width),
            jnp.float32,
        ),
        in_specs=[smem, smem, smem, vmem, vmem],
        out_specs=vmem,
        scratch_shapes=[pltpu.VMEM((row_tiles, TILE, feat_width), jnp.float32)],
        cost_estimate=pl.CostEstimate(
            flops=2 * slots * TILE * TILE * feat_width,
            bytes_accessed=slots * TILE * TILE * 2 + row_tiles * TILE * feat_width * 4,
            transcendentals=0,
        ),
    )(row_ids, col_ids, count, dev_tiles, col_panel)


def shards(features, degrees, adj_tiles, tile_rows, tile_cols, tile_counts):
    col_count = lax.axis_size("col")
    nodes_dev = features.shape[0]
    feat_width = features.shape[1]
    tile_slots = adj_tiles.shape[2]
    dev_tiles = adj_tiles.reshape(tile_slots, TILE, TILE)
    row_ids_all = tile_rows.reshape(tile_slots)
    col_ids_all = tile_cols.reshape(tile_slots)
    live_count = tile_counts.reshape(1)
    row_tiles = nodes_dev * col_count // TILE
    norm_scale = jnp.sqrt(KNN / degrees.astype(jnp.float32))[:, None]
    teleport = ALPHA * features.astype(jnp.float32)
    current = features.astype(jnp.float32)
    for repeat in range(STEPS):
        source = (norm_scale * current).astype(jnp.bfloat16)
        col_panel = row_all_gather(source).reshape(-1, TILE, feat_width)
        pieces = block_product(
            row_ids_all, col_ids_all, live_count, dev_tiles, col_panel, row_tiles, nodes_dev
        )
        own_rows = col_reduce_scatter(pieces.reshape(pieces.shape[:3] + (nodes_dev, feat_width)))
        current = (1.0 - ALPHA) * norm_scale * own_rows + teleport
    return current.astype(jnp.bfloat16)


def solution(mesh):
    return jax.shard_map(
        shards,
        mesh=mesh,
        in_specs=(
            P(("row", "col"), None),
            P(("row", "col")),
            P("row", "col", None, None),
            P("row", "col", None),
            P("row", "col", None),
            P("row", "col"),
        ),
        out_specs=P(("row", "col"), None),
        check_vma=False,
    )
```

```python
import functools

import jax
import jax.numpy as jnp
from jax import lax
from jax.experimental import pallas as pl
from jax.experimental.pallas import tpu as pltpu
from jax.sharding import PartitionSpec as P

TILE = 64
KNN = 32
STEPS = 2

MESH = pl.DeviceIdType.MESH

ALPHA = 0.1


CORES = 2
Z_RING = 8


def reduce_scatter_kernel(n_z, chunks, x_ref, out_ref, ra, recv_cw, recv_ccw, send_cw, send_ccw,
                          fin, y_recv, a_sems, cw_sems, ccw_sems, y_sems):
    c = lax.axis_index("col")
    row = lax.axis_index("row")
    core = lax.rem(c, CORES)
    z = lax.rem(c // CORES, n_z)
    yh = c // (CORES * n_z)

    def dev(yh_, z_, core_):
        return (row, (yh_ * n_z + z_) * CORES + core_)

    partner = dev(yh, z, 1 - core)
    right = dev(yh, lax.rem(z + 1, n_z), core)
    left = dev(yh, lax.rem(z + n_z - 1, n_z), core)
    y_partner = dev(1 - yh, z, core)

    barrier = pltpu.get_barrier_semaphore()
    for peer in (partner, right, left, y_partner):
        pl.semaphore_signal(barrier, inc=1, device_id=peer, device_id_type=MESH)
    pl.semaphore_wait(barrier, 4)

    def rcopy(src, dst, sems, idx, peer):
        return pltpu.make_async_remote_copy(
            src_ref=src, dst_ref=dst, send_sem=sems.at[(0,) + idx], recv_sem=sems.at[(1,) + idx],
            device_id=peer, device_id_type=MESH,
        )

    def first(d):
        return lax.rem(z + (n_z - 1 if d == 0 else 1), n_z)

    def got(d, s):
        return lax.rem(z + ((2 * n_z - s - 2) if d == 0 else (s + 2)), n_z)

    need = [(first(0), 0), (first(1), 1)]
    for s in range(n_z - 1):
        need += [(got(0, s), 0), (got(1, s), 1)]
    copies_a = []
    for k, (g, h) in enumerate(need):
        cp = rcopy(x_ref.at[1 - core, g, h], ra.at[g, h], a_sems, (k,), partner)
        cp.start()
        copies_a.append(cp)

    def ready(d, s):
        copies_a[d if s < 0 else 2 + 2 * s + d].wait_recv()

    size = x_ref.shape[3] // chunks
    recv = (recv_cw, recv_ccw)
    send = (send_cw, send_ccw)
    sems = (cw_sems, ccw_sems)
    to = (right, left)
    sends = list(copies_a)

    def ring_copy(d, s, i):
        part = pl.ds(i * size, size)
        return rcopy(send[d].at[s, part], recv[d].at[s, part], sems[d], (s, i), to[d])

    for d in range(2):
        ready(d, -1)
        g = first(d)
        send[d][0] = x_ref[core, g, d] + ra[g, d]
        for i in range(chunks):
            cp = ring_copy(d, 0, i)
            cp.start()
            sends.append(cp)
    for s in range(n_z - 1):
        for d in range(2):
            ready(d, s)
        for i in range(chunks):
            part = pl.ds(i * size, size)
            for d in range(2):
                g = got(d, s)
                ring_copy(d, s, i).wait_recv()
                val = recv[d][s, part] + x_ref[core, g, d, part] + ra[g, d, part]
                if s < n_z - 2:
                    send[d][s + 1, part] = val
                    cp = ring_copy(d, s + 1, i)
                    cp.start()
                    sends.append(cp)
                else:
                    fin[d, part] = val

    copy_y = rcopy(fin.at[1 - yh], y_recv, y_sems, (0,), y_partner)
    copy_y.start()
    sends.append(copy_y)
    copy_y.wait_recv()
    out_ref[...] = fin[yh] + y_recv[...]
    for cp in sends:
        cp.wait_send()


def col_reduce_scatter(pieces):
    cores, n_z, n_y, nodes_dev, feat_width = pieces.shape
    chunks = 4
    piece = (nodes_dev, feat_width)
    vmem = pl.BlockSpec(memory_space=pltpu.VMEM)
    return pl.pallas_call(
        functools.partial(reduce_scatter_kernel, n_z, chunks),
        out_shape=jax.ShapeDtypeStruct(piece, jnp.float32),
        in_specs=[vmem],
        out_specs=vmem,
        scratch_shapes=[
            pltpu.VMEM((n_z, n_y) + piece, jnp.float32),
            pltpu.VMEM((n_z - 1,) + piece, jnp.float32),
            pltpu.VMEM((n_z - 1,) + piece, jnp.float32),
            pltpu.VMEM((n_z - 1,) + piece, jnp.float32),
            pltpu.VMEM((n_z - 1,) + piece, jnp.float32),
            pltpu.VMEM((n_y,) + piece, jnp.float32),
            pltpu.VMEM(piece, jnp.float32),
            pltpu.SemaphoreType.DMA((2, 2 * n_z)),
            pltpu.SemaphoreType.DMA((2, n_z - 1, chunks)),
            pltpu.SemaphoreType.DMA((2, n_z - 1, chunks)),
            pltpu.SemaphoreType.DMA((2, 1)),
        ],
        compiler_params=pltpu.CompilerParams(collective_id=0, has_side_effects=True),
    )(pieces)


def all_gather_kernel(n, src_ref, out_ref, send_sem, recv_sem):
    me = lax.axis_index("row")
    col = lax.axis_index("col")

    barrier = pltpu.get_barrier_semaphore()

    def greet(k, carry):
        peer = lax.rem(me + k, n)
        pl.semaphore_signal(barrier, inc=1, device_id=(peer, col), device_id_type=MESH)
        return carry

    lax.fori_loop(1, n, greet, 0)
    pl.semaphore_wait(barrier, n - 1)

    def copy(peer, slot):
        return pltpu.make_async_remote_copy(
            src_ref=src_ref,
            dst_ref=out_ref.at[slot],
            send_sem=send_sem.at[peer],
            recv_sem=recv_sem.at[slot],
            device_id=(peer, col),
            device_id_type=MESH,
        )

    def start(k, carry):
        copy(lax.rem(me + k, n), me).start()
        return carry

    lax.fori_loop(1, n, start, 0)
    out_ref[me] = src_ref[...]

    def finish(k, carry):
        sender = lax.rem(me + n - k, n)
        copy(sender, sender).wait_recv()
        copy(lax.rem(me + k, n), me).wait_send()
        return carry

    lax.fori_loop(1, n, finish, 0)


def row_all_gather(source):
    n = lax.axis_size("row")
    nodes_dev, feat_width = source.shape
    vmem = pl.BlockSpec(memory_space=pltpu.VMEM)
    return pl.pallas_call(
        functools.partial(all_gather_kernel, n),
        out_shape=jax.ShapeDtypeStruct((n, nodes_dev, feat_width), source.dtype),
        in_specs=[vmem],
        out_specs=vmem,
        scratch_shapes=[pltpu.SemaphoreType.DMA((n,)), pltpu.SemaphoreType.DMA((n,))],
        compiler_params=pltpu.CompilerParams(collective_id=1, has_side_effects=True),
    )(source)


def block_product_kernel(group, rows_ref, cols_ref, count_ref, adj_ref, panel_ref,
                         pieces_ref, acc_ref):
    acc_ref[...] = jnp.zeros_like(acc_ref)
    count = count_ref[0]
    slots = adj_ref.shape[0]

    def body(g, carry):
        base = g * group
        prods = []
        for i in range(group):
            t = base + i
            p = jnp.dot(adj_ref[t], panel_ref[cols_ref[t]], preferred_element_type=jnp.float32)
            prods.append(jnp.where(t < count, p, jnp.zeros_like(p)))
        for i in range(group):
            r = rows_ref[base + i]
            acc_ref[r] += prods[i]
        return carry

    lax.fori_loop(0, slots // group, body, 0)
    cores, n_z, n_y, per_piece = pieces_ref.shape[:4]
    for j in range(cores * n_z * n_y):
        core_j, z_j, yh_j = j % cores, (j // cores) % n_z, j // (cores * n_z)
        pieces_ref[core_j, z_j, yh_j] = acc_ref[j * per_piece:(j + 1) * per_piece]


def block_product(row_ids, col_ids, count, dev_tiles, col_panel, row_tiles, nodes_dev):
    slots = dev_tiles.shape[0]
    feat_width = col_panel.shape[2]
    per_piece = nodes_dev // TILE
    group = 4 if slots % 4 == 0 else 1
    smem = pl.BlockSpec(memory_space=pltpu.SMEM)
    vmem = pl.BlockSpec(memory_space=pltpu.VMEM)
    return pl.pallas_call(
        functools.partial(block_product_kernel, group),
        out_shape=jax.ShapeDtypeStruct(
            (CORES, Z_RING, row_tiles // (per_piece * CORES * Z_RING), per_piece, TILE, feat_width),
            jnp.float32,
        ),
        in_specs=[smem, smem, smem, vmem, vmem],
        out_specs=vmem,
        scratch_shapes=[pltpu.VMEM((row_tiles, TILE, feat_width), jnp.float32)],
        cost_estimate=pl.CostEstimate(
            flops=2 * slots * TILE * TILE * feat_width,
            bytes_accessed=slots * TILE * TILE * 2 + row_tiles * TILE * feat_width * 4,
            transcendentals=0,
        ),
    )(row_ids, col_ids, count, dev_tiles, col_panel)


def shards(features, degrees, adj_tiles, tile_rows, tile_cols, tile_counts):
    col_count = lax.axis_size("col")
    nodes_dev = features.shape[0]
    feat_width = features.shape[1]
    tile_slots = adj_tiles.shape[2]
    dev_tiles = adj_tiles.reshape(tile_slots, TILE, TILE)
    row_ids_all = tile_rows.reshape(tile_slots)
    col_ids_all = tile_cols.reshape(tile_slots)
    live_count = tile_counts.reshape(1)
    row_tiles = nodes_dev * col_count // TILE
    norm_scale = jnp.sqrt(KNN / degrees.astype(jnp.float32))[:, None]
    teleport = ALPHA * features.astype(jnp.float32)
    current = features.astype(jnp.float32)
    for repeat in range(STEPS):
        source = (norm_scale * current).astype(jnp.bfloat16)
        col_panel = row_all_gather(source).reshape(-1, TILE, feat_width)
        pieces = block_product(
            row_ids_all, col_ids_all, live_count, dev_tiles, col_panel, row_tiles, nodes_dev
        )
        own_rows = col_reduce_scatter(pieces.reshape(pieces.shape[:3] + (nodes_dev, feat_width)))
        current = (1.0 - ALPHA) * norm_scale * own_rows + teleport
    return current.astype(jnp.bfloat16)


def solution(mesh):
    return jax.shard_map(
        shards,
        mesh=mesh,
        in_specs=(
            P(("row", "col"), None),
            P(("row", "col")),
            P("row", "col", None, None),
            P("row", "col", None),
            P("row", "col", None),
            P("row", "col"),
        ),
        out_specs=P(("row", "col"), None),
        check_vma=False,
    )
```

```python
import functools

import jax
import jax.numpy as jnp
from jax import lax
from jax.experimental import pallas as pl
from jax.experimental.pallas import tpu as pltpu
from jax.sharding import PartitionSpec as P

TILE = 64
KNN = 32
STEPS = 2

MESH = pl.DeviceIdType.MESH

ALPHA = 0.1


CORES = 2
Z_RING = 8


def reduce_scatter_kernel(n_z, chunks, x_ref, out_ref, ra, recv_cw, recv_ccw, send_cw, send_ccw,
                          fin, y_recv, a_sems, cw_sems, ccw_sems, y_sems):
    c = lax.axis_index("col")
    row = lax.axis_index("row")
    core = lax.rem(c, CORES)
    z = lax.rem(c // CORES, n_z)
    yh = c // (CORES * n_z)

    def dev(yh_, z_, core_):
        return (row, (yh_ * n_z + z_) * CORES + core_)

    partner = dev(yh, z, 1 - core)
    right = dev(yh, lax.rem(z + 1, n_z), core)
    left = dev(yh, lax.rem(z + n_z - 1, n_z), core)
    y_partner = dev(1 - yh, z, core)

    barrier = pltpu.get_barrier_semaphore()
    for peer in (partner, right, left, y_partner):
        pl.semaphore_signal(barrier, inc=1, device_id=peer, device_id_type=MESH)
    pl.semaphore_wait(barrier, 4)

    def rcopy(src, dst, sems, idx, peer):
        return pltpu.make_async_remote_copy(
            src_ref=src, dst_ref=dst, send_sem=sems.at[(0,) + idx], recv_sem=sems.at[(1,) + idx],
            device_id=peer, device_id_type=MESH,
        )

    def first(d):
        return lax.rem(z + (n_z - 1 if d == 0 else 1), n_z)

    def got(d, s):
        return lax.rem(z + ((2 * n_z - s - 2) if d == 0 else (s + 2)), n_z)

    need = [(first(0), 0), (first(1), 1)]
    for s in range(n_z - 1):
        need += [(got(0, s), 0), (got(1, s), 1)]
    copies_a = []
    for k, (g, h) in enumerate(need):
        cp = rcopy(x_ref.at[1 - core, g, h], ra.at[g, h], a_sems, (k,), partner)
        cp.start()
        copies_a.append(cp)

    def ready(d, s):
        copies_a[d if s < 0 else 2 + 2 * s + d].wait_recv()

    size = x_ref.shape[3] // chunks
    recv = (recv_cw, recv_ccw)
    send = (send_cw, send_ccw)
    sems = (cw_sems, ccw_sems)
    to = (right, left)
    sends = list(copies_a)

    def ring_copy(d, s, i):
        part = pl.ds(i * size, size)
        return rcopy(send[d].at[s, part], recv[d].at[s, part], sems[d], (s, i), to[d])

    def y_copy(i):
        part = pl.ds(i * size, size)
        return rcopy(fin.at[1 - yh, part], y_recv.at[part], y_sems, (i,), y_partner)

    for d in range(2):
        ready(d, -1)
        g = first(d)
        send[d][0] = x_ref[core, g, d] + ra[g, d]
        for i in range(chunks):
            cp = ring_copy(d, 0, i)
            cp.start()
            sends.append(cp)
    for s in range(n_z - 1):
        for d in range(2):
            ready(d, s)
        for i in range(chunks):
            part = pl.ds(i * size, size)
            for d in range(2):
                g = got(d, s)
                ring_copy(d, s, i).wait_recv()
                val = recv[d][s, part] + x_ref[core, g, d, part] + ra[g, d, part]
                if s < n_z - 2:
                    send[d][s + 1, part] = val
                    cp = ring_copy(d, s + 1, i)
                    cp.start()
                    sends.append(cp)
                else:
                    fin[d, part] = val
            if s == n_z - 2:
                cp = y_copy(i)
                cp.start()
                sends.append(cp)

    for i in range(chunks):
        part = pl.ds(i * size, size)
        y_copy(i).wait_recv()
        out_ref[part] = fin[yh, part] + y_recv[part]
    for cp in sends:
        cp.wait_send()


RS_CHUNKS = 4


def col_reduce_scatter(pieces):
    cores, n_z, n_y, nodes_dev, feat_width = pieces.shape
    chunks = RS_CHUNKS
    piece = (nodes_dev, feat_width)
    vmem = pl.BlockSpec(memory_space=pltpu.VMEM)
    return pl.pallas_call(
        functools.partial(reduce_scatter_kernel, n_z, chunks),
        out_shape=jax.ShapeDtypeStruct(piece, jnp.float32),
        in_specs=[vmem],
        out_specs=vmem,
        scratch_shapes=[
            pltpu.VMEM((n_z, n_y) + piece, jnp.float32),
            pltpu.VMEM((n_z - 1,) + piece, jnp.float32),
            pltpu.VMEM((n_z - 1,) + piece, jnp.float32),
            pltpu.VMEM((n_z - 1,) + piece, jnp.float32),
            pltpu.VMEM((n_z - 1,) + piece, jnp.float32),
            pltpu.VMEM((n_y,) + piece, jnp.float32),
            pltpu.VMEM(piece, jnp.float32),
            pltpu.SemaphoreType.DMA((2, 2 * n_z)),
            pltpu.SemaphoreType.DMA((2, n_z - 1, chunks)),
            pltpu.SemaphoreType.DMA((2, n_z - 1, chunks)),
            pltpu.SemaphoreType.DMA((2, chunks)),
        ],
        compiler_params=pltpu.CompilerParams(collective_id=0, has_side_effects=True),
    )(pieces)


def all_gather_kernel(n, src_ref, out_ref, send_sem, recv_sem):
    me = lax.axis_index("row")
    col = lax.axis_index("col")

    barrier = pltpu.get_barrier_semaphore()

    def greet(k, carry):
        peer = lax.rem(me + k, n)
        pl.semaphore_signal(barrier, inc=1, device_id=(peer, col), device_id_type=MESH)
        return carry

    lax.fori_loop(1, n, greet, 0)
    pl.semaphore_wait(barrier, n - 1)

    def copy(peer, slot):
        return pltpu.make_async_remote_copy(
            src_ref=src_ref,
            dst_ref=out_ref.at[slot],
            send_sem=send_sem.at[peer],
            recv_sem=recv_sem.at[slot],
            device_id=(peer, col),
            device_id_type=MESH,
        )

    def start(k, carry):
        copy(lax.rem(me + k, n), me).start()
        return carry

    lax.fori_loop(1, n, start, 0)
    out_ref[me] = src_ref[...]

    def finish(k, carry):
        sender = lax.rem(me + n - k, n)
        copy(sender, sender).wait_recv()
        copy(lax.rem(me + k, n), me).wait_send()
        return carry

    lax.fori_loop(1, n, finish, 0)


def row_all_gather(source):
    n = lax.axis_size("row")
    nodes_dev, feat_width = source.shape
    vmem = pl.BlockSpec(memory_space=pltpu.VMEM)
    return pl.pallas_call(
        functools.partial(all_gather_kernel, n),
        out_shape=jax.ShapeDtypeStruct((n, nodes_dev, feat_width), source.dtype),
        in_specs=[vmem],
        out_specs=vmem,
        scratch_shapes=[pltpu.SemaphoreType.DMA((n,)), pltpu.SemaphoreType.DMA((n,))],
        compiler_params=pltpu.CompilerParams(collective_id=1, has_side_effects=True),
    )(source)


def block_product_kernel(group, rows_ref, cols_ref, count_ref, adj_ref, panel_ref,
                         pieces_ref, acc_ref):
    acc_ref[...] = jnp.zeros_like(acc_ref)
    count = count_ref[0]
    slots = adj_ref.shape[0]

    def body(g, carry):
        base = g * group
        prods = []
        for i in range(group):
            t = base + i
            p = jnp.dot(adj_ref[t], panel_ref[cols_ref[t]], preferred_element_type=jnp.float32)
            prods.append(jnp.where(t < count, p, jnp.zeros_like(p)))
        for i in range(group):
            r = rows_ref[base + i]
            acc_ref[r] += prods[i]
        return carry

    lax.fori_loop(0, slots // group, body, 0)
    cores, n_z, n_y, per_piece = pieces_ref.shape[:4]
    for j in range(cores * n_z * n_y):
        core_j, z_j, yh_j = j % cores, (j // cores) % n_z, j // (cores * n_z)
        pieces_ref[core_j, z_j, yh_j] = acc_ref[j * per_piece:(j + 1) * per_piece]


def block_product(row_ids, col_ids, count, dev_tiles, col_panel, row_tiles, nodes_dev):
    slots = dev_tiles.shape[0]
    feat_width = col_panel.shape[2]
    per_piece = nodes_dev // TILE
    group = 4 if slots % 4 == 0 else 1
    smem = pl.BlockSpec(memory_space=pltpu.SMEM)
    vmem = pl.BlockSpec(memory_space=pltpu.VMEM)
    return pl.pallas_call(
        functools.partial(block_product_kernel, group),
        out_shape=jax.ShapeDtypeStruct(
            (CORES, Z_RING, row_tiles // (per_piece * CORES * Z_RING), per_piece, TILE, feat_width),
            jnp.float32,
        ),
        in_specs=[smem, smem, smem, vmem, vmem],
        out_specs=vmem,
        scratch_shapes=[pltpu.VMEM((row_tiles, TILE, feat_width), jnp.float32)],
        cost_estimate=pl.CostEstimate(
            flops=2 * slots * TILE * TILE * feat_width,
            bytes_accessed=slots * TILE * TILE * 2 + row_tiles * TILE * feat_width * 4,
            transcendentals=0,
        ),
    )(row_ids, col_ids, count, dev_tiles, col_panel)


def shards(features, degrees, adj_tiles, tile_rows, tile_cols, tile_counts):
    col_count = lax.axis_size("col")
    nodes_dev = features.shape[0]
    feat_width = features.shape[1]
    tile_slots = adj_tiles.shape[2]
    dev_tiles = adj_tiles.reshape(tile_slots, TILE, TILE)
    row_ids_all = tile_rows.reshape(tile_slots)
    col_ids_all = tile_cols.reshape(tile_slots)
    live_count = tile_counts.reshape(1)
    row_tiles = nodes_dev * col_count // TILE
    norm_scale = jnp.sqrt(KNN / degrees.astype(jnp.float32))[:, None]
    teleport = ALPHA * features.astype(jnp.float32)
    current = features.astype(jnp.float32)
    for repeat in range(STEPS):
        source = (norm_scale * current).astype(jnp.bfloat16)
        col_panel = row_all_gather(source).reshape(-1, TILE, feat_width)
        pieces = block_product(
            row_ids_all, col_ids_all, live_count, dev_tiles, col_panel, row_tiles, nodes_dev
        )
        own_rows = col_reduce_scatter(pieces.reshape(pieces.shape[:3] + (nodes_dev, feat_width)))
        current = (1.0 - ALPHA) * norm_scale * own_rows + teleport
    return current.astype(jnp.bfloat16)


def solution(mesh):
    return jax.shard_map(
        shards,
        mesh=mesh,
        in_specs=(
            P(("row", "col"), None),
            P(("row", "col")),
            P("row", "col", None, None),
            P("row", "col", None),
            P("row", "col", None),
            P("row", "col"),
        ),
        out_specs=P(("row", "col"), None),
        check_vma=False,
    )
```

```python
import functools

import jax
import jax.numpy as jnp
from jax import lax
from jax.experimental import pallas as pl
from jax.experimental.pallas import tpu as pltpu
from jax.sharding import PartitionSpec as P

TILE = 64
KNN = 32
STEPS = 2

MESH = pl.DeviceIdType.MESH

ALPHA = 0.1


CORES = 2
Z_RING = 8


def reduce_scatter_kernel(n_z, chunks, x_ref, out_ref, ra, recv_cw, recv_ccw, send_cw, send_ccw,
                          fin, y_recv, a_sems, cw_sems, ccw_sems, y_sems):
    c = lax.axis_index("col")
    row = lax.axis_index("row")
    core = lax.rem(c, CORES)
    z = lax.rem(c // CORES, n_z)
    yh = c // (CORES * n_z)

    def dev(yh_, z_, core_):
        return (row, (yh_ * n_z + z_) * CORES + core_)

    partner = dev(yh, z, 1 - core)
    right = dev(yh, lax.rem(z + 1, n_z), core)
    left = dev(yh, lax.rem(z + n_z - 1, n_z), core)
    y_partner = dev(1 - yh, z, core)

    barrier = pltpu.get_barrier_semaphore()
    for peer in (partner, right, left, y_partner):
        pl.semaphore_signal(barrier, inc=1, device_id=peer, device_id_type=MESH)
    pl.semaphore_wait(barrier, 4)

    def rcopy(src, dst, sems, idx, peer):
        return pltpu.make_async_remote_copy(
            src_ref=src, dst_ref=dst, send_sem=sems.at[(0,) + idx], recv_sem=sems.at[(1,) + idx],
            device_id=peer, device_id_type=MESH,
        )

    def first(d):
        return lax.rem(z + (n_z - 1 if d == 0 else 1), n_z)

    def got(d, s):
        return lax.rem(z + ((2 * n_z - s - 2) if d == 0 else (s + 2)), n_z)

    need = [(first(0), 0), (first(1), 1)]
    for s in range(n_z - 1):
        need += [(got(0, s), 0), (got(1, s), 1)]
    copies_a = []
    for k, (g, h) in enumerate(need):
        cp = rcopy(x_ref.at[1 - core, g, h], ra.at[g, h], a_sems, (k,), partner)
        cp.start()
        copies_a.append(cp)

    def ready(d, s):
        copies_a[d if s < 0 else 2 + 2 * s + d].wait_recv()

    size = x_ref.shape[3] // chunks
    recv = (recv_cw, recv_ccw)
    send = (send_cw, send_ccw)
    sems = (cw_sems, ccw_sems)
    to = (right, left)
    sends = list(copies_a)

    def ring_copy(d, s, i):
        part = pl.ds(i * size, size)
        return rcopy(send[d].at[s, part], recv[d].at[s, part], sems[d], (s, i), to[d])

    def y_copy(i):
        part = pl.ds(i * size, size)
        return rcopy(fin.at[1 - yh, part], y_recv.at[part], y_sems, (i,), y_partner)

    for d in range(2):
        ready(d, -1)
        g = first(d)
        send[d][0] = x_ref[core, g, d] + ra[g, d]
        for i in range(chunks):
            cp = ring_copy(d, 0, i)
            cp.start()
            sends.append(cp)
    for s in range(n_z - 1):
        for d in range(2):
            ready(d, s)
        for i in range(chunks):
            part = pl.ds(i * size, size)
            for d in range(2):
                g = got(d, s)
                ring_copy(d, s, i).wait_recv()
                val = recv[d][s, part] + x_ref[core, g, d, part] + ra[g, d, part]
                if s < n_z - 2:
                    send[d][s + 1, part] = val
                    cp = ring_copy(d, s + 1, i)
                    cp.start()
                    sends.append(cp)
                else:
                    fin[d, part] = val
            if s == n_z - 2:
                cp = y_copy(i)
                cp.start()
                sends.append(cp)

    for i in range(chunks):
        part = pl.ds(i * size, size)
        y_copy(i).wait_recv()
        out_ref[part] = fin[yh, part] + y_recv[part]
    for cp in sends:
        cp.wait_send()


RS_CHUNKS = 4


def col_reduce_scatter(pieces):
    cores, n_z, n_y, nodes_dev, feat_width = pieces.shape
    chunks = RS_CHUNKS
    piece = (nodes_dev, feat_width)
    vmem = pl.BlockSpec(memory_space=pltpu.VMEM)
    return pl.pallas_call(
        functools.partial(reduce_scatter_kernel, n_z, chunks),
        out_shape=jax.ShapeDtypeStruct(piece, jnp.float32),
        in_specs=[vmem],
        out_specs=vmem,
        scratch_shapes=[
            pltpu.VMEM((n_z, n_y) + piece, jnp.float32),
            pltpu.VMEM((n_z - 1,) + piece, jnp.float32),
            pltpu.VMEM((n_z - 1,) + piece, jnp.float32),
            pltpu.VMEM((n_z - 1,) + piece, jnp.float32),
            pltpu.VMEM((n_z - 1,) + piece, jnp.float32),
            pltpu.VMEM((n_y,) + piece, jnp.float32),
            pltpu.VMEM(piece, jnp.float32),
            pltpu.SemaphoreType.DMA((2, 2 * n_z)),
            pltpu.SemaphoreType.DMA((2, n_z - 1, chunks)),
            pltpu.SemaphoreType.DMA((2, n_z - 1, chunks)),
            pltpu.SemaphoreType.DMA((2, chunks)),
        ],
        compiler_params=pltpu.CompilerParams(collective_id=0, has_side_effects=True),
    )(pieces)


def all_gather_kernel(n, src_ref, out_ref, send_sem, recv_sem):
    me = lax.axis_index("row")
    col = lax.axis_index("col")

    barrier = pltpu.get_barrier_semaphore()

    def greet(k, carry):
        peer = lax.rem(me + k, n)
        pl.semaphore_signal(barrier, inc=1, device_id=(peer, col), device_id_type=MESH)
        return carry

    lax.fori_loop(1, n, greet, 0)
    pl.semaphore_wait(barrier, n - 1)

    def copy(peer, slot):
        return pltpu.make_async_remote_copy(
            src_ref=src_ref,
            dst_ref=out_ref.at[slot],
            send_sem=send_sem.at[peer],
            recv_sem=recv_sem.at[slot],
            device_id=(peer, col),
            device_id_type=MESH,
        )

    def start(k, carry):
        copy(lax.rem(me + k, n), me).start()
        return carry

    lax.fori_loop(1, n, start, 0)
    out_ref[me] = src_ref[...]

    def finish(k, carry):
        sender = lax.rem(me + n - k, n)
        copy(sender, sender).wait_recv()
        copy(lax.rem(me + k, n), me).wait_send()
        return carry

    lax.fori_loop(1, n, finish, 0)


def row_all_gather(source):
    n = lax.axis_size("row")
    nodes_dev, feat_width = source.shape
    vmem = pl.BlockSpec(memory_space=pltpu.VMEM)
    return pl.pallas_call(
        functools.partial(all_gather_kernel, n),
        out_shape=jax.ShapeDtypeStruct((n, nodes_dev, feat_width), source.dtype),
        in_specs=[vmem],
        out_specs=vmem,
        scratch_shapes=[pltpu.SemaphoreType.DMA((n,)), pltpu.SemaphoreType.DMA((n,))],
        compiler_params=pltpu.CompilerParams(collective_id=1, has_side_effects=True),
    )(source)


def block_product_kernel(group, rows_ref, cols_ref, count_ref, adj_ref, panel_ref,
                         pieces_ref):
    cores, n_z, n_y, per_piece = pieces_ref.shape[:4]
    pieces_ref[...] = jnp.zeros_like(pieces_ref)
    count = count_ref[0]
    slots = adj_ref.shape[0]

    def body(g, carry):
        base = g * group
        prods = []
        for i in range(group):
            t = base + i
            p = jnp.dot(adj_ref[t], panel_ref[cols_ref[t]], preferred_element_type=jnp.float32)
            prods.append(jnp.where(t < count, p, jnp.zeros_like(p)))
        for i in range(group):
            r = rows_ref[base + i]
            j = r // per_piece
            at = (lax.rem(j, cores), lax.rem(j // cores, n_z), j // (cores * n_z), lax.rem(r, per_piece))
            pieces_ref[at] += prods[i]
        return carry

    lax.fori_loop(0, slots // group, body, 0)


def block_product(row_ids, col_ids, count, dev_tiles, col_panel, row_tiles, nodes_dev):
    slots = dev_tiles.shape[0]
    feat_width = col_panel.shape[2]
    per_piece = nodes_dev // TILE
    group = 4 if slots % 4 == 0 else 1
    smem = pl.BlockSpec(memory_space=pltpu.SMEM)
    vmem = pl.BlockSpec(memory_space=pltpu.VMEM)
    return pl.pallas_call(
        functools.partial(block_product_kernel, group),
        out_shape=jax.ShapeDtypeStruct(
            (CORES, Z_RING, row_tiles // (per_piece * CORES * Z_RING), per_piece, TILE, feat_width),
            jnp.float32,
        ),
        in_specs=[smem, smem, smem, vmem, vmem],
        out_specs=vmem,
        cost_estimate=pl.CostEstimate(
            flops=2 * slots * TILE * TILE * feat_width,
            bytes_accessed=slots * TILE * TILE * 2 + row_tiles * TILE * feat_width * 4,
            transcendentals=0,
        ),
    )(row_ids, col_ids, count, dev_tiles, col_panel)


def shards(features, degrees, adj_tiles, tile_rows, tile_cols, tile_counts):
    col_count = lax.axis_size("col")
    nodes_dev = features.shape[0]
    feat_width = features.shape[1]
    tile_slots = adj_tiles.shape[2]
    dev_tiles = adj_tiles.reshape(tile_slots, TILE, TILE)
    row_ids_all = tile_rows.reshape(tile_slots)
    col_ids_all = tile_cols.reshape(tile_slots)
    live_count = tile_counts.reshape(1)
    row_tiles = nodes_dev * col_count // TILE
    norm_scale = jnp.sqrt(KNN / degrees.astype(jnp.float32))[:, None]
    teleport = ALPHA * features.astype(jnp.float32)
    current = features.astype(jnp.float32)
    for repeat in range(STEPS):
        source = (norm_scale * current).astype(jnp.bfloat16)
        col_panel = row_all_gather(source).reshape(-1, TILE, feat_width)
        pieces = block_product(
            row_ids_all, col_ids_all, live_count, dev_tiles, col_panel, row_tiles, nodes_dev
        )
        own_rows = col_reduce_scatter(pieces.reshape(pieces.shape[:3] + (nodes_dev, feat_width)))
        current = (1.0 - ALPHA) * norm_scale * own_rows + teleport
    return current.astype(jnp.bfloat16)


def solution(mesh):
    return jax.shard_map(
        shards,
        mesh=mesh,
        in_specs=(
            P(("row", "col"), None),
            P(("row", "col")),
            P("row", "col", None, None),
            P("row", "col", None),
            P("row", "col", None),
            P("row", "col"),
        ),
        out_specs=P(("row", "col"), None),
        check_vma=False,
    )
```

```python
import functools

import jax
import jax.numpy as jnp
from jax import lax
from jax.experimental import pallas as pl
from jax.experimental.pallas import tpu as pltpu
from jax.sharding import PartitionSpec as P

TILE = 64
KNN = 32
STEPS = 2

MESH = pl.DeviceIdType.MESH

ALPHA = 0.1


CORES = 2
Z_RING = 8


def reduce_scatter_kernel(n_z, chunks, last, x_ref, s9_ref, scale_ref, tele_ref, out_ref, ra,
                          recv_cw, recv_ccw, send_cw, send_ccw, fin, y_recv,
                          a_sems, cw_sems, ccw_sems, y_sems, *ag_sems):
    c = lax.axis_index("col")
    row = lax.axis_index("row")
    core = lax.rem(c, CORES)
    z = lax.rem(c // CORES, n_z)
    yh = c // (CORES * n_z)

    def dev(yh_, z_, core_):
        return (row, (yh_ * n_z + z_) * CORES + core_)

    partner = dev(yh, z, 1 - core)
    right = dev(yh, lax.rem(z + 1, n_z), core)
    left = dev(yh, lax.rem(z + n_z - 1, n_z), core)
    y_partner = dev(1 - yh, z, core)

    n_row = lax.axis_size("row")
    barrier = pltpu.get_barrier_semaphore()
    for peer in (partner, right, left, y_partner):
        pl.semaphore_signal(barrier, inc=1, device_id=peer, device_id_type=MESH)
    if not last:
        def greet(k, carry):
            pl.semaphore_signal(barrier, inc=1, device_id=(lax.rem(row + k, n_row), c),
                                device_id_type=MESH)
            return carry

        lax.fori_loop(1, n_row, greet, 0)
    pl.semaphore_wait(barrier, 4 if last else 3 + n_row)

    def rcopy(src, dst, sems, idx, peer):
        return pltpu.make_async_remote_copy(
            src_ref=src, dst_ref=dst, send_sem=sems.at[(0,) + idx], recv_sem=sems.at[(1,) + idx],
            device_id=peer, device_id_type=MESH,
        )

    def first(d):
        return lax.rem(z + (n_z - 1 if d == 0 else 1), n_z)

    def got(d, s):
        return lax.rem(z + ((2 * n_z - s - 2) if d == 0 else (s + 2)), n_z)

    need = [(first(0), 0), (first(1), 1)]
    for s in range(n_z - 1):
        need += [(got(0, s), 0), (got(1, s), 1)]
    copies_a = []
    for k, (g, h) in enumerate(need):
        cp = rcopy(x_ref.at[1 - core, g, h], ra.at[g, h], a_sems, (k,), partner)
        cp.start()
        copies_a.append(cp)

    def ready(d, s):
        copies_a[d if s < 0 else 2 + 2 * s + d].wait_recv()

    size = x_ref.shape[3] // chunks
    recv = (recv_cw, recv_ccw)
    send = (send_cw, send_ccw)
    sems = (cw_sems, ccw_sems)
    to = (right, left)
    sends = list(copies_a)

    def ring_copy(d, s, i):
        part = pl.ds(i * size, size)
        return rcopy(send[d].at[s, part], recv[d].at[s, part], sems[d], (s, i), to[d])

    def y_copy(i):
        part = pl.ds(i * size, size)
        return rcopy(fin.at[1 - yh, part], y_recv.at[part], y_sems, (i,), y_partner)

    for d in range(2):
        ready(d, -1)
        g = first(d)
        send[d][0] = x_ref[core, g, d] + ra[g, d]
        for i in range(chunks):
            cp = ring_copy(d, 0, i)
            cp.start()
            sends.append(cp)
    for s in range(n_z - 1):
        for d in range(2):
            ready(d, s)
        for i in range(chunks):
            part = pl.ds(i * size, size)
            for d in range(2):
                g = got(d, s)
                ring_copy(d, s, i).wait_recv()
                val = recv[d][s, part] + x_ref[core, g, d, part] + ra[g, d, part]
                if s < n_z - 2:
                    send[d][s + 1, part] = val
                    cp = ring_copy(d, s + 1, i)
                    cp.start()
                    sends.append(cp)
                else:
                    fin[d, part] = val
            if s == n_z - 2:
                cp = y_copy(i)
                cp.start()
                sends.append(cp)

    for i in range(chunks):
        part = pl.ds(i * size, size)
        y_copy(i).wait_recv()
        own = fin[yh, part] + y_recv[part]
        current = s9_ref[part] * own + tele_ref[part]
        if last:
            out_ref[part] = current.astype(out_ref.dtype)
        else:
            out_ref[row, part] = (scale_ref[part] * current).astype(out_ref.dtype)
    if not last:
        ag_send, ag_recv = ag_sems

        def ag_copy(peer, slot):
            return pltpu.make_async_remote_copy(
                src_ref=out_ref.at[row], dst_ref=out_ref.at[slot], send_sem=ag_send.at[peer],
                recv_sem=ag_recv.at[slot], device_id=(peer, c), device_id_type=MESH,
            )

        def ag_start(k, carry):
            ag_copy(lax.rem(row + k, n_row), row).start()
            return carry

        lax.fori_loop(1, n_row, ag_start, 0)

        def ag_finish(k, carry):
            sender = lax.rem(row + n_row - k, n_row)
            ag_copy(sender, sender).wait_recv()
            ag_copy(lax.rem(row + k, n_row), row).wait_send()
            return carry

        lax.fori_loop(1, n_row, ag_finish, 0)
    for cp in sends:
        cp.wait_send()


RS_CHUNKS = 4


def col_reduce_scatter(pieces, s9, scale, tele, last):
    cores, n_z, n_y, nodes_dev, feat_width = pieces.shape
    n_row = lax.axis_size("row")
    chunks = RS_CHUNKS
    piece = (nodes_dev, feat_width)
    vmem = pl.BlockSpec(memory_space=pltpu.VMEM)
    out_shape = piece if last else (n_row,) + piece
    ag_sems = [] if last else [pltpu.SemaphoreType.DMA((n_row,))] * 2
    return pl.pallas_call(
        functools.partial(reduce_scatter_kernel, n_z, chunks, last),
        out_shape=jax.ShapeDtypeStruct(out_shape, jnp.bfloat16),
        in_specs=[vmem] * 4,
        out_specs=vmem,
        scratch_shapes=[
            pltpu.VMEM((n_z, n_y) + piece, jnp.float32),
            pltpu.VMEM((n_z - 1,) + piece, jnp.float32),
            pltpu.VMEM((n_z - 1,) + piece, jnp.float32),
            pltpu.VMEM((n_z - 1,) + piece, jnp.float32),
            pltpu.VMEM((n_z - 1,) + piece, jnp.float32),
            pltpu.VMEM((n_y,) + piece, jnp.float32),
            pltpu.VMEM(piece, jnp.float32),
            pltpu.SemaphoreType.DMA((2, 2 * n_z)),
            pltpu.SemaphoreType.DMA((2, n_z - 1, chunks)),
            pltpu.SemaphoreType.DMA((2, n_z - 1, chunks)),
            pltpu.SemaphoreType.DMA((2, chunks)),
        ] + ag_sems,
        compiler_params=pltpu.CompilerParams(collective_id=2 if last else 0, has_side_effects=True),
    )(pieces, s9, scale, tele)


def all_gather_kernel(n, src_ref, out_ref, send_sem, recv_sem):
    me = lax.axis_index("row")
    col = lax.axis_index("col")

    barrier = pltpu.get_barrier_semaphore()

    def greet(k, carry):
        peer = lax.rem(me + k, n)
        pl.semaphore_signal(barrier, inc=1, device_id=(peer, col), device_id_type=MESH)
        return carry

    lax.fori_loop(1, n, greet, 0)
    pl.semaphore_wait(barrier, n - 1)

    def copy(peer, slot):
        return pltpu.make_async_remote_copy(
            src_ref=src_ref,
            dst_ref=out_ref.at[slot],
            send_sem=send_sem.at[peer],
            recv_sem=recv_sem.at[slot],
            device_id=(peer, col),
            device_id_type=MESH,
        )

    def start(k, carry):
        copy(lax.rem(me + k, n), me).start()
        return carry

    lax.fori_loop(1, n, start, 0)
    out_ref[me] = src_ref[...]

    def finish(k, carry):
        sender = lax.rem(me + n - k, n)
        copy(sender, sender).wait_recv()
        copy(lax.rem(me + k, n), me).wait_send()
        return carry

    lax.fori_loop(1, n, finish, 0)


def row_all_gather(source):
    n = lax.axis_size("row")
    nodes_dev, feat_width = source.shape
    vmem = pl.BlockSpec(memory_space=pltpu.VMEM)
    return pl.pallas_call(
        functools.partial(all_gather_kernel, n),
        out_shape=jax.ShapeDtypeStruct((n, nodes_dev, feat_width), source.dtype),
        in_specs=[vmem],
        out_specs=vmem,
        scratch_shapes=[pltpu.SemaphoreType.DMA((n,)), pltpu.SemaphoreType.DMA((n,))],
        compiler_params=pltpu.CompilerParams(collective_id=1, has_side_effects=True),
    )(source)


def block_product_kernel(group, rows_ref, cols_ref, count_ref, adj_ref, panel_ref,
                         pieces_ref):
    cores, n_z, n_y, per_piece = pieces_ref.shape[:4]
    pieces_ref[...] = jnp.zeros_like(pieces_ref)
    count = count_ref[0]
    slots = adj_ref.shape[0]

    def body(g, carry):
        base = g * group
        prods = []
        for i in range(group):
            t = base + i
            p = jnp.dot(adj_ref[t], panel_ref[cols_ref[t]], preferred_element_type=jnp.float32)
            prods.append(jnp.where(t < count, p, jnp.zeros_like(p)))
        for i in range(group):
            r = rows_ref[base + i]
            j = r // per_piece
            at = (lax.rem(j, cores), lax.rem(j // cores, n_z), j // (cores * n_z), lax.rem(r, per_piece))
            pieces_ref[at] += prods[i]
        return carry

    lax.fori_loop(0, slots // group, body, 0)


def block_product(row_ids, col_ids, count, dev_tiles, col_panel, row_tiles, nodes_dev):
    slots = dev_tiles.shape[0]
    feat_width = col_panel.shape[2]
    per_piece = nodes_dev // TILE
    group = 4 if slots % 4 == 0 else 1
    smem = pl.BlockSpec(memory_space=pltpu.SMEM)
    vmem = pl.BlockSpec(memory_space=pltpu.VMEM)
    return pl.pallas_call(
        functools.partial(block_product_kernel, group),
        out_shape=jax.ShapeDtypeStruct(
            (CORES, Z_RING, row_tiles // (per_piece * CORES * Z_RING), per_piece, TILE, feat_width),
            jnp.float32,
        ),
        in_specs=[smem, smem, smem, vmem, vmem],
        out_specs=vmem,
        cost_estimate=pl.CostEstimate(
            flops=2 * slots * TILE * TILE * feat_width,
            bytes_accessed=slots * TILE * TILE * 2 + row_tiles * TILE * feat_width * 4,
            transcendentals=0,
        ),
    )(row_ids, col_ids, count, dev_tiles, col_panel)


def shards(features, degrees, adj_tiles, tile_rows, tile_cols, tile_counts):
    col_count = lax.axis_size("col")
    nodes_dev = features.shape[0]
    feat_width = features.shape[1]
    tile_slots = adj_tiles.shape[2]
    dev_tiles = adj_tiles.reshape(tile_slots, TILE, TILE)
    row_ids_all = tile_rows.reshape(tile_slots)
    col_ids_all = tile_cols.reshape(tile_slots)
    live_count = tile_counts.reshape(1)
    row_tiles = nodes_dev * col_count // TILE
    norm_scale = jnp.sqrt(KNN / degrees.astype(jnp.float32))[:, None]
    teleport = ALPHA * features.astype(jnp.float32)
    scale9 = jnp.broadcast_to((1.0 - ALPHA) * norm_scale, features.shape)
    scale = jnp.broadcast_to(norm_scale, features.shape)
    source = (norm_scale * features.astype(jnp.float32)).astype(jnp.bfloat16)
    gathered = row_all_gather(source)
    for repeat in range(STEPS):
        col_panel = gathered.reshape(-1, TILE, feat_width)
        pieces = block_product(
            row_ids_all, col_ids_all, live_count, dev_tiles, col_panel, row_tiles, nodes_dev
        )
        gathered = col_reduce_scatter(
            pieces.reshape(pieces.shape[:3] + (nodes_dev, feat_width)),
            scale9, scale, teleport, repeat == STEPS - 1,
        )
    return gathered


def solution(mesh):
    return jax.shard_map(
        shards,
        mesh=mesh,
        in_specs=(
            P(("row", "col"), None),
            P(("row", "col")),
            P("row", "col", None, None),
            P("row", "col", None),
            P("row", "col", None),
            P("row", "col"),
        ),
        out_specs=P(("row", "col"), None),
        check_vma=False,
    )
```

```python
import functools

import jax
import jax.numpy as jnp
from jax import lax
from jax.experimental import pallas as pl
from jax.experimental.pallas import tpu as pltpu
from jax.sharding import PartitionSpec as P

TILE = 64
KNN = 32
STEPS = 2

MESH = pl.DeviceIdType.MESH

ALPHA = 0.1


CORES = 2
Z_RING = 8


def reduce_scatter_kernel(n_z, chunks, last, x_ref, s9_ref, scale_ref, tele_ref, out_ref, ra,
                          recv_cw, recv_ccw, send_cw, send_ccw, fin, y_recv,
                          a_sems, cw_sems, ccw_sems, y_sems, *ag_sems):
    c = lax.axis_index("col")
    row = lax.axis_index("row")
    core = lax.rem(c, CORES)
    z = lax.rem(c // CORES, n_z)
    yh = c // (CORES * n_z)

    def dev(yh_, z_, core_):
        return (row, (yh_ * n_z + z_) * CORES + core_)

    partner = dev(yh, z, 1 - core)
    right = dev(yh, lax.rem(z + 1, n_z), core)
    left = dev(yh, lax.rem(z + n_z - 1, n_z), core)
    y_partner = dev(1 - yh, z, core)

    n_row = lax.axis_size("row")
    barrier = pltpu.get_barrier_semaphore()
    for peer in (partner, right, left, y_partner):
        pl.semaphore_signal(barrier, inc=1, device_id=peer, device_id_type=MESH)
    if not last:
        def greet(k, carry):
            pl.semaphore_signal(barrier, inc=1, device_id=(lax.rem(row + k, n_row), c),
                                device_id_type=MESH)
            return carry

        lax.fori_loop(1, n_row, greet, 0)
    pl.semaphore_wait(barrier, 4 if last else 3 + n_row)

    def rcopy(src, dst, sems, idx, peer):
        return pltpu.make_async_remote_copy(
            src_ref=src, dst_ref=dst, send_sem=sems.at[(0,) + idx], recv_sem=sems.at[(1,) + idx],
            device_id=peer, device_id_type=MESH,
        )

    def first(d):
        return lax.rem(z + (n_z - 1 if d == 0 else 1), n_z)

    def got(d, s):
        return lax.rem(z + ((2 * n_z - s - 2) if d == 0 else (s + 2)), n_z)

    need = [(first(0), 0), (first(1), 1)]
    for s in range(n_z - 1):
        need += [(got(0, s), 0), (got(1, s), 1)]
    copies_a = []
    for k, (g, h) in enumerate(need):
        cp = rcopy(x_ref.at[1 - core, g, h], ra.at[g, h], a_sems, (k,), partner)
        cp.start()
        copies_a.append(cp)

    def ready(d, s):
        copies_a[d if s < 0 else 2 + 2 * s + d].wait_recv()

    size = x_ref.shape[3] // chunks
    recv = (recv_cw, recv_ccw)
    send = (send_cw, send_ccw)
    sems = (cw_sems, ccw_sems)
    to = (right, left)
    sends = list(copies_a)

    def ring_copy(d, s, i):
        part = pl.ds(i * size, size)
        return rcopy(send[d].at[s, part], recv[d].at[s, part], sems[d], (s, i), to[d])

    def y_copy(i):
        part = pl.ds(i * size, size)
        return rcopy(fin.at[1 - yh, part], y_recv.at[part], y_sems, (i,), y_partner)

    for d in range(2):
        ready(d, -1)
        g = first(d)
        send[d][0] = x_ref[core, g, d] + ra[g, d]
        for i in range(chunks):
            cp = ring_copy(d, 0, i)
            cp.start()
            sends.append(cp)
    for s in range(n_z - 1):
        for d in range(2):
            ready(d, s)
        for i in range(chunks):
            part = pl.ds(i * size, size)
            for d in range(2):
                g = got(d, s)
                ring_copy(d, s, i).wait_recv()
                val = recv[d][s, part] + x_ref[core, g, d, part] + ra[g, d, part]
                if s < n_z - 2:
                    send[d][s + 1, part] = val
                    cp = ring_copy(d, s + 1, i)
                    cp.start()
                    sends.append(cp)
                else:
                    fin[d, part] = val
            if s == n_z - 2:
                cp = y_copy(i)
                cp.start()
                sends.append(cp)

    for i in range(chunks):
        part = pl.ds(i * size, size)
        y_copy(i).wait_recv()
        own = fin[yh, part] + y_recv[part]
        current = s9_ref[part] * own + tele_ref[part]
        if last:
            out_ref[part] = current.astype(out_ref.dtype)
        else:
            out_ref[row, part] = (scale_ref[part] * current).astype(out_ref.dtype)
    if not last:
        ag_send, ag_recv = ag_sems

        def ag_copy(peer, slot):
            return pltpu.make_async_remote_copy(
                src_ref=out_ref.at[row], dst_ref=out_ref.at[slot], send_sem=ag_send.at[peer],
                recv_sem=ag_recv.at[slot], device_id=(peer, c), device_id_type=MESH,
            )

        def ag_start(k, carry):
            ag_copy(lax.rem(row + k, n_row), row).start()
            return carry

        lax.fori_loop(1, n_row, ag_start, 0)

        def ag_finish(k, carry):
            sender = lax.rem(row + n_row - k, n_row)
            ag_copy(sender, sender).wait_recv()
            ag_copy(lax.rem(row + k, n_row), row).wait_send()
            return carry

        lax.fori_loop(1, n_row, ag_finish, 0)
    for cp in sends:
        cp.wait_send()


RS_CHUNKS = 4


def col_reduce_scatter(pieces, s9, scale, tele, last):
    cores, n_z, n_y, nodes_dev, feat_width = pieces.shape
    n_row = lax.axis_size("row")
    chunks = RS_CHUNKS
    piece = (nodes_dev, feat_width)
    vmem = pl.BlockSpec(memory_space=pltpu.VMEM)
    out_shape = piece if last else (n_row,) + piece
    ag_sems = [] if last else [pltpu.SemaphoreType.DMA((n_row,))] * 2
    return pl.pallas_call(
        functools.partial(reduce_scatter_kernel, n_z, chunks, last),
        out_shape=jax.ShapeDtypeStruct(out_shape, jnp.bfloat16),
        in_specs=[vmem] * 4,
        out_specs=vmem,
        scratch_shapes=[
            pltpu.VMEM((n_z, n_y) + piece, jnp.float32),
            pltpu.VMEM((n_z - 1,) + piece, jnp.float32),
            pltpu.VMEM((n_z - 1,) + piece, jnp.float32),
            pltpu.VMEM((n_z - 1,) + piece, jnp.float32),
            pltpu.VMEM((n_z - 1,) + piece, jnp.float32),
            pltpu.VMEM((n_y,) + piece, jnp.float32),
            pltpu.VMEM(piece, jnp.float32),
            pltpu.SemaphoreType.DMA((2, 2 * n_z)),
            pltpu.SemaphoreType.DMA((2, n_z - 1, chunks)),
            pltpu.SemaphoreType.DMA((2, n_z - 1, chunks)),
            pltpu.SemaphoreType.DMA((2, chunks)),
        ] + ag_sems,
        compiler_params=pltpu.CompilerParams(collective_id=2 if last else 0, has_side_effects=True),
    )(pieces, s9, scale, tele)


def all_gather_kernel(n, src_ref, out_ref, send_sem, recv_sem):
    me = lax.axis_index("row")
    col = lax.axis_index("col")

    barrier = pltpu.get_barrier_semaphore()

    def greet(k, carry):
        peer = lax.rem(me + k, n)
        pl.semaphore_signal(barrier, inc=1, device_id=(peer, col), device_id_type=MESH)
        return carry

    lax.fori_loop(1, n, greet, 0)
    pl.semaphore_wait(barrier, n - 1)

    def copy(peer, slot):
        return pltpu.make_async_remote_copy(
            src_ref=src_ref,
            dst_ref=out_ref.at[slot],
            send_sem=send_sem.at[peer],
            recv_sem=recv_sem.at[slot],
            device_id=(peer, col),
            device_id_type=MESH,
        )

    def start(k, carry):
        copy(lax.rem(me + k, n), me).start()
        return carry

    lax.fori_loop(1, n, start, 0)
    out_ref[me] = src_ref[...]

    def finish(k, carry):
        sender = lax.rem(me + n - k, n)
        copy(sender, sender).wait_recv()
        copy(lax.rem(me + k, n), me).wait_send()
        return carry

    lax.fori_loop(1, n, finish, 0)


def row_all_gather(source):
    n = lax.axis_size("row")
    nodes_dev, feat_width = source.shape
    vmem = pl.BlockSpec(memory_space=pltpu.VMEM)
    return pl.pallas_call(
        functools.partial(all_gather_kernel, n),
        out_shape=jax.ShapeDtypeStruct((n, nodes_dev, feat_width), source.dtype),
        in_specs=[vmem],
        out_specs=vmem,
        scratch_shapes=[pltpu.SemaphoreType.DMA((n,)), pltpu.SemaphoreType.DMA((n,))],
        compiler_params=pltpu.CompilerParams(collective_id=1, has_side_effects=True),
    )(source)


def block_product_kernel(group, rows_ref, cols_ref, count_ref, adj_ref, panel_ref,
                         pieces_ref):
    cores, n_z, n_y, per_piece = pieces_ref.shape[:4]
    pieces_ref[...] = jnp.zeros_like(pieces_ref)
    count = count_ref[0]
    slots = adj_ref.shape[0]

    def body(g, carry):
        base = g * group
        prods = []
        for i in range(group):
            t = base + i
            p = jnp.dot(adj_ref[t], panel_ref[cols_ref[t]], preferred_element_type=jnp.float32)
            prods.append(jnp.where(t < count, p, jnp.zeros_like(p)))
        for i in range(group):
            r = rows_ref[base + i]
            j = r // per_piece
            at = (lax.rem(j, cores), lax.rem(j // cores, n_z), j // (cores * n_z), lax.rem(r, per_piece))
            pieces_ref[at] += prods[i]
        return carry

    lax.fori_loop(0, slots // group, body, 0)


def block_product(row_ids, col_ids, count, dev_tiles, col_panel, row_tiles, nodes_dev):
    slots = dev_tiles.shape[0]
    feat_width = col_panel.shape[2]
    per_piece = nodes_dev // TILE
    group = 16 if slots % 16 == 0 else 1
    smem = pl.BlockSpec(memory_space=pltpu.SMEM)
    vmem = pl.BlockSpec(memory_space=pltpu.VMEM)
    return pl.pallas_call(
        functools.partial(block_product_kernel, group),
        out_shape=jax.ShapeDtypeStruct(
            (CORES, Z_RING, row_tiles // (per_piece * CORES * Z_RING), per_piece, TILE, feat_width),
            jnp.float32,
        ),
        in_specs=[smem, smem, smem, vmem, vmem],
        out_specs=vmem,
        cost_estimate=pl.CostEstimate(
            flops=2 * slots * TILE * TILE * feat_width,
            bytes_accessed=slots * TILE * TILE * 2 + row_tiles * TILE * feat_width * 4,
            transcendentals=0,
        ),
    )(row_ids, col_ids, count, dev_tiles, col_panel)


def shards(features, degrees, adj_tiles, tile_rows, tile_cols, tile_counts):
    col_count = lax.axis_size("col")
    nodes_dev = features.shape[0]
    feat_width = features.shape[1]
    tile_slots = adj_tiles.shape[2]
    dev_tiles = adj_tiles.reshape(tile_slots, TILE, TILE)
    row_ids_all = tile_rows.reshape(tile_slots)
    col_ids_all = tile_cols.reshape(tile_slots)
    live_count = tile_counts.reshape(1)
    row_tiles = nodes_dev * col_count // TILE
    norm_scale = jnp.sqrt(KNN / degrees.astype(jnp.float32))[:, None]
    teleport = ALPHA * features.astype(jnp.float32)
    scale9 = jnp.broadcast_to((1.0 - ALPHA) * norm_scale, features.shape)
    scale = jnp.broadcast_to(norm_scale, features.shape)
    source = (norm_scale * features.astype(jnp.float32)).astype(jnp.bfloat16)
    gathered = row_all_gather(source)
    for repeat in range(STEPS):
        col_panel = gathered.reshape(-1, TILE, feat_width)
        pieces = block_product(
            row_ids_all, col_ids_all, live_count, dev_tiles, col_panel, row_tiles, nodes_dev
        )
        gathered = col_reduce_scatter(
            pieces.reshape(pieces.shape[:3] + (nodes_dev, feat_width)),
            scale9, scale, teleport, repeat == STEPS - 1,
        )
    return gathered


def solution(mesh):
    return jax.shard_map(
        shards,
        mesh=mesh,
        in_specs=(
            P(("row", "col"), None),
            P(("row", "col")),
            P("row", "col", None, None),
            P("row", "col", None),
            P("row", "col", None),
            P("row", "col"),
        ),
        out_specs=P(("row", "col"), None),
        check_vma=False,
    )
```

```python
import functools

import jax
import jax.numpy as jnp
from jax import lax
from jax.experimental import pallas as pl
from jax.experimental.pallas import tpu as pltpu
from jax.sharding import PartitionSpec as P

TILE = 64
KNN = 32
STEPS = 2

MESH = pl.DeviceIdType.MESH

ALPHA = 0.1


CORES = 2
Z_RING = 8


def reduce_scatter_kernel(n_z, chunks, last, x_ref, s9_ref, scale_ref, tele_ref, out_ref, ra,
                          recv_cw, recv_ccw, send_cw, send_ccw, fin, y_recv,
                          a_sems, cw_sems, ccw_sems, y_sems, *ag_sems):
    c = lax.axis_index("col")
    row = lax.axis_index("row")
    core = lax.rem(c, CORES)
    z = lax.rem(c // CORES, n_z)
    yh = c // (CORES * n_z)

    def dev(yh_, z_, core_):
        return (row, (yh_ * n_z + z_) * CORES + core_)

    partner = dev(yh, z, 1 - core)
    right = dev(yh, lax.rem(z + 1, n_z), core)
    left = dev(yh, lax.rem(z + n_z - 1, n_z), core)
    y_partner = dev(1 - yh, z, core)

    n_row = lax.axis_size("row")
    barrier = pltpu.get_barrier_semaphore()
    for peer in (partner, right, left, y_partner):
        pl.semaphore_signal(barrier, inc=1, device_id=peer, device_id_type=MESH)
    if not last:
        def greet(k, carry):
            pl.semaphore_signal(barrier, inc=1, device_id=(lax.rem(row + k, n_row), c),
                                device_id_type=MESH)
            return carry

        lax.fori_loop(1, n_row, greet, 0)
    pl.semaphore_wait(barrier, 4 if last else 3 + n_row)

    def rcopy(src, dst, sems, idx, peer):
        return pltpu.make_async_remote_copy(
            src_ref=src, dst_ref=dst, send_sem=sems.at[(0,) + idx], recv_sem=sems.at[(1,) + idx],
            device_id=peer, device_id_type=MESH,
        )

    def first(d):
        return lax.rem(z + (n_z - 1 if d == 0 else 1), n_z)

    def got(d, s):
        return lax.rem(z + ((2 * n_z - s - 2) if d == 0 else (s + 2)), n_z)

    need = [(first(0), 0), (first(1), 1)]
    for s in range(n_z - 1):
        need += [(got(0, s), 0), (got(1, s), 1)]
    copies_a = []
    for k, (g, h) in enumerate(need):
        cp = rcopy(x_ref.at[1 - core, g, h], ra.at[g, h], a_sems, (k,), partner)
        cp.start()
        copies_a.append(cp)

    def ready(d, s):
        copies_a[d if s < 0 else 2 + 2 * s + d].wait_recv()

    size = x_ref.shape[3] // chunks
    recv = (recv_cw, recv_ccw)
    send = (send_cw, send_ccw)
    sems = (cw_sems, ccw_sems)
    to = (right, left)
    sends = list(copies_a)

    def ring_copy(d, s, i):
        part = pl.ds(i * size, size)
        return rcopy(send[d].at[s, part], recv[d].at[s, part], sems[d], (s, i), to[d])

    def y_copy(i):
        part = pl.ds(i * size, size)
        return rcopy(fin.at[1 - yh, part], y_recv.at[part], y_sems, (i,), y_partner)

    for d in range(2):
        ready(d, -1)
        g = first(d)
        send[d][0] = x_ref[core, g, d] + ra[g, d]
        for i in range(chunks):
            cp = ring_copy(d, 0, i)
            cp.start()
            sends.append(cp)
    for s in range(n_z - 1):
        for d in range(2):
            ready(d, s)
        for i in range(chunks):
            part = pl.ds(i * size, size)
            for d in range(2):
                g = got(d, s)
                ring_copy(d, s, i).wait_recv()
                val = recv[d][s, part] + x_ref[core, g, d, part] + ra[g, d, part]
                if s < n_z - 2:
                    send[d][s + 1, part] = val
                    cp = ring_copy(d, s + 1, i)
                    cp.start()
                    sends.append(cp)
                else:
                    fin[d, part] = val
            if s == n_z - 2:
                cp = y_copy(i)
                cp.start()
                sends.append(cp)

    for i in range(chunks):
        part = pl.ds(i * size, size)
        y_copy(i).wait_recv()
        own = fin[yh, part] + y_recv[part]
        current = s9_ref[part] * own + tele_ref[part]
        if last:
            out_ref[part] = current.astype(out_ref.dtype)
        else:
            out_ref[row, part] = (scale_ref[part] * current).astype(out_ref.dtype)
    if not last:
        ag_send, ag_recv = ag_sems

        def ag_copy(peer, slot):
            return pltpu.make_async_remote_copy(
                src_ref=out_ref.at[row], dst_ref=out_ref.at[slot], send_sem=ag_send.at[peer],
                recv_sem=ag_recv.at[slot], device_id=(peer, c), device_id_type=MESH,
            )

        def ag_start(k, carry):
            ag_copy(lax.rem(row + k, n_row), row).start()
            return carry

        lax.fori_loop(1, n_row, ag_start, 0)

        def ag_finish(k, carry):
            sender = lax.rem(row + n_row - k, n_row)
            ag_copy(sender, sender).wait_recv()
            ag_copy(lax.rem(row + k, n_row), row).wait_send()
            return carry

        lax.fori_loop(1, n_row, ag_finish, 0)
    for cp in sends:
        cp.wait_send()


RS_CHUNKS = 4


def col_reduce_scatter(pieces, s9, scale, tele, last):
    cores, n_z, n_y, nodes_dev, feat_width = pieces.shape
    n_row = lax.axis_size("row")
    chunks = RS_CHUNKS
    piece = (nodes_dev, feat_width)
    vmem = pl.BlockSpec(memory_space=pltpu.VMEM)
    out_shape = piece if last else (n_row,) + piece
    ag_sems = [] if last else [pltpu.SemaphoreType.DMA((n_row,))] * 2
    return pl.pallas_call(
        functools.partial(reduce_scatter_kernel, n_z, chunks, last),
        out_shape=jax.ShapeDtypeStruct(out_shape, jnp.bfloat16),
        in_specs=[vmem] * 4,
        out_specs=vmem,
        scratch_shapes=[
            pltpu.VMEM((n_z, n_y) + piece, jnp.float32),
            pltpu.VMEM((n_z - 1,) + piece, jnp.float32),
            pltpu.VMEM((n_z - 1,) + piece, jnp.float32),
            pltpu.VMEM((n_z - 1,) + piece, jnp.float32),
            pltpu.VMEM((n_z - 1,) + piece, jnp.float32),
            pltpu.VMEM((n_y,) + piece, jnp.float32),
            pltpu.VMEM(piece, jnp.float32),
            pltpu.SemaphoreType.DMA((2, 2 * n_z)),
            pltpu.SemaphoreType.DMA((2, n_z - 1, chunks)),
            pltpu.SemaphoreType.DMA((2, n_z - 1, chunks)),
            pltpu.SemaphoreType.DMA((2, chunks)),
        ] + ag_sems,
        compiler_params=pltpu.CompilerParams(collective_id=2 if last else 0, has_side_effects=True),
    )(pieces, s9, scale, tele)


def all_gather_kernel(n, src_ref, out_ref, send_sem, recv_sem):
    me = lax.axis_index("row")
    col = lax.axis_index("col")

    barrier = pltpu.get_barrier_semaphore()

    def greet(k, carry):
        peer = lax.rem(me + k, n)
        pl.semaphore_signal(barrier, inc=1, device_id=(peer, col), device_id_type=MESH)
        return carry

    lax.fori_loop(1, n, greet, 0)
    pl.semaphore_wait(barrier, n - 1)

    def copy(peer, slot):
        return pltpu.make_async_remote_copy(
            src_ref=src_ref,
            dst_ref=out_ref.at[slot],
            send_sem=send_sem.at[peer],
            recv_sem=recv_sem.at[slot],
            device_id=(peer, col),
            device_id_type=MESH,
        )

    def start(k, carry):
        copy(lax.rem(me + k, n), me).start()
        return carry

    lax.fori_loop(1, n, start, 0)
    out_ref[me] = src_ref[...]

    def finish(k, carry):
        sender = lax.rem(me + n - k, n)
        copy(sender, sender).wait_recv()
        copy(lax.rem(me + k, n), me).wait_send()
        return carry

    lax.fori_loop(1, n, finish, 0)


def row_all_gather(source):
    n = lax.axis_size("row")
    nodes_dev, feat_width = source.shape
    vmem = pl.BlockSpec(memory_space=pltpu.VMEM)
    return pl.pallas_call(
        functools.partial(all_gather_kernel, n),
        out_shape=jax.ShapeDtypeStruct((n, nodes_dev, feat_width), source.dtype),
        in_specs=[vmem],
        out_specs=vmem,
        scratch_shapes=[pltpu.SemaphoreType.DMA((n,)), pltpu.SemaphoreType.DMA((n,))],
        compiler_params=pltpu.CompilerParams(collective_id=1, has_side_effects=True),
    )(source)


def block_product_kernel(group, rows_ref, cols_ref, count_ref, adj_ref, panel_ref,
                         pieces_ref):
    cores, n_z, n_y, per_piece = pieces_ref.shape[:4]
    pieces_ref[...] = jnp.zeros_like(pieces_ref)
    count = count_ref[0]
    slots = adj_ref.shape[0]

    def body(g, carry):
        base = g * group
        prods = []
        for i in range(group):
            t = base + i
            p = jnp.dot(adj_ref[t], panel_ref[cols_ref[t]], preferred_element_type=jnp.float32)
            prods.append(jnp.where(t < count, p, jnp.zeros_like(p)))
        for i in range(group):
            r = rows_ref[base + i]
            j = r // per_piece
            at = (lax.rem(j, cores), lax.rem(j // cores, n_z), j // (cores * n_z), lax.rem(r, per_piece))
            pieces_ref[at] += prods[i]
        return carry

    lax.fori_loop(0, slots // group, body, 0)


def block_product(row_ids, col_ids, count, dev_tiles, col_panel, row_tiles, nodes_dev):
    slots = dev_tiles.shape[0]
    feat_width = col_panel.shape[2]
    per_piece = nodes_dev // TILE
    group = 16 if slots % 16 == 0 else 1
    smem = pl.BlockSpec(memory_space=pltpu.SMEM)
    vmem = pl.BlockSpec(memory_space=pltpu.VMEM)
    return pl.pallas_call(
        functools.partial(block_product_kernel, group),
        out_shape=jax.ShapeDtypeStruct(
            (CORES, Z_RING, row_tiles // (per_piece * CORES * Z_RING), per_piece, TILE, feat_width),
            jnp.float32,
        ),
        in_specs=[smem, smem, smem, vmem, vmem],
        out_specs=vmem,
        cost_estimate=pl.CostEstimate(
            flops=2 * slots * TILE * TILE * feat_width,
            bytes_accessed=slots * TILE * TILE * 2 + row_tiles * TILE * feat_width * 4,
            transcendentals=0,
        ),
    )(row_ids, col_ids, count, dev_tiles, col_panel)


def shards(features, degrees, adj_tiles, tile_rows, tile_cols, tile_counts):
    col_count = lax.axis_size("col")
    nodes_dev = features.shape[0]
    feat_width = features.shape[1]
    tile_slots = adj_tiles.shape[2]
    dev_tiles = adj_tiles.reshape(tile_slots, TILE, TILE)
    row_ids_all = tile_rows.reshape(tile_slots)
    col_ids_all = tile_cols.reshape(tile_slots)
    live_count = tile_counts.reshape(1)
    row_tiles = nodes_dev * col_count // TILE
    norm_scale = jnp.sqrt(KNN / degrees.astype(jnp.float32))[:, None]
    teleport = ALPHA * features.astype(jnp.float32)
    scale9 = jnp.broadcast_to((1.0 - ALPHA) * norm_scale, features.shape)
    scale = jnp.broadcast_to(norm_scale, features.shape)
    source = (norm_scale * features.astype(jnp.float32)).astype(jnp.bfloat16)
    n_row = lax.axis_size("row")
    me_row = lax.axis_index("row")
    gathered = jnp.stack([source] + [
        lax.ppermute(source, "row", [(i, (i + k) % n_row) for i in range(n_row)])
        for k in range(1, n_row)
    ])
    per_piece = nodes_dev // TILE
    rotated_cols = lax.rem(me_row - col_ids_all // per_piece + n_row, n_row) * per_piece + lax.rem(
        col_ids_all, per_piece)
    for repeat in range(STEPS):
        col_panel = gathered.reshape(-1, TILE, feat_width)
        pieces = block_product(
            row_ids_all, rotated_cols if repeat == 0 else col_ids_all, live_count, dev_tiles,
            col_panel, row_tiles, nodes_dev,
        )
        gathered = col_reduce_scatter(
            pieces.reshape(pieces.shape[:3] + (nodes_dev, feat_width)),
            scale9, scale, teleport, repeat == STEPS - 1,
        )
    return gathered


def solution(mesh):
    return jax.shard_map(
        shards,
        mesh=mesh,
        in_specs=(
            P(("row", "col"), None),
            P(("row", "col")),
            P("row", "col", None, None),
            P("row", "col", None),
            P("row", "col", None),
            P("row", "col"),
        ),
        out_specs=P(("row", "col"), None),
        check_vma=False,
    )
```

```python
import functools

import jax
import jax.numpy as jnp
from jax import lax
from jax.experimental import pallas as pl
from jax.experimental.pallas import tpu as pltpu
from jax.sharding import PartitionSpec as P

TILE = 64
KNN = 32
STEPS = 2

MESH = pl.DeviceIdType.MESH

ALPHA = 0.1


CORES = 2
Z_RING = 8


def reduce_scatter_kernel(n_z, chunks, last, x_ref, s9_ref, scale_ref, tele_ref, out_ref, ra,
                          recv_cw, recv_ccw, send_cw, send_ccw, fin, y_recv,
                          a_sems, cw_sems, ccw_sems, y_sems, *ag_sems):
    c = lax.axis_index("col")
    row = lax.axis_index("row")
    core = lax.rem(c, CORES)
    z = lax.rem(c // CORES, n_z)
    yh = c // (CORES * n_z)

    def dev(yh_, z_, core_):
        return (row, (yh_ * n_z + z_) * CORES + core_)

    partner = dev(yh, z, 1 - core)
    right = dev(yh, lax.rem(z + 1, n_z), core)
    left = dev(yh, lax.rem(z + n_z - 1, n_z), core)
    y_partner = dev(1 - yh, z, core)

    n_row = lax.axis_size("row")
    barrier = pltpu.get_barrier_semaphore()
    for peer in (partner, right, left, y_partner):
        pl.semaphore_signal(barrier, inc=1, device_id=peer, device_id_type=MESH)
    if not last:
        def greet(k, carry):
            pl.semaphore_signal(barrier, inc=1, device_id=(lax.rem(row + k, n_row), c),
                                device_id_type=MESH)
            return carry

        lax.fori_loop(1, n_row, greet, 0)
    pl.semaphore_wait(barrier, 4 if last else 3 + n_row)

    def rcopy(src, dst, sems, idx, peer):
        return pltpu.make_async_remote_copy(
            src_ref=src, dst_ref=dst, send_sem=sems.at[(0,) + idx], recv_sem=sems.at[(1,) + idx],
            device_id=peer, device_id_type=MESH,
        )

    def first(d):
        return lax.rem(z + (n_z - 1 if d == 0 else 1), n_z)

    def got(d, s):
        return lax.rem(z + ((2 * n_z - s - 2) if d == 0 else (s + 2)), n_z)

    need = [(first(0), 0), (first(1), 1)]
    for s in range(n_z - 1):
        need += [(got(0, s), 0), (got(1, s), 1)]
    copies_a = []
    for k, (g, h) in enumerate(need):
        cp = rcopy(x_ref.at[1 - core, g, h], ra.at[g, h], a_sems, (k,), partner)
        cp.start()
        copies_a.append(cp)

    def ready(d, s):
        copies_a[d if s < 0 else 2 + 2 * s + d].wait_recv()

    size = x_ref.shape[3] // chunks
    recv = (recv_cw, recv_ccw)
    send = (send_cw, send_ccw)
    sems = (cw_sems, ccw_sems)
    to = (right, left)
    sends = list(copies_a)

    def ring_copy(d, s, i):
        part = pl.ds(i * size, size)
        return rcopy(send[d].at[s, part], recv[d].at[s, part], sems[d], (s, i), to[d])

    def y_copy(i):
        part = pl.ds(i * size, size)
        return rcopy(fin.at[1 - yh, part], y_recv.at[part], y_sems, (i,), y_partner)

    for d in range(2):
        ready(d, -1)
        g = first(d)
        send[d][0] = x_ref[core, g, d] + ra[g, d]
        for i in range(chunks):
            cp = ring_copy(d, 0, i)
            cp.start()
            sends.append(cp)
    for s in range(n_z - 1):
        for d in range(2):
            ready(d, s)
        for i in range(chunks):
            part = pl.ds(i * size, size)
            for d in range(2):
                g = got(d, s)
                ring_copy(d, s, i).wait_recv()
                val = recv[d][s, part] + x_ref[core, g, d, part] + ra[g, d, part]
                if s < n_z - 2:
                    send[d][s + 1, part] = val
                    cp = ring_copy(d, s + 1, i)
                    cp.start()
                    sends.append(cp)
                else:
                    fin[d, part] = val
            if s == n_z - 2:
                cp = y_copy(i)
                cp.start()
                sends.append(cp)

    for i in range(chunks):
        part = pl.ds(i * size, size)
        y_copy(i).wait_recv()
        own = fin[yh, part] + y_recv[part]
        current = s9_ref[part] * own + tele_ref[part]
        if last:
            out_ref[part] = current.astype(out_ref.dtype)
        else:
            out_ref[row, part] = (scale_ref[part] * current).astype(out_ref.dtype)
    if not last:
        ag_send, ag_recv = ag_sems

        def ag_copy(peer, slot):
            return pltpu.make_async_remote_copy(
                src_ref=out_ref.at[row], dst_ref=out_ref.at[slot], send_sem=ag_send.at[peer],
                recv_sem=ag_recv.at[slot], device_id=(peer, c), device_id_type=MESH,
            )

        def ag_start(k, carry):
            ag_copy(lax.rem(row + k, n_row), row).start()
            return carry

        lax.fori_loop(1, n_row, ag_start, 0)

        def ag_finish(k, carry):
            sender = lax.rem(row + n_row - k, n_row)
            ag_copy(sender, sender).wait_recv()
            ag_copy(lax.rem(row + k, n_row), row).wait_send()
            return carry

        lax.fori_loop(1, n_row, ag_finish, 0)
    for cp in sends:
        cp.wait_send()


RS_CHUNKS = 4


def col_reduce_scatter(pieces, s9, scale, tele, last):
    cores, n_z, n_y, nodes_dev, feat_width = pieces.shape
    n_row = lax.axis_size("row")
    chunks = RS_CHUNKS
    piece = (nodes_dev, feat_width)
    vmem = pl.BlockSpec(memory_space=pltpu.VMEM)
    out_shape = piece if last else (n_row,) + piece
    ag_sems = [] if last else [pltpu.SemaphoreType.DMA((n_row,))] * 2
    return pl.pallas_call(
        functools.partial(reduce_scatter_kernel, n_z, chunks, last),
        out_shape=jax.ShapeDtypeStruct(out_shape, jnp.bfloat16),
        in_specs=[vmem] * 4,
        out_specs=vmem,
        scratch_shapes=[
            pltpu.VMEM((n_z, n_y) + piece, jnp.float32),
            pltpu.VMEM((n_z - 1,) + piece, jnp.float32),
            pltpu.VMEM((n_z - 1,) + piece, jnp.float32),
            pltpu.VMEM((n_z - 1,) + piece, jnp.float32),
            pltpu.VMEM((n_z - 1,) + piece, jnp.float32),
            pltpu.VMEM((n_y,) + piece, jnp.float32),
            pltpu.VMEM(piece, jnp.float32),
            pltpu.SemaphoreType.DMA((2, 2 * n_z)),
            pltpu.SemaphoreType.DMA((2, n_z - 1, chunks)),
            pltpu.SemaphoreType.DMA((2, n_z - 1, chunks)),
            pltpu.SemaphoreType.DMA((2, chunks)),
        ] + ag_sems,
        compiler_params=pltpu.CompilerParams(collective_id=2 if last else 0, has_side_effects=True),
    )(pieces, s9, scale, tele)


def all_gather_kernel(n, src_ref, out_ref, send_sem, recv_sem):
    me = lax.axis_index("row")
    col = lax.axis_index("col")

    barrier = pltpu.get_barrier_semaphore()

    def greet(k, carry):
        peer = lax.rem(me + k, n)
        pl.semaphore_signal(barrier, inc=1, device_id=(peer, col), device_id_type=MESH)
        return carry

    lax.fori_loop(1, n, greet, 0)
    pl.semaphore_wait(barrier, n - 1)

    def copy(peer, slot):
        return pltpu.make_async_remote_copy(
            src_ref=src_ref,
            dst_ref=out_ref.at[slot],
            send_sem=send_sem.at[peer],
            recv_sem=recv_sem.at[slot],
            device_id=(peer, col),
            device_id_type=MESH,
        )

    def start(k, carry):
        copy(lax.rem(me + k, n), me).start()
        return carry

    lax.fori_loop(1, n, start, 0)
    out_ref[me] = src_ref[...]

    def finish(k, carry):
        sender = lax.rem(me + n - k, n)
        copy(sender, sender).wait_recv()
        copy(lax.rem(me + k, n), me).wait_send()
        return carry

    lax.fori_loop(1, n, finish, 0)


def row_all_gather(source):
    n = lax.axis_size("row")
    nodes_dev, feat_width = source.shape
    vmem = pl.BlockSpec(memory_space=pltpu.VMEM)
    return pl.pallas_call(
        functools.partial(all_gather_kernel, n),
        out_shape=jax.ShapeDtypeStruct((n, nodes_dev, feat_width), source.dtype),
        in_specs=[vmem],
        out_specs=vmem,
        scratch_shapes=[pltpu.SemaphoreType.DMA((n,)), pltpu.SemaphoreType.DMA((n,))],
        compiler_params=pltpu.CompilerParams(collective_id=1, has_side_effects=True),
    )(source)


def block_product_kernel(group, rows_ref, cols_ref, count_ref, adj_ref, panel_ref,
                         pieces_ref):
    pieces_ref[...] = jnp.zeros_like(pieces_ref)
    count = count_ref[0]
    slots = adj_ref.shape[0]

    def body(g, carry):
        base = g * group
        prods = []
        for i in range(group):
            t = base + i
            p = jnp.dot(adj_ref[t], panel_ref[cols_ref[t]], preferred_element_type=jnp.float32)
            prods.append(jnp.where(t < count, p, jnp.zeros_like(p)))
        for i in range(group):
            slot = rows_ref[base + i]
            pieces_ref[slot] += prods[i]
        return carry

    lax.fori_loop(0, slots // group, body, 0)


def block_product(row_ids, col_ids, count, dev_tiles, col_panel, row_tiles, nodes_dev):
    slots = dev_tiles.shape[0]
    feat_width = col_panel.shape[2]
    group = 16 if slots % 16 == 0 else 1
    smem = pl.BlockSpec(memory_space=pltpu.SMEM)
    vmem = pl.BlockSpec(memory_space=pltpu.VMEM)
    return pl.pallas_call(
        functools.partial(block_product_kernel, group),
        out_shape=jax.ShapeDtypeStruct((row_tiles, TILE, feat_width), jnp.float32),
        in_specs=[smem, smem, smem, vmem, vmem],
        out_specs=vmem,
        cost_estimate=pl.CostEstimate(
            flops=2 * slots * TILE * TILE * feat_width,
            bytes_accessed=slots * TILE * TILE * 2 + row_tiles * TILE * feat_width * 4,
            transcendentals=0,
        ),
    )(row_ids, col_ids, count, dev_tiles, col_panel)


def shards(features, degrees, adj_tiles, tile_rows, tile_cols, tile_counts):
    col_count = lax.axis_size("col")
    nodes_dev = features.shape[0]
    feat_width = features.shape[1]
    tile_slots = adj_tiles.shape[2]
    dev_tiles = adj_tiles.reshape(tile_slots, TILE, TILE)
    row_ids_all = tile_rows.reshape(tile_slots)
    col_ids_all = tile_cols.reshape(tile_slots)
    live_count = tile_counts.reshape(1)
    row_tiles = nodes_dev * col_count // TILE
    norm_scale = jnp.sqrt(KNN / degrees.astype(jnp.float32))[:, None]
    teleport = ALPHA * features.astype(jnp.float32)
    scale9 = jnp.broadcast_to((1.0 - ALPHA) * norm_scale, features.shape)
    scale = jnp.broadcast_to(norm_scale, features.shape)
    source = (norm_scale * features.astype(jnp.float32)).astype(jnp.bfloat16)
    gathered = row_all_gather(source)
    per_piece = nodes_dev // TILE
    n_y = col_count // (CORES * Z_RING)
    piece_j = row_ids_all // per_piece
    row_slots = (((piece_j % CORES) * Z_RING + (piece_j // CORES) % Z_RING) * n_y
                 + piece_j // (CORES * Z_RING)) * per_piece + row_ids_all % per_piece
    for repeat in range(STEPS):
        col_panel = gathered.reshape(-1, TILE, feat_width)
        pieces = block_product(
            row_slots, col_ids_all, live_count, dev_tiles, col_panel, row_tiles, nodes_dev
        )
        gathered = col_reduce_scatter(
            pieces.reshape(CORES, Z_RING, -1, nodes_dev, feat_width),
            scale9, scale, teleport, repeat == STEPS - 1,
        )
    return gathered


def solution(mesh):
    return jax.shard_map(
        shards,
        mesh=mesh,
        in_specs=(
            P(("row", "col"), None),
            P(("row", "col")),
            P("row", "col", None, None),
            P("row", "col", None),
            P("row", "col", None),
            P("row", "col"),
        ),
        out_specs=P(("row", "col"), None),
        check_vma=False,
    )
```

```python
import functools

import jax
import jax.numpy as jnp
from jax import lax
from jax.experimental import pallas as pl
from jax.experimental.pallas import tpu as pltpu
from jax.sharding import PartitionSpec as P

TILE = 64
KNN = 32
STEPS = 2

MESH = pl.DeviceIdType.MESH

ALPHA = 0.1


CORES = 2
Z_RING = 8


def reduce_scatter_kernel(n_z, chunks, last, x_ref, s9_ref, scale_ref, tele_ref, out_ref, ra,
                          recv_cw, recv_ccw, send_cw, send_ccw, fin, y_recv,
                          a_sems, cw_sems, ccw_sems, y_sems, *ag_sems):
    c = lax.axis_index("col")
    row = lax.axis_index("row")
    core = lax.rem(c, CORES)
    z = lax.rem(c // CORES, n_z)
    yh = c // (CORES * n_z)

    def dev(yh_, z_, core_):
        return (row, (yh_ * n_z + z_) * CORES + core_)

    partner = dev(yh, z, 1 - core)
    right = dev(yh, lax.rem(z + 1, n_z), core)
    left = dev(yh, lax.rem(z + n_z - 1, n_z), core)
    y_partner = dev(1 - yh, z, core)

    n_row = lax.axis_size("row")
    barrier = pltpu.get_barrier_semaphore()
    for peer in (partner, right, left, y_partner):
        pl.semaphore_signal(barrier, inc=1, device_id=peer, device_id_type=MESH)
    if not last:
        def greet(k, carry):
            pl.semaphore_signal(barrier, inc=1, device_id=(lax.rem(row + k, n_row), c),
                                device_id_type=MESH)
            return carry

        lax.fori_loop(1, n_row, greet, 0)
    pl.semaphore_wait(barrier, 4 if last else 3 + n_row)

    def rcopy(src, dst, sems, idx, peer):
        return pltpu.make_async_remote_copy(
            src_ref=src, dst_ref=dst, send_sem=sems.at[(0,) + idx], recv_sem=sems.at[(1,) + idx],
            device_id=peer, device_id_type=MESH,
        )

    def first(d):
        return lax.rem(z + (n_z - 1 if d == 0 else 1), n_z)

    def got(d, s):
        return lax.rem(z + ((2 * n_z - s - 2) if d == 0 else (s + 2)), n_z)

    need = [(first(0), 0), (first(1), 1)]
    for s in range(n_z - 1):
        need += [(got(0, s), 0), (got(1, s), 1)]
    copies_a = []
    for k, (g, h) in enumerate(need):
        cp = rcopy(x_ref.at[1 - core, g, h], ra.at[g, h], a_sems, (k,), partner)
        cp.start()
        copies_a.append(cp)

    def ready(d, s):
        copies_a[d if s < 0 else 2 + 2 * s + d].wait_recv()

    size = x_ref.shape[3] // chunks
    recv = (recv_cw, recv_ccw)
    send = (send_cw, send_ccw)
    sems = (cw_sems, ccw_sems)
    to = (right, left)
    sends = list(copies_a)

    def ring_copy(d, s, i):
        part = pl.ds(i * size, size)
        return rcopy(send[d].at[s, part], recv[d].at[s, part], sems[d], (s, i), to[d])

    def y_copy(i):
        part = pl.ds(i * size, size)
        return rcopy(fin.at[1 - yh, part], y_recv.at[part], y_sems, (i,), y_partner)

    for d in range(2):
        ready(d, -1)
        g = first(d)
        send[d][0] = x_ref[core, g, d] + ra[g, d]
        for i in range(chunks):
            cp = ring_copy(d, 0, i)
            cp.start()
            sends.append(cp)
    for s in range(n_z - 1):
        for d in range(2):
            ready(d, s)
        for i in range(chunks):
            part = pl.ds(i * size, size)
            for d in range(2):
                g = got(d, s)
                ring_copy(d, s, i).wait_recv()
                val = recv[d][s, part] + x_ref[core, g, d, part] + ra[g, d, part]
                if s < n_z - 2:
                    send[d][s + 1, part] = val
                    cp = ring_copy(d, s + 1, i)
                    cp.start()
                    sends.append(cp)
                else:
                    fin[d, part] = val
            if s == n_z - 2:
                cp = y_copy(i)
                cp.start()
                sends.append(cp)

    for i in range(chunks):
        part = pl.ds(i * size, size)
        y_copy(i).wait_recv()
        own = fin[yh, part] + y_recv[part]
        current = s9_ref[part] * own + tele_ref[part]
        if last:
            out_ref[part] = current.astype(out_ref.dtype)
        else:
            out_ref[row, part] = (scale_ref[part] * current).astype(out_ref.dtype)
    if not last:
        ag_send, ag_recv = ag_sems

        def ag_copy(peer, slot):
            return pltpu.make_async_remote_copy(
                src_ref=out_ref.at[row], dst_ref=out_ref.at[slot], send_sem=ag_send.at[peer],
                recv_sem=ag_recv.at[slot], device_id=(peer, c), device_id_type=MESH,
            )

        def ag_start(k, carry):
            ag_copy(lax.rem(row + k, n_row), row).start()
            return carry

        lax.fori_loop(1, n_row, ag_start, 0)

        def ag_finish(k, carry):
            sender = lax.rem(row + n_row - k, n_row)
            ag_copy(sender, sender).wait_recv()
            ag_copy(lax.rem(row + k, n_row), row).wait_send()
            return carry

        lax.fori_loop(1, n_row, ag_finish, 0)
    for cp in sends:
        cp.wait_send()


RS_CHUNKS = 4


def col_reduce_scatter(pieces, s9, scale, tele, last):
    cores, n_z, n_y, nodes_dev, feat_width = pieces.shape
    n_row = lax.axis_size("row")
    chunks = RS_CHUNKS
    piece = (nodes_dev, feat_width)
    vmem = pl.BlockSpec(memory_space=pltpu.VMEM)
    out_shape = piece if last else (n_row,) + piece
    ag_sems = [] if last else [pltpu.SemaphoreType.DMA((n_row,))] * 2
    return pl.pallas_call(
        functools.partial(reduce_scatter_kernel, n_z, chunks, last),
        out_shape=jax.ShapeDtypeStruct(out_shape, jnp.bfloat16),
        in_specs=[vmem] * 4,
        out_specs=vmem,
        scratch_shapes=[
            pltpu.VMEM((n_z, n_y) + piece, jnp.float32),
            pltpu.VMEM((n_z - 1,) + piece, jnp.float32),
            pltpu.VMEM((n_z - 1,) + piece, jnp.float32),
            pltpu.VMEM((n_z - 1,) + piece, jnp.float32),
            pltpu.VMEM((n_z - 1,) + piece, jnp.float32),
            pltpu.VMEM((n_y,) + piece, jnp.float32),
            pltpu.VMEM(piece, jnp.float32),
            pltpu.SemaphoreType.DMA((2, 2 * n_z)),
            pltpu.SemaphoreType.DMA((2, n_z - 1, chunks)),
            pltpu.SemaphoreType.DMA((2, n_z - 1, chunks)),
            pltpu.SemaphoreType.DMA((2, chunks)),
        ] + ag_sems,
        compiler_params=pltpu.CompilerParams(collective_id=2 if last else 0, has_side_effects=True),
    )(pieces, s9, scale, tele)


def all_gather_kernel(n, src_ref, out_ref, send_sem, recv_sem):
    me = lax.axis_index("row")
    col = lax.axis_index("col")

    barrier = pltpu.get_barrier_semaphore()

    def greet(k, carry):
        peer = lax.rem(me + k, n)
        pl.semaphore_signal(barrier, inc=1, device_id=(peer, col), device_id_type=MESH)
        return carry

    lax.fori_loop(1, n, greet, 0)
    pl.semaphore_wait(barrier, n - 1)

    def copy(peer, slot):
        return pltpu.make_async_remote_copy(
            src_ref=src_ref,
            dst_ref=out_ref.at[slot],
            send_sem=send_sem.at[peer],
            recv_sem=recv_sem.at[slot],
            device_id=(peer, col),
            device_id_type=MESH,
        )

    def start(k, carry):
        copy(lax.rem(me + k, n), me).start()
        return carry

    lax.fori_loop(1, n, start, 0)
    out_ref[me] = src_ref[...]

    def finish(k, carry):
        sender = lax.rem(me + n - k, n)
        copy(sender, sender).wait_recv()
        copy(lax.rem(me + k, n), me).wait_send()
        return carry

    lax.fori_loop(1, n, finish, 0)


def row_all_gather(source):
    n = lax.axis_size("row")
    nodes_dev, feat_width = source.shape
    vmem = pl.BlockSpec(memory_space=pltpu.VMEM)
    return pl.pallas_call(
        functools.partial(all_gather_kernel, n),
        out_shape=jax.ShapeDtypeStruct((n, nodes_dev, feat_width), source.dtype),
        in_specs=[vmem],
        out_specs=vmem,
        scratch_shapes=[pltpu.SemaphoreType.DMA((n,)), pltpu.SemaphoreType.DMA((n,))],
        compiler_params=pltpu.CompilerParams(collective_id=1, has_side_effects=True),
    )(source)


def block_product_kernel(group, rows_ref, cols_ref, count_ref, adj_ref, panel_ref,
                         pieces_ref):
    pieces_ref[...] = jnp.zeros_like(pieces_ref)
    slots = adj_ref.shape[0]

    def body(g, carry):
        base = g * group
        prods = []
        for i in range(group):
            t = base + i
            prods.append(
                jnp.dot(adj_ref[t], panel_ref[cols_ref[t]], preferred_element_type=jnp.float32))
        for i in range(group):
            slot = rows_ref[base + i]
            pieces_ref[slot] += prods[i]
        return carry

    lax.fori_loop(0, slots // group, body, 0)


def block_product(row_ids, col_ids, count, dev_tiles, col_panel, row_tiles, nodes_dev):
    slots = dev_tiles.shape[0]
    feat_width = col_panel.shape[2]
    group = 16 if slots % 16 == 0 else 1
    smem = pl.BlockSpec(memory_space=pltpu.SMEM)
    vmem = pl.BlockSpec(memory_space=pltpu.VMEM)
    return pl.pallas_call(
        functools.partial(block_product_kernel, group),
        out_shape=jax.ShapeDtypeStruct((row_tiles, TILE, feat_width), jnp.float32),
        in_specs=[smem, smem, smem, vmem, vmem],
        out_specs=vmem,
        cost_estimate=pl.CostEstimate(
            flops=2 * slots * TILE * TILE * feat_width,
            bytes_accessed=slots * TILE * TILE * 2 + row_tiles * TILE * feat_width * 4,
            transcendentals=0,
        ),
    )(row_ids, col_ids, count, dev_tiles, col_panel)


def shards(features, degrees, adj_tiles, tile_rows, tile_cols, tile_counts):
    col_count = lax.axis_size("col")
    nodes_dev = features.shape[0]
    feat_width = features.shape[1]
    tile_slots = adj_tiles.shape[2]
    live = jnp.arange(tile_slots, dtype=jnp.int32) < tile_counts.reshape(())
    dev_tiles = jnp.where(live[:, None, None], adj_tiles.reshape(tile_slots, TILE, TILE),
                          jnp.zeros((), adj_tiles.dtype))
    row_ids_all = tile_rows.reshape(tile_slots)
    col_ids_all = tile_cols.reshape(tile_slots)
    live_count = tile_counts.reshape(1)
    row_tiles = nodes_dev * col_count // TILE
    norm_scale = jnp.sqrt(KNN / degrees.astype(jnp.float32))[:, None]
    teleport = ALPHA * features.astype(jnp.float32)
    scale9 = jnp.broadcast_to((1.0 - ALPHA) * norm_scale, features.shape)
    scale = jnp.broadcast_to(norm_scale, features.shape)
    source = (norm_scale * features.astype(jnp.float32)).astype(jnp.bfloat16)
    gathered = row_all_gather(source)
    per_piece = nodes_dev // TILE
    n_y = col_count // (CORES * Z_RING)
    piece_j = row_ids_all // per_piece
    row_slots = (((piece_j % CORES) * Z_RING + (piece_j // CORES) % Z_RING) * n_y
                 + piece_j // (CORES * Z_RING)) * per_piece + row_ids_all % per_piece
    for repeat in range(STEPS):
        col_panel = gathered.reshape(-1, TILE, feat_width)
        pieces = block_product(
            row_slots, col_ids_all, live_count, dev_tiles, col_panel, row_tiles, nodes_dev
        )
        gathered = col_reduce_scatter(
            pieces.reshape(CORES, Z_RING, -1, nodes_dev, feat_width),
            scale9, scale, teleport, repeat == STEPS - 1,
        )
    return gathered


def solution(mesh):
    return jax.shard_map(
        shards,
        mesh=mesh,
        in_specs=(
            P(("row", "col"), None),
            P(("row", "col")),
            P("row", "col", None, None),
            P("row", "col", None),
            P("row", "col", None),
            P("row", "col"),
        ),
        out_specs=P(("row", "col"), None),
        check_vma=False,
    )
```

```python
import functools

import jax
import jax.numpy as jnp
from jax import lax
from jax.experimental import pallas as pl
from jax.experimental.pallas import tpu as pltpu
from jax.sharding import PartitionSpec as P

TILE = 64
KNN = 32
STEPS = 2

MESH = pl.DeviceIdType.MESH

ALPHA = 0.1


CORES = 2
Z_RING = 8


def reduce_scatter_kernel(n_z, chunks, last, x_ref, s9_ref, scale_ref, tele_ref, out_ref, ra,
                          recv_cw, recv_ccw, send_cw, send_ccw, fin, y_recv,
                          a_sems, cw_sems, ccw_sems, y_sems, *ag_sems):
    c = lax.axis_index("col")
    row = lax.axis_index("row")
    core = lax.rem(c, CORES)
    z = lax.rem(c // CORES, n_z)
    yh = c // (CORES * n_z)

    def dev(yh_, z_, core_):
        return (row, (yh_ * n_z + z_) * CORES + core_)

    partner = dev(yh, z, 1 - core)
    right = dev(yh, lax.rem(z + 1, n_z), core)
    left = dev(yh, lax.rem(z + n_z - 1, n_z), core)
    y_partner = dev(1 - yh, z, core)

    n_row = lax.axis_size("row")
    barrier = pltpu.get_barrier_semaphore()
    for peer in (partner, right, left, y_partner):
        pl.semaphore_signal(barrier, inc=1, device_id=peer, device_id_type=MESH)
    if not last:
        def greet(k, carry):
            pl.semaphore_signal(barrier, inc=1, device_id=(lax.rem(row + k, n_row), c),
                                device_id_type=MESH)
            return carry

        lax.fori_loop(1, n_row, greet, 0)
    pl.semaphore_wait(barrier, 4 if last else 3 + n_row)

    def rcopy(src, dst, sems, idx, peer):
        return pltpu.make_async_remote_copy(
            src_ref=src, dst_ref=dst, send_sem=sems.at[(0,) + idx], recv_sem=sems.at[(1,) + idx],
            device_id=peer, device_id_type=MESH,
        )

    def first(d):
        return lax.rem(z + (n_z - 1 if d == 0 else 1), n_z)

    def got(d, s):
        return lax.rem(z + ((2 * n_z - s - 2) if d == 0 else (s + 2)), n_z)

    need = [(first(0), 0), (first(1), 1)]
    for s in range(n_z - 1):
        need += [(got(0, s), 0), (got(1, s), 1)]
    copies_a = []
    for k, (g, h) in enumerate(need):
        cp = rcopy(x_ref.at[1 - core, g, h], ra.at[g, h], a_sems, (k,), partner)
        cp.start()
        copies_a.append(cp)

    def ready(d, s):
        copies_a[d if s < 0 else 2 + 2 * s + d].wait_recv()

    size = x_ref.shape[3] // chunks
    recv = (recv_cw, recv_ccw)
    send = (send_cw, send_ccw)
    sems = (cw_sems, ccw_sems)
    to = (right, left)
    sends = list(copies_a)

    def ring_copy(d, s, i):
        part = pl.ds(i * size, size)
        return rcopy(send[d].at[s, part], recv[d].at[s, part], sems[d], (s, i), to[d])

    def y_copy(i):
        part = pl.ds(i * size, size)
        return rcopy(fin.at[1 - yh, part], y_recv.at[part], y_sems, (i,), y_partner)

    for d in range(2):
        ready(d, -1)
        g = first(d)
        send[d][0] = x_ref[core, g, d] + ra[g, d]
        for i in range(chunks):
            cp = ring_copy(d, 0, i)
            cp.start()
            sends.append(cp)
    for s in range(n_z - 1):
        for d in range(2):
            ready(d, s)
        for i in range(chunks):
            part = pl.ds(i * size, size)
            for d in range(2):
                g = got(d, s)
                ring_copy(d, s, i).wait_recv()
                val = recv[d][s, part] + x_ref[core, g, d, part] + ra[g, d, part]
                if s < n_z - 2:
                    send[d][s + 1, part] = val
                    cp = ring_copy(d, s + 1, i)
                    cp.start()
                    sends.append(cp)
                else:
                    fin[d, part] = val
            if s == n_z - 2:
                cp = y_copy(i)
                cp.start()
                sends.append(cp)

    if not last:
        ag_send, ag_recv = ag_sems

        def ag_copy(peer, slot, i):
            part = pl.ds(i * size, size)
            return pltpu.make_async_remote_copy(
                src_ref=out_ref.at[row, part], dst_ref=out_ref.at[slot, part],
                send_sem=ag_send.at[peer, i], recv_sem=ag_recv.at[slot, i],
                device_id=(peer, c), device_id_type=MESH,
            )

    for i in range(chunks):
        part = pl.ds(i * size, size)
        y_copy(i).wait_recv()
        own = fin[yh, part] + y_recv[part]
        current = s9_ref[part] * own + tele_ref[part]
        if last:
            out_ref[part] = current.astype(out_ref.dtype)
        else:
            out_ref[row, part] = (scale_ref[part] * current).astype(out_ref.dtype)

            def ag_start(k, carry, i=i):
                ag_copy(lax.rem(row + k, n_row), row, i).start()
                return carry

            lax.fori_loop(1, n_row, ag_start, 0)
    if not last:
        def ag_finish(k, carry):
            for i in range(chunks):
                ag_copy(lax.rem(row + n_row - k, n_row), lax.rem(row + n_row - k, n_row), i).wait_recv()
                ag_copy(lax.rem(row + k, n_row), row, i).wait_send()
            return carry

        lax.fori_loop(1, n_row, ag_finish, 0)
    for cp in sends:
        cp.wait_send()


RS_CHUNKS = 4


def col_reduce_scatter(pieces, s9, scale, tele, last):
    cores, n_z, n_y, nodes_dev, feat_width = pieces.shape
    n_row = lax.axis_size("row")
    chunks = RS_CHUNKS
    piece = (nodes_dev, feat_width)
    vmem = pl.BlockSpec(memory_space=pltpu.VMEM)
    out_shape = piece if last else (n_row,) + piece
    ag_sems = [] if last else [pltpu.SemaphoreType.DMA((n_row, chunks))] * 2
    return pl.pallas_call(
        functools.partial(reduce_scatter_kernel, n_z, chunks, last),
        out_shape=jax.ShapeDtypeStruct(out_shape, jnp.bfloat16),
        in_specs=[vmem] * 4,
        out_specs=vmem,
        scratch_shapes=[
            pltpu.VMEM((n_z, n_y) + piece, jnp.float32),
            pltpu.VMEM((n_z - 1,) + piece, jnp.float32),
            pltpu.VMEM((n_z - 1,) + piece, jnp.float32),
            pltpu.VMEM((n_z - 1,) + piece, jnp.float32),
            pltpu.VMEM((n_z - 1,) + piece, jnp.float32),
            pltpu.VMEM((n_y,) + piece, jnp.float32),
            pltpu.VMEM(piece, jnp.float32),
            pltpu.SemaphoreType.DMA((2, 2 * n_z)),
            pltpu.SemaphoreType.DMA((2, n_z - 1, chunks)),
            pltpu.SemaphoreType.DMA((2, n_z - 1, chunks)),
            pltpu.SemaphoreType.DMA((2, chunks)),
        ] + ag_sems,
        compiler_params=pltpu.CompilerParams(collective_id=2 if last else 0, has_side_effects=True),
    )(pieces, s9, scale, tele)


def all_gather_kernel(n, src_ref, out_ref, send_sem, recv_sem):
    me = lax.axis_index("row")
    col = lax.axis_index("col")

    barrier = pltpu.get_barrier_semaphore()

    def greet(k, carry):
        peer = lax.rem(me + k, n)
        pl.semaphore_signal(barrier, inc=1, device_id=(peer, col), device_id_type=MESH)
        return carry

    lax.fori_loop(1, n, greet, 0)
    pl.semaphore_wait(barrier, n - 1)

    def copy(peer, slot):
        return pltpu.make_async_remote_copy(
            src_ref=src_ref,
            dst_ref=out_ref.at[slot],
            send_sem=send_sem.at[peer],
            recv_sem=recv_sem.at[slot],
            device_id=(peer, col),
            device_id_type=MESH,
        )

    def start(k, carry):
        copy(lax.rem(me + k, n), me).start()
        return carry

    lax.fori_loop(1, n, start, 0)
    out_ref[me] = src_ref[...]

    def finish(k, carry):
        sender = lax.rem(me + n - k, n)
        copy(sender, sender).wait_recv()
        copy(lax.rem(me + k, n), me).wait_send()
        return carry

    lax.fori_loop(1, n, finish, 0)


def row_all_gather(source):
    n = lax.axis_size("row")
    nodes_dev, feat_width = source.shape
    vmem = pl.BlockSpec(memory_space=pltpu.VMEM)
    return pl.pallas_call(
        functools.partial(all_gather_kernel, n),
        out_shape=jax.ShapeDtypeStruct((n, nodes_dev, feat_width), source.dtype),
        in_specs=[vmem],
        out_specs=vmem,
        scratch_shapes=[pltpu.SemaphoreType.DMA((n,)), pltpu.SemaphoreType.DMA((n,))],
        compiler_params=pltpu.CompilerParams(collective_id=1, has_side_effects=True),
    )(source)


def block_product_kernel(group, rows_ref, cols_ref, count_ref, adj_ref, panel_ref,
                         pieces_ref):
    pieces_ref[...] = jnp.zeros_like(pieces_ref)
    count = count_ref[0]
    slots = adj_ref.shape[0]

    def body(g, carry):
        base = g * group
        prods = []
        for i in range(group):
            t = base + i
            p = jnp.dot(adj_ref[t], panel_ref[cols_ref[t]], preferred_element_type=jnp.float32)
            prods.append(jnp.where(t < count, p, jnp.zeros_like(p)))
        for i in range(group):
            slot = rows_ref[base + i]
            pieces_ref[slot] += prods[i]
        return carry

    lax.fori_loop(0, slots // group, body, 0)


def block_product(row_ids, col_ids, count, dev_tiles, col_panel, row_tiles, nodes_dev):
    slots = dev_tiles.shape[0]
    feat_width = col_panel.shape[2]
    group = 16 if slots % 16 == 0 else 1
    smem = pl.BlockSpec(memory_space=pltpu.SMEM)
    vmem = pl.BlockSpec(memory_space=pltpu.VMEM)
    return pl.pallas_call(
        functools.partial(block_product_kernel, group),
        out_shape=jax.ShapeDtypeStruct((row_tiles, TILE, feat_width), jnp.float32),
        in_specs=[smem, smem, smem, vmem, vmem],
        out_specs=vmem,
        cost_estimate=pl.CostEstimate(
            flops=2 * slots * TILE * TILE * feat_width,
            bytes_accessed=slots * TILE * TILE * 2 + row_tiles * TILE * feat_width * 4,
            transcendentals=0,
        ),
    )(row_ids, col_ids, count, dev_tiles, col_panel)


def shards(features, degrees, adj_tiles, tile_rows, tile_cols, tile_counts):
    col_count = lax.axis_size("col")
    nodes_dev = features.shape[0]
    feat_width = features.shape[1]
    tile_slots = adj_tiles.shape[2]
    dev_tiles = adj_tiles.reshape(tile_slots, TILE, TILE)
    row_ids_all = tile_rows.reshape(tile_slots)
    col_ids_all = tile_cols.reshape(tile_slots)
    live_count = tile_counts.reshape(1)
    row_tiles = nodes_dev * col_count // TILE
    norm_scale = jnp.sqrt(KNN / degrees.astype(jnp.float32))[:, None]
    teleport = ALPHA * features.astype(jnp.float32)
    scale9 = jnp.broadcast_to((1.0 - ALPHA) * norm_scale, features.shape)
    scale = jnp.broadcast_to(norm_scale, features.shape)
    source = (norm_scale * features.astype(jnp.float32)).astype(jnp.bfloat16)
    gathered = row_all_gather(source)
    per_piece = nodes_dev // TILE
    n_y = col_count // (CORES * Z_RING)
    piece_j = row_ids_all // per_piece
    row_slots = (((piece_j % CORES) * Z_RING + (piece_j // CORES) % Z_RING) * n_y
                 + piece_j // (CORES * Z_RING)) * per_piece + row_ids_all % per_piece
    for repeat in range(STEPS):
        col_panel = gathered.reshape(-1, TILE, feat_width)
        pieces = block_product(
            row_slots, col_ids_all, live_count, dev_tiles, col_panel, row_tiles, nodes_dev
        )
        gathered = col_reduce_scatter(
            pieces.reshape(CORES, Z_RING, -1, nodes_dev, feat_width),
            scale9, scale, teleport, repeat == STEPS - 1,
        )
    return gathered


def solution(mesh):
    return jax.shard_map(
        shards,
        mesh=mesh,
        in_specs=(
            P(("row", "col"), None),
            P(("row", "col")),
            P("row", "col", None, None),
            P("row", "col", None),
            P("row", "col", None),
            P("row", "col"),
        ),
        out_specs=P(("row", "col"), None),
        check_vma=False,
    )
```

```python
import functools

import jax
import jax.numpy as jnp
from jax import lax
from jax.experimental import pallas as pl
from jax.experimental.pallas import tpu as pltpu
from jax.sharding import PartitionSpec as P

TILE = 64
KNN = 32
STEPS = 2

MESH = pl.DeviceIdType.MESH

ALPHA = 0.1


CORES = 2
Z_RING = 8


def reduce_scatter_kernel(n_z, chunks, last, x_ref, s9_ref, scale_ref, tele_ref, out_ref, ra,
                          recv_cw, recv_ccw, send_cw, send_ccw, fin, y_recv,
                          a_sems, cw_sems, ccw_sems, y_sems, *ag_sems):
    c = lax.axis_index("col")
    row = lax.axis_index("row")
    core = lax.rem(c, CORES)
    z = lax.rem(c // CORES, n_z)
    yh = c // (CORES * n_z)

    def dev(yh_, z_, core_):
        return (row, (yh_ * n_z + z_) * CORES + core_)

    partner = dev(yh, z, 1 - core)
    right = dev(yh, lax.rem(z + 1, n_z), core)
    left = dev(yh, lax.rem(z + n_z - 1, n_z), core)
    y_partner = dev(1 - yh, z, core)

    n_row = lax.axis_size("row")
    barrier = pltpu.get_barrier_semaphore()
    for peer in (partner, right, left, y_partner):
        pl.semaphore_signal(barrier, inc=1, device_id=peer, device_id_type=MESH)
    if not last:
        def greet(k, carry):
            pl.semaphore_signal(barrier, inc=1, device_id=(lax.rem(row + k, n_row), c),
                                device_id_type=MESH)
            return carry

        lax.fori_loop(1, n_row, greet, 0)
    pl.semaphore_wait(barrier, 4 if last else 3 + n_row)

    def rcopy(src, dst, sems, idx, peer):
        return pltpu.make_async_remote_copy(
            src_ref=src, dst_ref=dst, send_sem=sems.at[(0,) + idx], recv_sem=sems.at[(1,) + idx],
            device_id=peer, device_id_type=MESH,
        )

    def first(d):
        return lax.rem(z + (n_z - 1 if d == 0 else 1), n_z)

    def got(d, s):
        return lax.rem(z + ((2 * n_z - s - 2) if d == 0 else (s + 2)), n_z)

    need = [(first(0), 0), (first(1), 1)]
    for s in range(n_z - 1):
        need += [(got(0, s), 0), (got(1, s), 1)]
    copies_a = []
    for k, (g, h) in enumerate(need):
        cp = rcopy(x_ref.at[1 - core, g, h], ra.at[g, h], a_sems, (k,), partner)
        cp.start()
        copies_a.append(cp)

    def ready(d, s):
        copies_a[d if s < 0 else 2 + 2 * s + d].wait_recv()

    size = x_ref.shape[3] // chunks
    recv = (recv_cw, recv_ccw)
    send = (send_cw, send_ccw)
    sems = (cw_sems, ccw_sems)
    to = (right, left)
    sends = list(copies_a)

    def ring_copy(d, s, i):
        part = pl.ds(i * size, size)
        return rcopy(send[d].at[s, part], recv[d].at[s, part], sems[d], (s, i), to[d])

    def y_copy(i):
        part = pl.ds(i * size, size)
        return rcopy(fin.at[1 - yh, part], y_recv.at[part], y_sems, (i,), y_partner)

    for d in range(2):
        ready(d, -1)
        g = first(d)
        send[d][0] = x_ref[core, g, d] + ra[g, d]
        for i in range(chunks):
            cp = ring_copy(d, 0, i)
            cp.start()
            sends.append(cp)
    for s in range(n_z - 1):
        for d in range(2):
            ready(d, s)
        for i in range(chunks):
            part = pl.ds(i * size, size)
            for d in range(2):
                g = got(d, s)
                ring_copy(d, s, i).wait_recv()
                val = recv[d][s, part] + x_ref[core, g, d, part] + ra[g, d, part]
                if s < n_z - 2:
                    send[d][s + 1, part] = val
                    cp = ring_copy(d, s + 1, i)
                    cp.start()
                    sends.append(cp)
                else:
                    fin[d, part] = val
            if s == n_z - 2:
                cp = y_copy(i)
                cp.start()
                sends.append(cp)

    if not last:
        ag_send, ag_recv = ag_sems

        def ag_copy(peer, slot, i):
            part = pl.ds(i * size, size)
            return pltpu.make_async_remote_copy(
                src_ref=out_ref.at[row, part], dst_ref=out_ref.at[slot, part],
                send_sem=ag_send.at[peer, i], recv_sem=ag_recv.at[slot, i],
                device_id=(peer, c), device_id_type=MESH,
            )

    for i in range(chunks):
        part = pl.ds(i * size, size)
        y_copy(i).wait_recv()
        own = fin[yh, part] + y_recv[part]
        current = s9_ref[part] * own + tele_ref[part]
        if last:
            out_ref[part] = current.astype(out_ref.dtype)
        else:
            out_ref[row, part] = (scale_ref[part] * current).astype(out_ref.dtype)

            def ag_start(k, carry, i=i):
                ag_copy(lax.rem(row + k, n_row), row, i).start()
                return carry

            lax.fori_loop(1, n_row, ag_start, 0)
    if not last:
        def ag_finish(k, carry):
            for i in range(chunks):
                ag_copy(lax.rem(row + n_row - k, n_row), lax.rem(row + n_row - k, n_row), i).wait_recv()
                ag_copy(lax.rem(row + k, n_row), row, i).wait_send()
            return carry

        lax.fori_loop(1, n_row, ag_finish, 0)
    for cp in sends:
        cp.wait_send()


RS_CHUNKS = 8


def col_reduce_scatter(pieces, s9, scale, tele, last):
    cores, n_z, n_y, nodes_dev, feat_width = pieces.shape
    n_row = lax.axis_size("row")
    chunks = RS_CHUNKS
    piece = (nodes_dev, feat_width)
    vmem = pl.BlockSpec(memory_space=pltpu.VMEM)
    out_shape = piece if last else (n_row,) + piece
    ag_sems = [] if last else [pltpu.SemaphoreType.DMA((n_row, chunks))] * 2
    return pl.pallas_call(
        functools.partial(reduce_scatter_kernel, n_z, chunks, last),
        out_shape=jax.ShapeDtypeStruct(out_shape, jnp.bfloat16),
        in_specs=[vmem] * 4,
        out_specs=vmem,
        scratch_shapes=[
            pltpu.VMEM((n_z, n_y) + piece, jnp.float32),
            pltpu.VMEM((n_z - 1,) + piece, jnp.float32),
            pltpu.VMEM((n_z - 1,) + piece, jnp.float32),
            pltpu.VMEM((n_z - 1,) + piece, jnp.float32),
            pltpu.VMEM((n_z - 1,) + piece, jnp.float32),
            pltpu.VMEM((n_y,) + piece, jnp.float32),
            pltpu.VMEM(piece, jnp.float32),
            pltpu.SemaphoreType.DMA((2, 2 * n_z)),
            pltpu.SemaphoreType.DMA((2, n_z - 1, chunks)),
            pltpu.SemaphoreType.DMA((2, n_z - 1, chunks)),
            pltpu.SemaphoreType.DMA((2, chunks)),
        ] + ag_sems,
        compiler_params=pltpu.CompilerParams(collective_id=2 if last else 0, has_side_effects=True),
    )(pieces, s9, scale, tele)


def all_gather_kernel(n, src_ref, out_ref, send_sem, recv_sem):
    me = lax.axis_index("row")
    col = lax.axis_index("col")

    barrier = pltpu.get_barrier_semaphore()

    def greet(k, carry):
        peer = lax.rem(me + k, n)
        pl.semaphore_signal(barrier, inc=1, device_id=(peer, col), device_id_type=MESH)
        return carry

    lax.fori_loop(1, n, greet, 0)
    pl.semaphore_wait(barrier, n - 1)

    def copy(peer, slot):
        return pltpu.make_async_remote_copy(
            src_ref=src_ref,
            dst_ref=out_ref.at[slot],
            send_sem=send_sem.at[peer],
            recv_sem=recv_sem.at[slot],
            device_id=(peer, col),
            device_id_type=MESH,
        )

    def start(k, carry):
        copy(lax.rem(me + k, n), me).start()
        return carry

    lax.fori_loop(1, n, start, 0)
    out_ref[me] = src_ref[...]

    def finish(k, carry):
        sender = lax.rem(me + n - k, n)
        copy(sender, sender).wait_recv()
        copy(lax.rem(me + k, n), me).wait_send()
        return carry

    lax.fori_loop(1, n, finish, 0)


def row_all_gather(source):
    n = lax.axis_size("row")
    nodes_dev, feat_width = source.shape
    vmem = pl.BlockSpec(memory_space=pltpu.VMEM)
    return pl.pallas_call(
        functools.partial(all_gather_kernel, n),
        out_shape=jax.ShapeDtypeStruct((n, nodes_dev, feat_width), source.dtype),
        in_specs=[vmem],
        out_specs=vmem,
        scratch_shapes=[pltpu.SemaphoreType.DMA((n,)), pltpu.SemaphoreType.DMA((n,))],
        compiler_params=pltpu.CompilerParams(collective_id=1, has_side_effects=True),
    )(source)


def block_product_kernel(group, rows_ref, cols_ref, count_ref, adj_ref, panel_ref,
                         pieces_ref):
    pieces_ref[...] = jnp.zeros_like(pieces_ref)
    count = count_ref[0]
    slots = adj_ref.shape[0]

    def body(g, carry):
        base = g * group
        prods = []
        for i in range(group):
            t = base + i
            p = jnp.dot(adj_ref[t], panel_ref[cols_ref[t]], preferred_element_type=jnp.float32)
            prods.append(jnp.where(t < count, p, jnp.zeros_like(p)))
        for i in range(group):
            slot = rows_ref[base + i]
            pieces_ref[slot] += prods[i]
        return carry

    lax.fori_loop(0, slots // group, body, 0)


def block_product(row_ids, col_ids, count, dev_tiles, col_panel, row_tiles, nodes_dev):
    slots = dev_tiles.shape[0]
    feat_width = col_panel.shape[2]
    group = 16 if slots % 16 == 0 else 1
    smem = pl.BlockSpec(memory_space=pltpu.SMEM)
    vmem = pl.BlockSpec(memory_space=pltpu.VMEM)
    return pl.pallas_call(
        functools.partial(block_product_kernel, group),
        out_shape=jax.ShapeDtypeStruct((row_tiles, TILE, feat_width), jnp.float32),
        in_specs=[smem, smem, smem, vmem, vmem],
        out_specs=vmem,
        cost_estimate=pl.CostEstimate(
            flops=2 * slots * TILE * TILE * feat_width,
            bytes_accessed=slots * TILE * TILE * 2 + row_tiles * TILE * feat_width * 4,
            transcendentals=0,
        ),
    )(row_ids, col_ids, count, dev_tiles, col_panel)


def shards(features, degrees, adj_tiles, tile_rows, tile_cols, tile_counts):
    col_count = lax.axis_size("col")
    nodes_dev = features.shape[0]
    feat_width = features.shape[1]
    tile_slots = adj_tiles.shape[2]
    dev_tiles = adj_tiles.reshape(tile_slots, TILE, TILE)
    row_ids_all = tile_rows.reshape(tile_slots)
    col_ids_all = tile_cols.reshape(tile_slots)
    live_count = tile_counts.reshape(1)
    row_tiles = nodes_dev * col_count // TILE
    norm_scale = jnp.sqrt(KNN / degrees.astype(jnp.float32))[:, None]
    teleport = ALPHA * features.astype(jnp.float32)
    scale9 = jnp.broadcast_to((1.0 - ALPHA) * norm_scale, features.shape)
    scale = jnp.broadcast_to(norm_scale, features.shape)
    source = (norm_scale * features.astype(jnp.float32)).astype(jnp.bfloat16)
    gathered = row_all_gather(source)
    per_piece = nodes_dev // TILE
    n_y = col_count // (CORES * Z_RING)
    piece_j = row_ids_all // per_piece
    row_slots = (((piece_j % CORES) * Z_RING + (piece_j // CORES) % Z_RING) * n_y
                 + piece_j // (CORES * Z_RING)) * per_piece + row_ids_all % per_piece
    for repeat in range(STEPS):
        col_panel = gathered.reshape(-1, TILE, feat_width)
        pieces = block_product(
            row_slots, col_ids_all, live_count, dev_tiles, col_panel, row_tiles, nodes_dev
        )
        gathered = col_reduce_scatter(
            pieces.reshape(CORES, Z_RING, -1, nodes_dev, feat_width),
            scale9, scale, teleport, repeat == STEPS - 1,
        )
    return gathered


def solution(mesh):
    return jax.shard_map(
        shards,
        mesh=mesh,
        in_specs=(
            P(("row", "col"), None),
            P(("row", "col")),
            P("row", "col", None, None),
            P("row", "col", None),
            P("row", "col", None),
            P("row", "col"),
        ),
        out_specs=P(("row", "col"), None),
        check_vma=False,
    )
```

```python
import functools

import jax
import jax.numpy as jnp
from jax import lax
from jax.experimental import pallas as pl
from jax.experimental.pallas import tpu as pltpu
from jax.sharding import PartitionSpec as P

TILE = 64
KNN = 32
STEPS = 2

MESH = pl.DeviceIdType.MESH

ALPHA = 0.1


CORES = 2
Z_RING = 8


def reduce_scatter_kernel(n_z, chunks, last, x_ref, s9_ref, scale_ref, tele_ref, out_ref, ra,
                          recv_cw, recv_ccw, send_cw, send_ccw, fin, y_recv,
                          a_sems, cw_sems, ccw_sems, y_sems, *ag_sems):
    c = lax.axis_index("col")
    row = lax.axis_index("row")
    core = lax.rem(c, CORES)
    z = lax.rem(c // CORES, n_z)
    yh = c // (CORES * n_z)

    def dev(yh_, z_, core_):
        return (row, (yh_ * n_z + z_) * CORES + core_)

    partner = dev(yh, z, 1 - core)
    right = dev(yh, lax.rem(z + 1, n_z), core)
    left = dev(yh, lax.rem(z + n_z - 1, n_z), core)
    y_partner = dev(1 - yh, z, core)

    n_row = lax.axis_size("row")
    barrier = pltpu.get_barrier_semaphore()
    for peer in (partner, right, left, y_partner):
        pl.semaphore_signal(barrier, inc=1, device_id=peer, device_id_type=MESH)
    if not last:
        def greet(k, carry):
            pl.semaphore_signal(barrier, inc=1, device_id=(lax.rem(row + k, n_row), c),
                                device_id_type=MESH)
            return carry

        lax.fori_loop(1, n_row, greet, 0)
    pl.semaphore_wait(barrier, 4 if last else 3 + n_row)

    def rcopy(src, dst, sems, idx, peer):
        return pltpu.make_async_remote_copy(
            src_ref=src, dst_ref=dst, send_sem=sems.at[(0,) + idx], recv_sem=sems.at[(1,) + idx],
            device_id=peer, device_id_type=MESH,
        )

    def first(d):
        return lax.rem(z + (n_z - 1 if d == 0 else 1), n_z)

    def got(d, s):
        return lax.rem(z + ((2 * n_z - s - 2) if d == 0 else (s + 2)), n_z)

    need = [(first(0), 0), (first(1), 1)]
    for s in range(n_z - 1):
        need += [(got(0, s), 0), (got(1, s), 1)]
    copies_a = []
    for k, (g, h) in enumerate(need):
        cp = rcopy(x_ref.at[1 - core, g, h], ra.at[g, h], a_sems, (k,), partner)
        cp.start()
        copies_a.append(cp)

    def ready(d, s):
        copies_a[d if s < 0 else 2 + 2 * s + d].wait_recv()

    size = x_ref.shape[3] // chunks
    recv = (recv_cw, recv_ccw)
    send = (send_cw, send_ccw)
    sems = (cw_sems, ccw_sems)
    to = (right, left)
    sends = list(copies_a)

    def ring_copy(d, s, i):
        part = pl.ds(i * size, size)
        return rcopy(send[d].at[s, part], recv[d].at[s, part], sems[d], (s, i), to[d])

    def y_copy(i):
        part = pl.ds(i * size, size)
        return rcopy(fin.at[1 - yh, part], y_recv.at[part], y_sems, (i,), y_partner)

    for d in range(2):
        ready(d, -1)
        g = first(d)
        send[d][0] = x_ref[core, g, d] + ra[g, d]
        for i in range(chunks):
            cp = ring_copy(d, 0, i)
            cp.start()
            sends.append(cp)
    for s in range(n_z - 1):
        for d in range(2):
            ready(d, s)
        for i in range(chunks):
            part = pl.ds(i * size, size)
            for d in range(2):
                g = got(d, s)
                ring_copy(d, s, i).wait_recv()
                val = recv[d][s, part] + x_ref[core, g, d, part] + ra[g, d, part]
                if s < n_z - 2:
                    send[d][s + 1, part] = val
                    cp = ring_copy(d, s + 1, i)
                    cp.start()
                    sends.append(cp)
                else:
                    fin[d, part] = val
            if s == n_z - 2:
                cp = y_copy(i)
                cp.start()
                sends.append(cp)

    if not last:
        ag_send, ag_recv = ag_sems

        def ag_copy(peer, slot, i):
            part = pl.ds(i * size, size)
            return pltpu.make_async_remote_copy(
                src_ref=out_ref.at[row * chunks + i], dst_ref=out_ref.at[slot * chunks + i],
                send_sem=ag_send.at[peer, i], recv_sem=ag_recv.at[slot, i],
                device_id=(peer, c), device_id_type=MESH,
            )

    for i in range(chunks):
        part = pl.ds(i * size, size)
        y_copy(i).wait_recv()
        own = fin[yh, part] + y_recv[part]
        current = s9_ref[part] * own + tele_ref[part]
        if last:
            out_ref[part] = current.astype(out_ref.dtype)
        else:
            out_ref[row * chunks + i] = (scale_ref[part] * current).astype(out_ref.dtype)

            def ag_start(k, carry, i=i):
                ag_copy(lax.rem(row + k, n_row), row, i).start()
                return carry

            lax.fori_loop(1, n_row, ag_start, 0)
    if not last:
        out_ref[n_row * chunks] = jnp.zeros(out_ref.shape[1:], out_ref.dtype)

        def ag_finish(k, carry):
            for i in range(chunks):
                ag_copy(lax.rem(row + n_row - k, n_row), lax.rem(row + n_row - k, n_row), i).wait_recv()
                ag_copy(lax.rem(row + k, n_row), row, i).wait_send()
            return carry

        lax.fori_loop(1, n_row, ag_finish, 0)
    for cp in sends:
        cp.wait_send()


RS_CHUNKS = 4


def col_reduce_scatter(pieces, s9, scale, tele, last):
    cores, n_z, n_y, nodes_dev, feat_width = pieces.shape
    n_row = lax.axis_size("row")
    chunks = nodes_dev // TILE
    piece = (nodes_dev, feat_width)
    vmem = pl.BlockSpec(memory_space=pltpu.VMEM)
    out_shape = piece if last else (n_row * chunks + 1, TILE, feat_width)
    ag_sems = [] if last else [pltpu.SemaphoreType.DMA((n_row, chunks))] * 2
    return pl.pallas_call(
        functools.partial(reduce_scatter_kernel, n_z, chunks, last),
        out_shape=jax.ShapeDtypeStruct(out_shape, jnp.bfloat16),
        in_specs=[vmem] * 4,
        out_specs=vmem,
        scratch_shapes=[
            pltpu.VMEM((n_z, n_y) + piece, jnp.float32),
            pltpu.VMEM((n_z - 1,) + piece, jnp.float32),
            pltpu.VMEM((n_z - 1,) + piece, jnp.float32),
            pltpu.VMEM((n_z - 1,) + piece, jnp.float32),
            pltpu.VMEM((n_z - 1,) + piece, jnp.float32),
            pltpu.VMEM((n_y,) + piece, jnp.float32),
            pltpu.VMEM(piece, jnp.float32),
            pltpu.SemaphoreType.DMA((2, 2 * n_z)),
            pltpu.SemaphoreType.DMA((2, n_z - 1, chunks)),
            pltpu.SemaphoreType.DMA((2, n_z - 1, chunks)),
            pltpu.SemaphoreType.DMA((2, chunks)),
        ] + ag_sems,
        compiler_params=pltpu.CompilerParams(collective_id=2 if last else 0, has_side_effects=True),
    )(pieces, s9, scale, tele)


def all_gather_kernel(n, src_ref, out_ref, send_sem, recv_sem):
    me = lax.axis_index("row")
    col = lax.axis_index("col")
    per_piece = src_ref.shape[0]

    barrier = pltpu.get_barrier_semaphore()

    def greet(k, carry):
        peer = lax.rem(me + k, n)
        pl.semaphore_signal(barrier, inc=1, device_id=(peer, col), device_id_type=MESH)
        return carry

    lax.fori_loop(1, n, greet, 0)
    pl.semaphore_wait(barrier, n - 1)

    def copy(peer, slot):
        return pltpu.make_async_remote_copy(
            src_ref=src_ref,
            dst_ref=out_ref.at[pl.ds(slot * per_piece, per_piece)],
            send_sem=send_sem.at[peer],
            recv_sem=recv_sem.at[slot],
            device_id=(peer, col),
            device_id_type=MESH,
        )

    def start(k, carry):
        copy(lax.rem(me + k, n), me).start()
        return carry

    lax.fori_loop(1, n, start, 0)
    out_ref[pl.ds(me * per_piece, per_piece)] = src_ref[...]
    out_ref[n * per_piece] = jnp.zeros(out_ref.shape[1:], out_ref.dtype)

    def finish(k, carry):
        sender = lax.rem(me + n - k, n)
        copy(sender, sender).wait_recv()
        copy(lax.rem(me + k, n), me).wait_send()
        return carry

    lax.fori_loop(1, n, finish, 0)


def row_all_gather(source):
    n = lax.axis_size("row")
    nodes_dev, feat_width = source.shape
    per_piece = nodes_dev // TILE
    vmem = pl.BlockSpec(memory_space=pltpu.VMEM)
    return pl.pallas_call(
        functools.partial(all_gather_kernel, n),
        out_shape=jax.ShapeDtypeStruct((n * per_piece + 1, TILE, feat_width), source.dtype),
        in_specs=[vmem],
        out_specs=vmem,
        scratch_shapes=[pltpu.SemaphoreType.DMA((n,)), pltpu.SemaphoreType.DMA((n,))],
        compiler_params=pltpu.CompilerParams(collective_id=1, has_side_effects=True),
    )(source.reshape(per_piece, TILE, feat_width))


def block_product_kernel(group, rows_ref, cols_ref, adj_ref, panel_ref,
                         pieces_ref):
    pieces_ref[...] = jnp.zeros_like(pieces_ref)
    slots = adj_ref.shape[0]

    def body(g, carry):
        base = g * group
        prods = []
        for i in range(group):
            t = base + i
            p = jnp.dot(adj_ref[t], panel_ref[cols_ref[t]], preferred_element_type=jnp.float32)
            prods.append(p)
        for i in range(group):
            slot = rows_ref[base + i]
            pieces_ref[slot] += prods[i]
        return carry

    lax.fori_loop(0, slots // group, body, 0)


def block_product(row_ids, col_ids, dev_tiles, col_panel, row_tiles):
    slots = dev_tiles.shape[0]
    feat_width = col_panel.shape[2]
    group = 16 if slots % 16 == 0 else 1
    smem = pl.BlockSpec(memory_space=pltpu.SMEM)
    vmem = pl.BlockSpec(memory_space=pltpu.VMEM)
    return pl.pallas_call(
        functools.partial(block_product_kernel, group),
        out_shape=jax.ShapeDtypeStruct((row_tiles, TILE, feat_width), jnp.float32),
        in_specs=[smem, smem, vmem, vmem],
        out_specs=vmem,
        cost_estimate=pl.CostEstimate(
            flops=2 * slots * TILE * TILE * feat_width,
            bytes_accessed=slots * TILE * TILE * 2 + row_tiles * TILE * feat_width * 4,
            transcendentals=0,
        ),
    )(row_ids, col_ids, dev_tiles, col_panel)


def shards(features, degrees, adj_tiles, tile_rows, tile_cols, tile_counts):
    col_count = lax.axis_size("col")
    nodes_dev = features.shape[0]
    feat_width = features.shape[1]
    tile_slots = adj_tiles.shape[2]
    dev_tiles = adj_tiles.reshape(tile_slots, TILE, TILE)
    row_ids_all = tile_rows.reshape(tile_slots)
    live = jnp.arange(tile_slots, dtype=jnp.int32) < tile_counts.reshape(())
    panel_tiles = lax.axis_size("row") * (nodes_dev // TILE)
    col_ids_all = jnp.where(live, tile_cols.reshape(tile_slots), panel_tiles)
    row_tiles = nodes_dev * col_count // TILE
    norm_scale = jnp.sqrt(KNN / degrees.astype(jnp.float32))[:, None]
    teleport = ALPHA * features.astype(jnp.float32)
    scale9 = jnp.broadcast_to((1.0 - ALPHA) * norm_scale, features.shape)
    scale = jnp.broadcast_to(norm_scale, features.shape)
    source = (norm_scale * features.astype(jnp.float32)).astype(jnp.bfloat16)
    gathered = row_all_gather(source)
    per_piece = nodes_dev // TILE
    n_y = col_count // (CORES * Z_RING)
    piece_j = row_ids_all // per_piece
    row_slots = (((piece_j % CORES) * Z_RING + (piece_j // CORES) % Z_RING) * n_y
                 + piece_j // (CORES * Z_RING)) * per_piece + row_ids_all % per_piece
    for repeat in range(STEPS):
        pieces = block_product(row_slots, col_ids_all, dev_tiles, gathered, row_tiles)
        gathered = col_reduce_scatter(
            pieces.reshape(CORES, Z_RING, -1, nodes_dev, feat_width),
            scale9, scale, teleport, repeat == STEPS - 1,
        )
    return gathered


def solution(mesh):
    return jax.shard_map(
        shards,
        mesh=mesh,
        in_specs=(
            P(("row", "col"), None),
            P(("row", "col")),
            P("row", "col", None, None),
            P("row", "col", None),
            P("row", "col", None),
            P("row", "col"),
        ),
        out_specs=P(("row", "col"), None),
        check_vma=False,
    )
```

```python
import functools

import jax
import jax.numpy as jnp
from jax import lax
from jax.experimental import pallas as pl
from jax.experimental.pallas import tpu as pltpu
from jax.sharding import PartitionSpec as P

TILE = 64
KNN = 32
STEPS = 2

MESH = pl.DeviceIdType.MESH

ALPHA = 0.1


CORES = 2
Z_RING = 8


def reduce_scatter_kernel(n_z, chunks, last, x_ref, s9_ref, scale_ref, tele_ref, out_ref, ra,
                          recv_cw, recv_ccw, send_cw, send_ccw, fin, y_recv,
                          a_sems, cw_sems, ccw_sems, y_sems, *ag_sems):
    c = lax.axis_index("col")
    row = lax.axis_index("row")
    core = lax.rem(c, CORES)
    z = lax.rem(c // CORES, n_z)
    yh = c // (CORES * n_z)

    def dev(yh_, z_, core_):
        return (row, (yh_ * n_z + z_) * CORES + core_)

    partner = dev(yh, z, 1 - core)
    right = dev(yh, lax.rem(z + 1, n_z), core)
    left = dev(yh, lax.rem(z + n_z - 1, n_z), core)
    y_partner = dev(1 - yh, z, core)

    n_row = lax.axis_size("row")
    barrier = pltpu.get_barrier_semaphore()
    for peer in (partner, right, left, y_partner):
        pl.semaphore_signal(barrier, inc=1, device_id=peer, device_id_type=MESH)
    if not last:
        def greet(k, carry):
            pl.semaphore_signal(barrier, inc=1, device_id=(lax.rem(row + k, n_row), c),
                                device_id_type=MESH)
            return carry

        lax.fori_loop(1, n_row, greet, 0)
    pl.semaphore_wait(barrier, 4 if last else 3 + n_row)

    def rcopy(src, dst, sems, idx, peer):
        return pltpu.make_async_remote_copy(
            src_ref=src, dst_ref=dst, send_sem=sems.at[(0,) + idx], recv_sem=sems.at[(1,) + idx],
            device_id=peer, device_id_type=MESH,
        )

    def first(d):
        return lax.rem(z + (n_z - 1 if d == 0 else 1), n_z)

    def got(d, s):
        return lax.rem(z + ((2 * n_z - s - 2) if d == 0 else (s + 2)), n_z)

    need = [(first(0), 0), (first(1), 1)]
    for s in range(n_z - 1):
        need += [(got(0, s), 0), (got(1, s), 1)]
    copies_a = []
    for k, (g, h) in enumerate(need):
        cp = rcopy(x_ref.at[1 - core, g, h], ra.at[g, h], a_sems, (k,), partner)
        cp.start()
        copies_a.append(cp)

    def ready(d, s):
        copies_a[d if s < 0 else 2 + 2 * s + d].wait_recv()

    size = x_ref.shape[3] // chunks
    recv = (recv_cw, recv_ccw)
    send = (send_cw, send_ccw)
    sems = (cw_sems, ccw_sems)
    to = (right, left)
    sends = list(copies_a)

    def ring_copy(d, s, i):
        part = pl.ds(i * size, size)
        return rcopy(send[d].at[s, part], recv[d].at[s, part], sems[d], (s, i), to[d])

    def y_copy(i):
        part = pl.ds(i * size, size)
        return rcopy(fin.at[1 - yh, part], y_recv.at[part], y_sems, (i,), y_partner)

    for d in range(2):
        ready(d, -1)
        g = first(d)
        send[d][0] = x_ref[core, g, d] + ra[g, d]
        for i in range(chunks):
            cp = ring_copy(d, 0, i)
            cp.start()
            sends.append(cp)
    for s in range(n_z - 1):
        for d in range(2):
            ready(d, s)
        for i in range(chunks):
            part = pl.ds(i * size, size)
            for d in range(2):
                g = got(d, s)
                ring_copy(d, s, i).wait_recv()
                val = recv[d][s, part] + x_ref[core, g, d, part] + ra[g, d, part]
                if s < n_z - 2:
                    send[d][s + 1, part] = val
                    cp = ring_copy(d, s + 1, i)
                    cp.start()
                    sends.append(cp)
                else:
                    fin[d, part] = val
            if s == n_z - 2:
                cp = y_copy(i)
                cp.start()
                sends.append(cp)

    if not last:
        ag_send, ag_recv = ag_sems

        def ag_copy(peer, slot, i):
            part = pl.ds(i * size, size)
            return pltpu.make_async_remote_copy(
                src_ref=out_ref.at[row * chunks + i], dst_ref=out_ref.at[slot * chunks + i],
                send_sem=ag_send.at[peer, i], recv_sem=ag_recv.at[slot, i],
                device_id=(peer, c), device_id_type=MESH,
            )

    for i in range(chunks):
        part = pl.ds(i * size, size)
        y_copy(i).wait_recv()
        own = fin[yh, part] + y_recv[part]
        current = s9_ref[part] * own + tele_ref[part]
        if last:
            out_ref[part] = current.astype(out_ref.dtype)
        else:
            out_ref[row * chunks + i] = (scale_ref[part] * current).astype(out_ref.dtype)

            def ag_start(k, carry, i=i):
                ag_copy(lax.rem(row + k, n_row), row, i).start()
                return carry

            lax.fori_loop(1, n_row, ag_start, 0)
    if not last:
        out_ref[n_row * chunks] = jnp.zeros(out_ref.shape[1:], out_ref.dtype)

        def ag_finish(k, carry):
            for i in range(chunks):
                ag_copy(lax.rem(row + n_row - k, n_row), lax.rem(row + n_row - k, n_row), i).wait_recv()
                ag_copy(lax.rem(row + k, n_row), row, i).wait_send()
            return carry

        lax.fori_loop(1, n_row, ag_finish, 0)
    for cp in sends:
        cp.wait_send()


RS_CHUNKS = 4


def col_reduce_scatter(pieces, s9, scale, tele, last):
    cores, n_z, n_y, nodes_dev, feat_width = pieces.shape
    n_row = lax.axis_size("row")
    chunks = nodes_dev // TILE
    piece = (nodes_dev, feat_width)
    vmem = pl.BlockSpec(memory_space=pltpu.VMEM)
    out_shape = piece if last else (n_row * chunks + 1, TILE, feat_width)
    ag_sems = [] if last else [pltpu.SemaphoreType.DMA((n_row, chunks))] * 2
    return pl.pallas_call(
        functools.partial(reduce_scatter_kernel, n_z, chunks, last),
        out_shape=jax.ShapeDtypeStruct(out_shape, jnp.bfloat16),
        in_specs=[vmem] * 4,
        out_specs=vmem,
        scratch_shapes=[
            pltpu.VMEM((n_z, n_y) + piece, jnp.float32),
            pltpu.VMEM((n_z - 1,) + piece, jnp.float32),
            pltpu.VMEM((n_z - 1,) + piece, jnp.float32),
            pltpu.VMEM((n_z - 1,) + piece, jnp.float32),
            pltpu.VMEM((n_z - 1,) + piece, jnp.float32),
            pltpu.VMEM((n_y,) + piece, jnp.float32),
            pltpu.VMEM(piece, jnp.float32),
            pltpu.SemaphoreType.DMA((2, 2 * n_z)),
            pltpu.SemaphoreType.DMA((2, n_z - 1, chunks)),
            pltpu.SemaphoreType.DMA((2, n_z - 1, chunks)),
            pltpu.SemaphoreType.DMA((2, chunks)),
        ] + ag_sems,
        compiler_params=pltpu.CompilerParams(collective_id=2 if last else 0, has_side_effects=True),
    )(pieces, s9, scale, tele)


def all_gather_kernel(n, src_ref, adj_ref, out_ref, tiles_ref, send_sem, recv_sem):
    me = lax.axis_index("row")
    col = lax.axis_index("col")
    per_piece = src_ref.shape[0]

    barrier = pltpu.get_barrier_semaphore()

    def greet(k, carry):
        peer = lax.rem(me + k, n)
        pl.semaphore_signal(barrier, inc=1, device_id=(peer, col), device_id_type=MESH)
        return carry

    lax.fori_loop(1, n, greet, 0)
    pl.semaphore_wait(barrier, n - 1)

    def copy(peer, slot):
        return pltpu.make_async_remote_copy(
            src_ref=src_ref,
            dst_ref=out_ref.at[pl.ds(slot * per_piece, per_piece)],
            send_sem=send_sem.at[peer],
            recv_sem=recv_sem.at[slot],
            device_id=(peer, col),
            device_id_type=MESH,
        )

    def start(k, carry):
        copy(lax.rem(me + k, n), me).start()
        return carry

    lax.fori_loop(1, n, start, 0)
    out_ref[pl.ds(me * per_piece, per_piece)] = src_ref[...]
    out_ref[n * per_piece] = jnp.zeros(out_ref.shape[1:], out_ref.dtype)

    rows = 16

    def shape_tiles(g, carry):
        at = pl.ds(pl.multiple_of(g * rows, rows), rows)
        tiles_ref[at] = adj_ref[at].reshape((rows,) + tiles_ref.shape[1:])
        return carry

    lax.fori_loop(0, adj_ref.shape[0] // rows, shape_tiles, 0)

    def finish(k, carry):
        sender = lax.rem(me + n - k, n)
        copy(sender, sender).wait_recv()
        copy(lax.rem(me + k, n), me).wait_send()
        return carry

    lax.fori_loop(1, n, finish, 0)


def row_all_gather(source, adj_flat):
    n = lax.axis_size("row")
    nodes_dev, feat_width = source.shape
    per_piece = nodes_dev // TILE
    vmem = pl.BlockSpec(memory_space=pltpu.VMEM)
    return pl.pallas_call(
        functools.partial(all_gather_kernel, n),
        out_shape=(
            jax.ShapeDtypeStruct((n * per_piece + 1, TILE, feat_width), source.dtype),
            jax.ShapeDtypeStruct((adj_flat.shape[0], TILE, TILE), adj_flat.dtype),
        ),
        in_specs=[vmem, vmem],
        out_specs=(vmem, vmem),
        scratch_shapes=[pltpu.SemaphoreType.DMA((n,)), pltpu.SemaphoreType.DMA((n,))],
        compiler_params=pltpu.CompilerParams(collective_id=1, has_side_effects=True),
    )(source.reshape(per_piece, TILE, feat_width), adj_flat)


def block_product_kernel(group, rows_ref, cols_ref, adj_ref, panel_ref,
                         pieces_ref):
    pieces_ref[...] = jnp.zeros_like(pieces_ref)
    slots = adj_ref.shape[0]

    def body(g, carry):
        base = g * group
        prods = []
        for i in range(group):
            t = base + i
            p = jnp.dot(adj_ref[t], panel_ref[cols_ref[t]], preferred_element_type=jnp.float32)
            prods.append(p)
        for i in range(group):
            slot = rows_ref[base + i]
            pieces_ref[slot] += prods[i]
        return carry

    lax.fori_loop(0, slots // group, body, 0)


def block_product(row_ids, col_ids, dev_tiles, col_panel, row_tiles):
    slots = dev_tiles.shape[0]
    feat_width = col_panel.shape[2]
    group = 16 if slots % 16 == 0 else 1
    smem = pl.BlockSpec(memory_space=pltpu.SMEM)
    vmem = pl.BlockSpec(memory_space=pltpu.VMEM)
    return pl.pallas_call(
        functools.partial(block_product_kernel, group),
        out_shape=jax.ShapeDtypeStruct((row_tiles, TILE, feat_width), jnp.float32),
        in_specs=[smem, smem, vmem, vmem],
        out_specs=vmem,
        cost_estimate=pl.CostEstimate(
            flops=2 * slots * TILE * TILE * feat_width,
            bytes_accessed=slots * TILE * TILE * 2 + row_tiles * TILE * feat_width * 4,
            transcendentals=0,
        ),
    )(row_ids, col_ids, dev_tiles, col_panel)


def shards(features, degrees, adj_tiles, tile_rows, tile_cols, tile_counts):
    col_count = lax.axis_size("col")
    nodes_dev = features.shape[0]
    feat_width = features.shape[1]
    tile_slots = adj_tiles.shape[2]
    row_ids_all = tile_rows.reshape(tile_slots)
    live = jnp.arange(tile_slots, dtype=jnp.int32) < tile_counts.reshape(())
    panel_tiles = lax.axis_size("row") * (nodes_dev // TILE)
    col_ids_all = jnp.where(live, tile_cols.reshape(tile_slots), panel_tiles)
    row_tiles = nodes_dev * col_count // TILE
    norm_scale = jnp.sqrt(KNN / degrees.astype(jnp.float32))[:, None]
    teleport = ALPHA * features.astype(jnp.float32)
    scale9 = jnp.broadcast_to((1.0 - ALPHA) * norm_scale, features.shape)
    scale = jnp.broadcast_to(norm_scale, features.shape)
    source = (norm_scale * features.astype(jnp.float32)).astype(jnp.bfloat16)
    gathered, dev_tiles = row_all_gather(source, adj_tiles.reshape(tile_slots, TILE * TILE))
    per_piece = nodes_dev // TILE
    n_y = col_count // (CORES * Z_RING)
    piece_j = row_ids_all // per_piece
    row_slots = (((piece_j % CORES) * Z_RING + (piece_j // CORES) % Z_RING) * n_y
                 + piece_j // (CORES * Z_RING)) * per_piece + row_ids_all % per_piece
    for repeat in range(STEPS):
        pieces = block_product(row_slots, col_ids_all, dev_tiles, gathered, row_tiles)
        gathered = col_reduce_scatter(
            pieces.reshape(CORES, Z_RING, -1, nodes_dev, feat_width),
            scale9, scale, teleport, repeat == STEPS - 1,
        )
    return gathered


def solution(mesh):
    return jax.shard_map(
        shards,
        mesh=mesh,
        in_specs=(
            P(("row", "col"), None),
            P(("row", "col")),
            P("row", "col", None, None),
            P("row", "col", None),
            P("row", "col", None),
            P("row", "col"),
        ),
        out_specs=P(("row", "col"), None),
        check_vma=False,
    )
```

```python
import functools

import jax
import jax.numpy as jnp
from jax import lax
from jax.experimental import pallas as pl
from jax.experimental.pallas import tpu as pltpu
from jax.sharding import PartitionSpec as P

TILE = 64
KNN = 32
STEPS = 2

MESH = pl.DeviceIdType.MESH

ALPHA = 0.1


CORES = 2
Z_RING = 8


def reduce_scatter_kernel(n_z, chunks, last, x_ref, s9_ref, scale_ref, tele_ref, out_ref, ra,
                          recv_cw, recv_ccw, send_cw, send_ccw, fin, y_recv,
                          a_sems, cw_sems, ccw_sems, y_sems, *ag_sems):
    c = lax.axis_index("col")
    row = lax.axis_index("row")
    core = lax.rem(c, CORES)
    z = lax.rem(c // CORES, n_z)
    yh = c // (CORES * n_z)

    def dev(yh_, z_, core_):
        return (row, (yh_ * n_z + z_) * CORES + core_)

    partner = dev(yh, z, 1 - core)
    right = dev(yh, lax.rem(z + 1, n_z), core)
    left = dev(yh, lax.rem(z + n_z - 1, n_z), core)
    y_partner = dev(1 - yh, z, core)

    n_row = lax.axis_size("row")
    barrier = pltpu.get_barrier_semaphore()
    for peer in (partner, right, left, y_partner):
        pl.semaphore_signal(barrier, inc=1, device_id=peer, device_id_type=MESH)
    if not last:
        def greet(k, carry):
            pl.semaphore_signal(barrier, inc=1, device_id=(lax.rem(row + k, n_row), c),
                                device_id_type=MESH)
            return carry

        lax.fori_loop(1, n_row, greet, 0)
    pl.semaphore_wait(barrier, 4 if last else 3 + n_row)

    def rcopy(src, dst, sems, idx, peer):
        return pltpu.make_async_remote_copy(
            src_ref=src, dst_ref=dst, send_sem=sems.at[(0,) + idx], recv_sem=sems.at[(1,) + idx],
            device_id=peer, device_id_type=MESH,
        )

    def first(d):
        return lax.rem(z + (n_z - 1 if d == 0 else 1), n_z)

    def got(d, s):
        return lax.rem(z + ((2 * n_z - s - 2) if d == 0 else (s + 2)), n_z)

    need = [(first(0), 0), (first(1), 1)]
    for s in range(n_z - 1):
        need += [(got(0, s), 0), (got(1, s), 1)]
    copies_a = []
    for k, (g, h) in enumerate(need):
        cp = rcopy(x_ref.at[1 - core, g, h], ra.at[g, h], a_sems, (k,), partner)
        cp.start()
        copies_a.append(cp)

    def ready(d, s):
        copies_a[d if s < 0 else 2 + 2 * s + d].wait_recv()

    size = x_ref.shape[3] // chunks
    recv = (recv_cw, recv_ccw)
    send = (send_cw, send_ccw)
    sems = (cw_sems, ccw_sems)
    to = (right, left)
    sends = list(copies_a)

    def ring_copy(d, s, i):
        part = pl.ds(i * size, size)
        return rcopy(send[d].at[s, part], recv[d].at[s, part], sems[d], (s, i), to[d])

    def y_copy(i):
        part = pl.ds(i * size, size)
        return rcopy(fin.at[1 - yh, part], y_recv.at[part], y_sems, (i,), y_partner)

    for d in range(2):
        ready(d, -1)
        g = first(d)
        send[d][0] = x_ref[core, g, d] + ra[g, d]
        for i in range(chunks):
            cp = ring_copy(d, 0, i)
            cp.start()
            sends.append(cp)
    for s in range(n_z - 1):
        for d in range(2):
            ready(d, s)
        for i in range(chunks):
            part = pl.ds(i * size, size)
            for d in range(2):
                g = got(d, s)
                ring_copy(d, s, i).wait_recv()
                val = recv[d][s, part] + x_ref[core, g, d, part] + ra[g, d, part]
                if s < n_z - 2:
                    send[d][s + 1, part] = val
                    cp = ring_copy(d, s + 1, i)
                    cp.start()
                    sends.append(cp)
                else:
                    fin[d, part] = val
            if s == n_z - 2:
                cp = y_copy(i)
                cp.start()
                sends.append(cp)

    if not last:
        ag_send, ag_recv = ag_sems

        def ag_copy(peer, slot, i):
            part = pl.ds(i * size, size)
            return pltpu.make_async_remote_copy(
                src_ref=out_ref.at[row * chunks + i], dst_ref=out_ref.at[slot * chunks + i],
                send_sem=ag_send.at[peer, i], recv_sem=ag_recv.at[slot, i],
                device_id=(peer, c), device_id_type=MESH,
            )

    for i in range(chunks):
        part = pl.ds(i * size, size)
        y_copy(i).wait_recv()
        own = fin[yh, part] + y_recv[part]
        current = s9_ref[part] * own + tele_ref[part]
        if last:
            out_ref[part] = current.astype(out_ref.dtype)
        else:
            out_ref[row * chunks + i] = (scale_ref[part] * current).astype(out_ref.dtype)

            def ag_start(k, carry, i=i):
                ag_copy(lax.rem(row + k, n_row), row, i).start()
                return carry

            lax.fori_loop(1, n_row, ag_start, 0)
    if not last:
        out_ref[n_row * chunks] = jnp.zeros(out_ref.shape[1:], out_ref.dtype)

        def ag_finish(k, carry):
            for i in range(chunks):
                ag_copy(lax.rem(row + n_row - k, n_row), lax.rem(row + n_row - k, n_row), i).wait_recv()
                ag_copy(lax.rem(row + k, n_row), row, i).wait_send()
            return carry

        lax.fori_loop(1, n_row, ag_finish, 0)
    for cp in sends:
        cp.wait_send()


RS_CHUNKS = 4


def col_reduce_scatter(pieces, s9, scale, tele, last):
    cores, n_z, n_y, nodes_dev, feat_width = pieces.shape
    n_row = lax.axis_size("row")
    chunks = nodes_dev // TILE
    piece = (nodes_dev, feat_width)
    vmem = pl.BlockSpec(memory_space=pltpu.VMEM)
    out_shape = piece if last else (n_row * chunks + 1, TILE, feat_width)
    ag_sems = [] if last else [pltpu.SemaphoreType.DMA((n_row, chunks))] * 2
    return pl.pallas_call(
        functools.partial(reduce_scatter_kernel, n_z, chunks, last),
        out_shape=jax.ShapeDtypeStruct(out_shape, jnp.float32 if last else jnp.bfloat16),
        in_specs=[vmem] * 4,
        out_specs=vmem,
        scratch_shapes=[
            pltpu.VMEM((n_z, n_y) + piece, jnp.float32),
            pltpu.VMEM((n_z - 1,) + piece, jnp.float32),
            pltpu.VMEM((n_z - 1,) + piece, jnp.float32),
            pltpu.VMEM((n_z - 1,) + piece, jnp.float32),
            pltpu.VMEM((n_z - 1,) + piece, jnp.float32),
            pltpu.VMEM((n_y,) + piece, jnp.float32),
            pltpu.VMEM(piece, jnp.float32),
            pltpu.SemaphoreType.DMA((2, 2 * n_z)),
            pltpu.SemaphoreType.DMA((2, n_z - 1, chunks)),
            pltpu.SemaphoreType.DMA((2, n_z - 1, chunks)),
            pltpu.SemaphoreType.DMA((2, chunks)),
        ] + ag_sems,
        compiler_params=pltpu.CompilerParams(collective_id=2 if last else 0, has_side_effects=True),
    )(pieces, s9, scale, tele)


def all_gather_kernel(n, src_ref, adj_ref, out_ref, tiles_ref, send_sem, recv_sem):
    me = lax.axis_index("row")
    col = lax.axis_index("col")
    per_piece = src_ref.shape[0]

    barrier = pltpu.get_barrier_semaphore()

    def greet(k, carry):
        peer = lax.rem(me + k, n)
        pl.semaphore_signal(barrier, inc=1, device_id=(peer, col), device_id_type=MESH)
        return carry

    lax.fori_loop(1, n, greet, 0)
    pl.semaphore_wait(barrier, n - 1)

    def copy(peer, slot):
        return pltpu.make_async_remote_copy(
            src_ref=src_ref,
            dst_ref=out_ref.at[pl.ds(slot * per_piece, per_piece)],
            send_sem=send_sem.at[peer],
            recv_sem=recv_sem.at[slot],
            device_id=(peer, col),
            device_id_type=MESH,
        )

    def start(k, carry):
        copy(lax.rem(me + k, n), me).start()
        return carry

    lax.fori_loop(1, n, start, 0)
    out_ref[pl.ds(me * per_piece, per_piece)] = src_ref[...]
    out_ref[n * per_piece] = jnp.zeros(out_ref.shape[1:], out_ref.dtype)

    rows = 16

    def shape_tiles(g, carry):
        at = pl.ds(pl.multiple_of(g * rows, rows), rows)
        tiles_ref[at] = adj_ref[at].reshape((rows,) + tiles_ref.shape[1:])
        return carry

    lax.fori_loop(0, adj_ref.shape[0] // rows, shape_tiles, 0)

    def finish(k, carry):
        sender = lax.rem(me + n - k, n)
        copy(sender, sender).wait_recv()
        copy(lax.rem(me + k, n), me).wait_send()
        return carry

    lax.fori_loop(1, n, finish, 0)


def row_all_gather(source, adj_flat):
    n = lax.axis_size("row")
    nodes_dev, feat_width = source.shape
    per_piece = nodes_dev // TILE
    vmem = pl.BlockSpec(memory_space=pltpu.VMEM)
    return pl.pallas_call(
        functools.partial(all_gather_kernel, n),
        out_shape=(
            jax.ShapeDtypeStruct((n * per_piece + 1, TILE, feat_width), source.dtype),
            jax.ShapeDtypeStruct((adj_flat.shape[0], TILE, TILE), adj_flat.dtype),
        ),
        in_specs=[vmem, vmem],
        out_specs=(vmem, vmem),
        scratch_shapes=[pltpu.SemaphoreType.DMA((n,)), pltpu.SemaphoreType.DMA((n,))],
        compiler_params=pltpu.CompilerParams(collective_id=1, has_side_effects=True),
    )(source.reshape(per_piece, TILE, feat_width), adj_flat)


def block_product_kernel(group, rows_ref, cols_ref, adj_ref, panel_ref,
                         pieces_ref):
    pieces_ref[...] = jnp.zeros_like(pieces_ref)
    slots = adj_ref.shape[0]

    def body(g, carry):
        base = g * group
        prods = []
        for i in range(group):
            t = base + i
            p = jnp.dot(adj_ref[t], panel_ref[cols_ref[t]], preferred_element_type=jnp.float32)
            prods.append(p)
        for i in range(group):
            slot = rows_ref[base + i]
            pieces_ref[slot] += prods[i]
        return carry

    lax.fori_loop(0, slots // group, body, 0)


def block_product(row_ids, col_ids, dev_tiles, col_panel, row_tiles):
    slots = dev_tiles.shape[0]
    feat_width = col_panel.shape[2]
    group = 16 if slots % 16 == 0 else 1
    smem = pl.BlockSpec(memory_space=pltpu.SMEM)
    vmem = pl.BlockSpec(memory_space=pltpu.VMEM)
    return pl.pallas_call(
        functools.partial(block_product_kernel, group),
        out_shape=jax.ShapeDtypeStruct((row_tiles, TILE, feat_width), jnp.float32),
        in_specs=[smem, smem, vmem, vmem],
        out_specs=vmem,
        cost_estimate=pl.CostEstimate(
            flops=2 * slots * TILE * TILE * feat_width,
            bytes_accessed=slots * TILE * TILE * 2 + row_tiles * TILE * feat_width * 4,
            transcendentals=0,
        ),
    )(row_ids, col_ids, dev_tiles, col_panel)


def shards(features, degrees, adj_tiles, tile_rows, tile_cols, tile_counts):
    col_count = lax.axis_size("col")
    nodes_dev = features.shape[0]
    feat_width = features.shape[1]
    tile_slots = adj_tiles.shape[2]
    row_ids_all = tile_rows.reshape(tile_slots)
    live = jnp.arange(tile_slots, dtype=jnp.int32) < tile_counts.reshape(())
    panel_tiles = lax.axis_size("row") * (nodes_dev // TILE)
    col_ids_all = jnp.where(live, tile_cols.reshape(tile_slots), panel_tiles)
    row_tiles = nodes_dev * col_count // TILE
    norm_scale = jnp.sqrt(KNN / degrees.astype(jnp.float32))[:, None]
    teleport = ALPHA * features.astype(jnp.float32)
    scale9 = jnp.broadcast_to((1.0 - ALPHA) * norm_scale, features.shape)
    scale = jnp.broadcast_to(norm_scale, features.shape)
    source = (norm_scale * features.astype(jnp.float32)).astype(jnp.bfloat16)
    gathered, dev_tiles = row_all_gather(source, adj_tiles.reshape(tile_slots, TILE * TILE))
    per_piece = nodes_dev // TILE
    n_y = col_count // (CORES * Z_RING)
    piece_j = row_ids_all // per_piece
    row_slots = (((piece_j % CORES) * Z_RING + (piece_j // CORES) % Z_RING) * n_y
                 + piece_j // (CORES * Z_RING)) * per_piece + row_ids_all % per_piece
    for repeat in range(STEPS):
        pieces = block_product(row_slots, col_ids_all, dev_tiles, gathered, row_tiles)
        gathered = col_reduce_scatter(
            pieces.reshape(CORES, Z_RING, -1, nodes_dev, feat_width),
            scale9, scale, teleport, repeat == STEPS - 1,
        )
    return gathered.astype(jnp.bfloat16)


def solution(mesh):
    return jax.shard_map(
        shards,
        mesh=mesh,
        in_specs=(
            P(("row", "col"), None),
            P(("row", "col")),
            P("row", "col", None, None),
            P("row", "col", None),
            P("row", "col", None),
            P("row", "col"),
        ),
        out_specs=P(("row", "col"), None),
        check_vma=False,
    )
```

```python
import functools

import jax
import jax.numpy as jnp
from jax import lax
from jax.experimental import pallas as pl
from jax.experimental.pallas import tpu as pltpu
from jax.sharding import PartitionSpec as P

TILE = 64
KNN = 32
STEPS = 2

MESH = pl.DeviceIdType.MESH

ALPHA = 0.1


CORES = 2
Z_RING = 8


def reduce_scatter_kernel(n_z, chunks, last, x_ref, scale_ref, feat_ref, out_ref, ra,
                          recv_cw, recv_ccw, send_cw, send_ccw, fin, y_recv,
                          a_sems, cw_sems, ccw_sems, y_sems, *ag_sems):
    c = lax.axis_index("col")
    row = lax.axis_index("row")
    core = lax.rem(c, CORES)
    z = lax.rem(c // CORES, n_z)
    yh = c // (CORES * n_z)

    def dev(yh_, z_, core_):
        return (row, (yh_ * n_z + z_) * CORES + core_)

    partner = dev(yh, z, 1 - core)
    right = dev(yh, lax.rem(z + 1, n_z), core)
    left = dev(yh, lax.rem(z + n_z - 1, n_z), core)
    y_partner = dev(1 - yh, z, core)

    n_row = lax.axis_size("row")
    barrier = pltpu.get_barrier_semaphore()
    for peer in (partner, right, left, y_partner):
        pl.semaphore_signal(barrier, inc=1, device_id=peer, device_id_type=MESH)
    if not last:
        def greet(k, carry):
            pl.semaphore_signal(barrier, inc=1, device_id=(lax.rem(row + k, n_row), c),
                                device_id_type=MESH)
            return carry

        lax.fori_loop(1, n_row, greet, 0)
    pl.semaphore_wait(barrier, 4 if last else 3 + n_row)

    def rcopy(src, dst, sems, idx, peer):
        return pltpu.make_async_remote_copy(
            src_ref=src, dst_ref=dst, send_sem=sems.at[(0,) + idx], recv_sem=sems.at[(1,) + idx],
            device_id=peer, device_id_type=MESH,
        )

    def first(d):
        return lax.rem(z + (n_z - 1 if d == 0 else 1), n_z)

    def got(d, s):
        return lax.rem(z + ((2 * n_z - s - 2) if d == 0 else (s + 2)), n_z)

    need = [(first(0), 0), (first(1), 1)]
    for s in range(n_z - 1):
        need += [(got(0, s), 0), (got(1, s), 1)]
    copies_a = []
    for k, (g, h) in enumerate(need):
        cp = rcopy(x_ref.at[1 - core, g, h], ra.at[g, h], a_sems, (k,), partner)
        cp.start()
        copies_a.append(cp)

    def ready(d, s):
        copies_a[d if s < 0 else 2 + 2 * s + d].wait_recv()

    size = x_ref.shape[3] // chunks
    recv = (recv_cw, recv_ccw)
    send = (send_cw, send_ccw)
    sems = (cw_sems, ccw_sems)
    to = (right, left)
    sends = list(copies_a)

    def ring_copy(d, s, i):
        part = pl.ds(i * size, size)
        return rcopy(send[d].at[s, part], recv[d].at[s, part], sems[d], (s, i), to[d])

    def y_copy(i):
        part = pl.ds(i * size, size)
        return rcopy(fin.at[1 - yh, part], y_recv.at[part], y_sems, (i,), y_partner)

    for d in range(2):
        ready(d, -1)
        g = first(d)
        send[d][0] = x_ref[core, g, d] + ra[g, d]
        for i in range(chunks):
            cp = ring_copy(d, 0, i)
            cp.start()
            sends.append(cp)
    for s in range(n_z - 1):
        for d in range(2):
            ready(d, s)
        for i in range(chunks):
            part = pl.ds(i * size, size)
            for d in range(2):
                g = got(d, s)
                ring_copy(d, s, i).wait_recv()
                val = recv[d][s, part] + x_ref[core, g, d, part] + ra[g, d, part]
                if s < n_z - 2:
                    send[d][s + 1, part] = val
                    cp = ring_copy(d, s + 1, i)
                    cp.start()
                    sends.append(cp)
                else:
                    fin[d, part] = val
            if s == n_z - 2:
                cp = y_copy(i)
                cp.start()
                sends.append(cp)

    if not last:
        ag_send, ag_recv = ag_sems

        def ag_copy(peer, slot, i):
            part = pl.ds(i * size, size)
            return pltpu.make_async_remote_copy(
                src_ref=out_ref.at[row * chunks + i], dst_ref=out_ref.at[slot * chunks + i],
                send_sem=ag_send.at[peer, i], recv_sem=ag_recv.at[slot, i],
                device_id=(peer, c), device_id_type=MESH,
            )

    for i in range(chunks):
        part = pl.ds(i * size, size)
        y_copy(i).wait_recv()
        own = fin[yh, part] + y_recv[part]
        current = ((1.0 - ALPHA) * scale_ref[part]) * own + ALPHA * feat_ref[part].astype(jnp.float32)
        if last:
            out_ref[part] = current.astype(out_ref.dtype)
        else:
            out_ref[row * chunks + i] = (scale_ref[part] * current).astype(out_ref.dtype)

            def ag_start(k, carry, i=i):
                ag_copy(lax.rem(row + k, n_row), row, i).start()
                return carry

            lax.fori_loop(1, n_row, ag_start, 0)
    if not last:
        out_ref[n_row * chunks] = jnp.zeros(out_ref.shape[1:], out_ref.dtype)

        def ag_finish(k, carry):
            for i in range(chunks):
                ag_copy(lax.rem(row + n_row - k, n_row), lax.rem(row + n_row - k, n_row), i).wait_recv()
                ag_copy(lax.rem(row + k, n_row), row, i).wait_send()
            return carry

        lax.fori_loop(1, n_row, ag_finish, 0)
    for cp in sends:
        cp.wait_send()


RS_CHUNKS = 4


def col_reduce_scatter(pieces, scale, features, last):
    cores, n_z, n_y, nodes_dev, feat_width = pieces.shape
    n_row = lax.axis_size("row")
    chunks = nodes_dev // TILE
    piece = (nodes_dev, feat_width)
    vmem = pl.BlockSpec(memory_space=pltpu.VMEM)
    out_shape = piece if last else (n_row * chunks + 1, TILE, feat_width)
    ag_sems = [] if last else [pltpu.SemaphoreType.DMA((n_row, chunks))] * 2
    return pl.pallas_call(
        functools.partial(reduce_scatter_kernel, n_z, chunks, last),
        out_shape=jax.ShapeDtypeStruct(out_shape, jnp.float32 if last else jnp.bfloat16),
        in_specs=[vmem] * 3,
        out_specs=vmem,
        scratch_shapes=[
            pltpu.VMEM((n_z, n_y) + piece, jnp.float32),
            pltpu.VMEM((n_z - 1,) + piece, jnp.float32),
            pltpu.VMEM((n_z - 1,) + piece, jnp.float32),
            pltpu.VMEM((n_z - 1,) + piece, jnp.float32),
            pltpu.VMEM((n_z - 1,) + piece, jnp.float32),
            pltpu.VMEM((n_y,) + piece, jnp.float32),
            pltpu.VMEM(piece, jnp.float32),
            pltpu.SemaphoreType.DMA((2, 2 * n_z)),
            pltpu.SemaphoreType.DMA((2, n_z - 1, chunks)),
            pltpu.SemaphoreType.DMA((2, n_z - 1, chunks)),
            pltpu.SemaphoreType.DMA((2, chunks)),
        ] + ag_sems,
        compiler_params=pltpu.CompilerParams(collective_id=2 if last else 0, has_side_effects=True),
    )(pieces, scale, features)


def all_gather_kernel(n, feat_ref, scale_ref, adj_ref, out_ref, tiles_ref, src_ref, send_sem,
                      recv_sem):
    me = lax.axis_index("row")
    col = lax.axis_index("col")
    per_piece = src_ref.shape[0]
    src_ref[...] = (scale_ref[...] * feat_ref[...].astype(jnp.float32)).astype(src_ref.dtype)

    barrier = pltpu.get_barrier_semaphore()

    def greet(k, carry):
        peer = lax.rem(me + k, n)
        pl.semaphore_signal(barrier, inc=1, device_id=(peer, col), device_id_type=MESH)
        return carry

    lax.fori_loop(1, n, greet, 0)
    pl.semaphore_wait(barrier, n - 1)

    def copy(peer, slot):
        return pltpu.make_async_remote_copy(
            src_ref=src_ref,
            dst_ref=out_ref.at[pl.ds(slot * per_piece, per_piece)],
            send_sem=send_sem.at[peer],
            recv_sem=recv_sem.at[slot],
            device_id=(peer, col),
            device_id_type=MESH,
        )

    def start(k, carry):
        copy(lax.rem(me + k, n), me).start()
        return carry

    lax.fori_loop(1, n, start, 0)
    out_ref[pl.ds(me * per_piece, per_piece)] = src_ref[...]
    out_ref[n * per_piece] = jnp.zeros(out_ref.shape[1:], out_ref.dtype)

    rows = 16

    def shape_tiles(g, carry):
        at = pl.ds(pl.multiple_of(g * rows, rows), rows)
        tiles_ref[at] = adj_ref[at].reshape((rows,) + tiles_ref.shape[1:])
        return carry

    lax.fori_loop(0, adj_ref.shape[0] // rows, shape_tiles, 0)

    def finish(k, carry):
        sender = lax.rem(me + n - k, n)
        copy(sender, sender).wait_recv()
        copy(lax.rem(me + k, n), me).wait_send()
        return carry

    lax.fori_loop(1, n, finish, 0)


def row_all_gather(features, scale, adj_flat):
    n = lax.axis_size("row")
    nodes_dev, feat_width = features.shape
    per_piece = nodes_dev // TILE
    vmem = pl.BlockSpec(memory_space=pltpu.VMEM)
    return pl.pallas_call(
        functools.partial(all_gather_kernel, n),
        out_shape=(
            jax.ShapeDtypeStruct((n * per_piece + 1, TILE, feat_width), jnp.bfloat16),
            jax.ShapeDtypeStruct((adj_flat.shape[0], TILE, TILE), adj_flat.dtype),
        ),
        in_specs=[vmem, vmem, vmem],
        out_specs=(vmem, vmem),
        scratch_shapes=[
            pltpu.VMEM((per_piece, TILE, feat_width), jnp.bfloat16),
            pltpu.SemaphoreType.DMA((n,)),
            pltpu.SemaphoreType.DMA((n,)),
        ],
        compiler_params=pltpu.CompilerParams(collective_id=1, has_side_effects=True),
    )(features.reshape(per_piece, TILE, feat_width), scale.reshape(per_piece, TILE, feat_width),
      adj_flat)


def block_product_kernel(group, rows_ref, cols_ref, adj_ref, panel_ref,
                         pieces_ref):
    pieces_ref[...] = jnp.zeros_like(pieces_ref)
    slots = adj_ref.shape[0]

    def body(g, carry):
        base = g * group
        prods = []
        for i in range(group):
            t = base + i
            p = jnp.dot(adj_ref[t], panel_ref[cols_ref[t]], preferred_element_type=jnp.float32)
            prods.append(p)
        for i in range(group):
            slot = rows_ref[base + i]
            pieces_ref[slot] += prods[i]
        return carry

    lax.fori_loop(0, slots // group, body, 0)


def block_product(row_ids, col_ids, dev_tiles, col_panel, row_tiles):
    slots = dev_tiles.shape[0]
    feat_width = col_panel.shape[2]
    group = 16 if slots % 16 == 0 else 1
    smem = pl.BlockSpec(memory_space=pltpu.SMEM)
    vmem = pl.BlockSpec(memory_space=pltpu.VMEM)
    return pl.pallas_call(
        functools.partial(block_product_kernel, group),
        out_shape=jax.ShapeDtypeStruct((row_tiles, TILE, feat_width), jnp.float32),
        in_specs=[smem, smem, vmem, vmem],
        out_specs=vmem,
        cost_estimate=pl.CostEstimate(
            flops=2 * slots * TILE * TILE * feat_width,
            bytes_accessed=slots * TILE * TILE * 2 + row_tiles * TILE * feat_width * 4,
            transcendentals=0,
        ),
    )(row_ids, col_ids, dev_tiles, col_panel)


def shards(features, degrees, adj_tiles, tile_rows, tile_cols, tile_counts):
    col_count = lax.axis_size("col")
    nodes_dev = features.shape[0]
    feat_width = features.shape[1]
    tile_slots = adj_tiles.shape[2]
    row_ids_all = tile_rows.reshape(tile_slots)
    live = jnp.arange(tile_slots, dtype=jnp.int32) < tile_counts.reshape(())
    panel_tiles = lax.axis_size("row") * (nodes_dev // TILE)
    col_ids_all = jnp.where(live, tile_cols.reshape(tile_slots), panel_tiles)
    row_tiles = nodes_dev * col_count // TILE
    norm_scale = jnp.sqrt(KNN / degrees.astype(jnp.float32))[:, None]
    scale = jnp.broadcast_to(norm_scale, features.shape)
    gathered, dev_tiles = row_all_gather(features, scale, adj_tiles.reshape(tile_slots, TILE * TILE))
    per_piece = nodes_dev // TILE
    n_y = col_count // (CORES * Z_RING)
    piece_j = row_ids_all // per_piece
    row_slots = (((piece_j % CORES) * Z_RING + (piece_j // CORES) % Z_RING) * n_y
                 + piece_j // (CORES * Z_RING)) * per_piece + row_ids_all % per_piece
    for repeat in range(STEPS):
        pieces = block_product(row_slots, col_ids_all, dev_tiles, gathered, row_tiles)
        gathered = col_reduce_scatter(
            pieces.reshape(CORES, Z_RING, -1, nodes_dev, feat_width),
            scale, features, repeat == STEPS - 1,
        )
    return gathered.astype(jnp.bfloat16)


def solution(mesh):
    return jax.shard_map(
        shards,
        mesh=mesh,
        in_specs=(
            P(("row", "col"), None),
            P(("row", "col")),
            P("row", "col", None, None),
            P("row", "col", None),
            P("row", "col", None),
            P("row", "col"),
        ),
        out_specs=P(("row", "col"), None),
        check_vma=False,
    )
```

```python
import functools

import jax
import jax.numpy as jnp
from jax import lax
from jax.experimental import pallas as pl
from jax.experimental.pallas import tpu as pltpu
from jax.sharding import PartitionSpec as P

TILE = 64
KNN = 32
STEPS = 2

MESH = pl.DeviceIdType.MESH

ALPHA = 0.1


CORES = 2
Z_RING = 8


def reduce_scatter_kernel(n_z, chunks, last, x_ref, scale_ref, feat_ref, out_ref, ra,
                          recv_cw, recv_ccw, send_cw, send_ccw, fin, y_recv,
                          a_sems, cw_sems, ccw_sems, y_sems, *ag_sems):
    c = lax.axis_index("col")
    row = lax.axis_index("row")
    core = lax.rem(c, CORES)
    z = lax.rem(c // CORES, n_z)
    yh = c // (CORES * n_z)

    def dev(yh_, z_, core_):
        return (row, (yh_ * n_z + z_) * CORES + core_)

    partner = dev(yh, z, 1 - core)
    right = dev(yh, lax.rem(z + 1, n_z), core)
    left = dev(yh, lax.rem(z + n_z - 1, n_z), core)
    y_partner = dev(1 - yh, z, core)

    n_row = lax.axis_size("row")
    barrier = pltpu.get_barrier_semaphore()
    for peer in (partner, right, left, y_partner):
        pl.semaphore_signal(barrier, inc=1, device_id=peer, device_id_type=MESH)
    if not last:
        def greet(k, carry):
            pl.semaphore_signal(barrier, inc=1, device_id=(lax.rem(row + k, n_row), c),
                                device_id_type=MESH)
            return carry

        lax.fori_loop(1, n_row, greet, 0)
    pl.semaphore_wait(barrier, 4 if last else 3 + n_row)

    def rcopy(src, dst, sems, idx, peer):
        return pltpu.make_async_remote_copy(
            src_ref=src, dst_ref=dst, send_sem=sems.at[(0,) + idx], recv_sem=sems.at[(1,) + idx],
            device_id=peer, device_id_type=MESH,
        )

    def first(d):
        return lax.rem(z + (n_z - 1 if d == 0 else 1), n_z)

    def got(d, s):
        return lax.rem(z + ((2 * n_z - s - 2) if d == 0 else (s + 2)), n_z)

    need = [(first(0), 0), (first(1), 1)]
    for s in range(n_z - 1):
        need += [(got(0, s), 0), (got(1, s), 1)]
    copies_a = []
    for k, (g, h) in enumerate(need):
        cp = rcopy(x_ref.at[1 - core, g, h], ra.at[g, h], a_sems, (k,), partner)
        cp.start()
        copies_a.append(cp)

    def ready(d, s):
        copies_a[d if s < 0 else 2 + 2 * s + d].wait_recv()

    size = x_ref.shape[3] // chunks
    recv = (recv_cw, recv_ccw)
    send = (send_cw, send_ccw)
    sems = (cw_sems, ccw_sems)
    to = (right, left)
    sends = list(copies_a)

    def ring_copy(d, s, i):
        part = pl.ds(i * size, size)
        return rcopy(send[d].at[s, part], recv[d].at[s, part], sems[d], (s, i), to[d])

    def y_copy(i):
        part = pl.ds(i * size, size)
        return rcopy(fin.at[1 - yh, part], y_recv.at[part], y_sems, (i,), y_partner)

    for d in range(2):
        ready(d, -1)
        g = first(d)
        send[d][0] = x_ref[core, g, d] + ra[g, d]
        for i in range(chunks):
            cp = ring_copy(d, 0, i)
            cp.start()
            sends.append(cp)
    for s in range(n_z - 1):
        for d in range(2):
            ready(d, s)
        for i in range(chunks):
            part = pl.ds(i * size, size)
            for d in range(2):
                g = got(d, s)
                ring_copy(d, s, i).wait_recv()
                val = recv[d][s, part] + x_ref[core, g, d, part] + ra[g, d, part]
                if s < n_z - 2:
                    send[d][s + 1, part] = val
                    cp = ring_copy(d, s + 1, i)
                    cp.start()
                    sends.append(cp)
                else:
                    fin[d, part] = val
            if s == n_z - 2:
                cp = y_copy(i)
                cp.start()
                sends.append(cp)

    if not last:
        ag_send, ag_recv = ag_sems

        def ag_copy(peer, slot, i):
            part = pl.ds(i * size, size)
            return pltpu.make_async_remote_copy(
                src_ref=out_ref.at[row * chunks + i], dst_ref=out_ref.at[slot * chunks + i],
                send_sem=ag_send.at[peer, i], recv_sem=ag_recv.at[slot, i],
                device_id=(peer, c), device_id_type=MESH,
            )

    for i in range(chunks):
        part = pl.ds(i * size, size)
        y_copy(i).wait_recv()
        own = fin[yh, part] + y_recv[part]
        current = ((1.0 - ALPHA) * scale_ref[i]) * own + ALPHA * feat_ref[i].astype(jnp.float32)
        if last:
            out_ref[part] = current.astype(out_ref.dtype)
        else:
            out_ref[row * chunks + i] = (scale_ref[i] * current).astype(out_ref.dtype)

            def ag_start(k, carry, i=i):
                ag_copy(lax.rem(row + k, n_row), row, i).start()
                return carry

            lax.fori_loop(1, n_row, ag_start, 0)
    if not last:
        out_ref[n_row * chunks] = jnp.zeros(out_ref.shape[1:], out_ref.dtype)

        def ag_finish(k, carry):
            for i in range(chunks):
                ag_copy(lax.rem(row + n_row - k, n_row), lax.rem(row + n_row - k, n_row), i).wait_recv()
                ag_copy(lax.rem(row + k, n_row), row, i).wait_send()
            return carry

        lax.fori_loop(1, n_row, ag_finish, 0)
    for cp in sends:
        cp.wait_send()


RS_CHUNKS = 4


def col_reduce_scatter(pieces, scale, features, last):
    cores, n_z, n_y, nodes_dev, feat_width = pieces.shape
    n_row = lax.axis_size("row")
    chunks = nodes_dev // TILE
    piece = (nodes_dev, feat_width)
    vmem = pl.BlockSpec(memory_space=pltpu.VMEM)
    out_shape = piece if last else (n_row * chunks + 1, TILE, feat_width)
    ag_sems = [] if last else [pltpu.SemaphoreType.DMA((n_row, chunks))] * 2
    return pl.pallas_call(
        functools.partial(reduce_scatter_kernel, n_z, chunks, last),
        out_shape=jax.ShapeDtypeStruct(out_shape, jnp.float32 if last else jnp.bfloat16),
        in_specs=[vmem] * 3,
        out_specs=vmem,
        scratch_shapes=[
            pltpu.VMEM((n_z, n_y) + piece, jnp.float32),
            pltpu.VMEM((n_z - 1,) + piece, jnp.float32),
            pltpu.VMEM((n_z - 1,) + piece, jnp.float32),
            pltpu.VMEM((n_z - 1,) + piece, jnp.float32),
            pltpu.VMEM((n_z - 1,) + piece, jnp.float32),
            pltpu.VMEM((n_y,) + piece, jnp.float32),
            pltpu.VMEM(piece, jnp.float32),
            pltpu.SemaphoreType.DMA((2, 2 * n_z)),
            pltpu.SemaphoreType.DMA((2, n_z - 1, chunks)),
            pltpu.SemaphoreType.DMA((2, n_z - 1, chunks)),
            pltpu.SemaphoreType.DMA((2, chunks)),
        ] + ag_sems,
        compiler_params=pltpu.CompilerParams(collective_id=2 if last else 0, has_side_effects=True),
    )(pieces, scale, features)


def all_gather_kernel(n, feat_ref, scale_ref, adj_ref, out_ref, tiles_ref, src_ref, send_sem,
                      recv_sem):
    me = lax.axis_index("row")
    col = lax.axis_index("col")
    per_piece = src_ref.shape[0]
    src_ref[...] = (scale_ref[...] * feat_ref[...].astype(jnp.float32)).astype(src_ref.dtype)

    barrier = pltpu.get_barrier_semaphore()

    def greet(k, carry):
        peer = lax.rem(me + k, n)
        pl.semaphore_signal(barrier, inc=1, device_id=(peer, col), device_id_type=MESH)
        return carry

    lax.fori_loop(1, n, greet, 0)
    pl.semaphore_wait(barrier, n - 1)

    def copy(peer, slot):
        return pltpu.make_async_remote_copy(
            src_ref=src_ref,
            dst_ref=out_ref.at[pl.ds(slot * per_piece, per_piece)],
            send_sem=send_sem.at[peer],
            recv_sem=recv_sem.at[slot],
            device_id=(peer, col),
            device_id_type=MESH,
        )

    def start(k, carry):
        copy(lax.rem(me + k, n), me).start()
        return carry

    lax.fori_loop(1, n, start, 0)
    out_ref[pl.ds(me * per_piece, per_piece)] = src_ref[...]
    out_ref[n * per_piece] = jnp.zeros(out_ref.shape[1:], out_ref.dtype)

    rows = 16

    def shape_tiles(g, carry):
        at = pl.ds(pl.multiple_of(g * rows, rows), rows)
        tiles_ref[at] = adj_ref[at].reshape((rows,) + tiles_ref.shape[1:])
        return carry

    lax.fori_loop(0, adj_ref.shape[0] // rows, shape_tiles, 0)

    def finish(k, carry):
        sender = lax.rem(me + n - k, n)
        copy(sender, sender).wait_recv()
        copy(lax.rem(me + k, n), me).wait_send()
        return carry

    lax.fori_loop(1, n, finish, 0)


def row_all_gather(features, scale, adj_flat):
    n = lax.axis_size("row")
    nodes_dev, feat_width = features.shape[0] * TILE, features.shape[2]
    per_piece = nodes_dev // TILE
    vmem = pl.BlockSpec(memory_space=pltpu.VMEM)
    return pl.pallas_call(
        functools.partial(all_gather_kernel, n),
        out_shape=(
            jax.ShapeDtypeStruct((n * per_piece + 1, TILE, feat_width), jnp.bfloat16),
            jax.ShapeDtypeStruct((adj_flat.shape[0], TILE, TILE), adj_flat.dtype),
        ),
        in_specs=[vmem, vmem, vmem],
        out_specs=(vmem, vmem),
        scratch_shapes=[
            pltpu.VMEM((per_piece, TILE, feat_width), jnp.bfloat16),
            pltpu.SemaphoreType.DMA((n,)),
            pltpu.SemaphoreType.DMA((n,)),
        ],
        compiler_params=pltpu.CompilerParams(collective_id=1, has_side_effects=True),
    )(features, scale, adj_flat)


def block_product_kernel(group, rows_ref, cols_ref, adj_ref, panel_ref,
                         pieces_ref):
    pieces_ref[...] = jnp.zeros_like(pieces_ref)
    slots = adj_ref.shape[0]

    def body(g, carry):
        base = g * group
        prods = []
        for i in range(group):
            t = base + i
            p = jnp.dot(adj_ref[t], panel_ref[cols_ref[t]], preferred_element_type=jnp.float32)
            prods.append(p)
        for i in range(group):
            slot = rows_ref[base + i]
            pieces_ref[slot] += prods[i]
        return carry

    lax.fori_loop(0, slots // group, body, 0)


def block_product(row_ids, col_ids, dev_tiles, col_panel, row_tiles):
    slots = dev_tiles.shape[0]
    feat_width = col_panel.shape[2]
    group = 16 if slots % 16 == 0 else 1
    smem = pl.BlockSpec(memory_space=pltpu.SMEM)
    vmem = pl.BlockSpec(memory_space=pltpu.VMEM)
    return pl.pallas_call(
        functools.partial(block_product_kernel, group),
        out_shape=jax.ShapeDtypeStruct((row_tiles, TILE, feat_width), jnp.float32),
        in_specs=[smem, smem, vmem, vmem],
        out_specs=vmem,
        cost_estimate=pl.CostEstimate(
            flops=2 * slots * TILE * TILE * feat_width,
            bytes_accessed=slots * TILE * TILE * 2 + row_tiles * TILE * feat_width * 4,
            transcendentals=0,
        ),
    )(row_ids, col_ids, dev_tiles, col_panel)


def shards(features, degrees, adj_tiles, tile_rows, tile_cols, tile_counts):
    col_count = lax.axis_size("col")
    nodes_dev = features.shape[0]
    feat_width = features.shape[1]
    tile_slots = adj_tiles.shape[2]
    row_ids_all = tile_rows.reshape(tile_slots)
    live = jnp.arange(tile_slots, dtype=jnp.int32) < tile_counts.reshape(())
    panel_tiles = lax.axis_size("row") * (nodes_dev // TILE)
    col_ids_all = jnp.where(live, tile_cols.reshape(tile_slots), panel_tiles)
    row_tiles = nodes_dev * col_count // TILE
    norm_scale = jnp.sqrt(KNN / degrees.astype(jnp.float32))[:, None]
    scale = jnp.broadcast_to(norm_scale, features.shape).reshape(-1, TILE, feat_width)
    features = features.reshape(-1, TILE, feat_width)
    gathered, dev_tiles = row_all_gather(features, scale, adj_tiles.reshape(tile_slots, TILE * TILE))
    per_piece = nodes_dev // TILE
    n_y = col_count // (CORES * Z_RING)
    piece_j = row_ids_all // per_piece
    row_slots = (((piece_j % CORES) * Z_RING + (piece_j // CORES) % Z_RING) * n_y
                 + piece_j // (CORES * Z_RING)) * per_piece + row_ids_all % per_piece
    for repeat in range(STEPS):
        pieces = block_product(row_slots, col_ids_all, dev_tiles, gathered, row_tiles)
        gathered = col_reduce_scatter(
            pieces.reshape(CORES, Z_RING, -1, nodes_dev, feat_width),
            scale, features, repeat == STEPS - 1,
        )
    return gathered.astype(jnp.bfloat16)


def solution(mesh):
    return jax.shard_map(
        shards,
        mesh=mesh,
        in_specs=(
            P(("row", "col"), None),
            P(("row", "col")),
            P("row", "col", None, None),
            P("row", "col", None),
            P("row", "col", None),
            P("row", "col"),
        ),
        out_specs=P(("row", "col"), None),
        check_vma=False,
    )
```

```python
import functools

import jax
import jax.numpy as jnp
from jax import lax
from jax.experimental import pallas as pl
from jax.experimental.pallas import tpu as pltpu
from jax.sharding import PartitionSpec as P

TILE = 64
KNN = 32
STEPS = 2

MESH = pl.DeviceIdType.MESH

ALPHA = 0.1


CORES = 2
Z_RING = 8


def reduce_scatter_kernel(n_z, chunks, last, x_ref, scale_ref, feat_ref, out_ref, ra,
                          recv_cw, recv_ccw, send_cw, send_ccw, fin, y_recv,
                          a_sems, cw_sems, ccw_sems, y_sems, *ag_sems):
    c = lax.axis_index("col")
    row = lax.axis_index("row")
    core = lax.rem(c, CORES)
    z = lax.rem(c // CORES, n_z)
    yh = c // (CORES * n_z)

    def dev(yh_, z_, core_):
        return (row, (yh_ * n_z + z_) * CORES + core_)

    partner = dev(yh, z, 1 - core)
    right = dev(yh, lax.rem(z + 1, n_z), core)
    left = dev(yh, lax.rem(z + n_z - 1, n_z), core)
    y_partner = dev(1 - yh, z, core)

    n_row = lax.axis_size("row")
    barrier = pltpu.get_barrier_semaphore()
    for peer in (partner, right, left, y_partner):
        pl.semaphore_signal(barrier, inc=1, device_id=peer, device_id_type=MESH)
    if not last:
        def greet(k, carry):
            pl.semaphore_signal(barrier, inc=1, device_id=(lax.rem(row + k, n_row), c),
                                device_id_type=MESH)
            return carry

        lax.fori_loop(1, n_row, greet, 0)
    pl.semaphore_wait(barrier, 4 if last else 3 + n_row)

    def rcopy(src, dst, sems, idx, peer):
        return pltpu.make_async_remote_copy(
            src_ref=src, dst_ref=dst, send_sem=sems.at[(0,) + idx], recv_sem=sems.at[(1,) + idx],
            device_id=peer, device_id_type=MESH,
        )

    def first(d):
        return lax.rem(z + (n_z - 1 if d == 0 else 1), n_z)

    def got(d, s):
        return lax.rem(z + ((2 * n_z - s - 2) if d == 0 else (s + 2)), n_z)

    need = [(first(0), 0), (first(1), 1)]
    for s in range(n_z - 1):
        need += [(got(0, s), 0), (got(1, s), 1)]
    copies_a = []
    for k, (g, h) in enumerate(need):
        cp = rcopy(x_ref.at[1 - core, g, h], ra.at[g, h], a_sems, (k,), partner)
        cp.start()
        copies_a.append(cp)

    def ready(d, s):
        copies_a[d if s < 0 else 2 + 2 * s + d].wait_recv()

    size = x_ref.shape[3] // chunks
    recv = (recv_cw, recv_ccw)
    send = (send_cw, send_ccw)
    sems = (cw_sems, ccw_sems)
    to = (right, left)
    sends = list(copies_a)

    def ring_copy(d, s, i):
        part = pl.ds(i * size, size)
        return rcopy(send[d].at[s, part], recv[d].at[s, part], sems[d], (s, i), to[d])

    def y_copy(i):
        part = pl.ds(i * size, size)
        return rcopy(fin.at[1 - yh, part], y_recv.at[part], y_sems, (i,), y_partner)

    for d in range(2):
        ready(d, -1)
        g = first(d)
        send[d][0] = x_ref[core, g, d] + ra[g, d]
        for i in range(chunks):
            cp = ring_copy(d, 0, i)
            cp.start()
            sends.append(cp)
    for s in range(n_z - 1):
        for d in range(2):
            ready(d, s)
        for i in range(chunks):
            part = pl.ds(i * size, size)
            for d in range(2):
                g = got(d, s)
                ring_copy(d, s, i).wait_recv()
                val = recv[d][s, part] + x_ref[core, g, d, part] + ra[g, d, part]
                if s < n_z - 2:
                    send[d][s + 1, part] = val
                    cp = ring_copy(d, s + 1, i)
                    cp.start()
                    sends.append(cp)
                else:
                    fin[d, part] = val
            if s == n_z - 2:
                cp = y_copy(i)
                cp.start()
                sends.append(cp)

    if not last:
        ag_send, ag_recv = ag_sems

        def ag_copy(peer, slot, i):
            part = pl.ds(i * size, size)
            return pltpu.make_async_remote_copy(
                src_ref=out_ref.at[row * chunks + i], dst_ref=out_ref.at[slot * chunks + i],
                send_sem=ag_send.at[peer, i], recv_sem=ag_recv.at[slot, i],
                device_id=(peer, c), device_id_type=MESH,
            )

    for i in range(chunks):
        part = pl.ds(i * size, size)
        y_copy(i).wait_recv()
        own = fin[yh, part] + y_recv[part]
        current = ((1.0 - ALPHA) * scale_ref[i]) * own + ALPHA * feat_ref[i].astype(jnp.float32)
        if last:
            out_ref[part] = current.astype(out_ref.dtype)
        else:
            out_ref[row * chunks + i] = (scale_ref[i] * current).astype(out_ref.dtype)

            def ag_start(k, carry, i=i):
                ag_copy(lax.rem(row + k, n_row), row, i).start()
                return carry

            lax.fori_loop(1, n_row, ag_start, 0)
    if not last:
        out_ref[n_row * chunks] = jnp.zeros(out_ref.shape[1:], out_ref.dtype)

        def ag_finish(k, carry):
            for i in range(chunks):
                ag_copy(lax.rem(row + n_row - k, n_row), lax.rem(row + n_row - k, n_row), i).wait_recv()
                ag_copy(lax.rem(row + k, n_row), row, i).wait_send()
            return carry

        lax.fori_loop(1, n_row, ag_finish, 0)
    for cp in sends:
        cp.wait_send()


RS_CHUNKS = 4


def col_reduce_scatter(pieces, scale, features, last):
    cores, n_z, n_y, nodes_dev, feat_width = pieces.shape
    n_row = lax.axis_size("row")
    chunks = nodes_dev // TILE
    piece = (nodes_dev, feat_width)
    vmem = pl.BlockSpec(memory_space=pltpu.VMEM)
    out_shape = piece if last else (n_row * chunks + 1, TILE, feat_width)
    ag_sems = [] if last else [pltpu.SemaphoreType.DMA((n_row, chunks))] * 2
    return pl.pallas_call(
        functools.partial(reduce_scatter_kernel, n_z, chunks, last),
        out_shape=jax.ShapeDtypeStruct(out_shape, jnp.float32 if last else jnp.bfloat16),
        in_specs=[vmem] * 3,
        out_specs=vmem,
        scratch_shapes=[
            pltpu.VMEM((n_z, n_y) + piece, jnp.float32),
            pltpu.VMEM((n_z - 1,) + piece, jnp.float32),
            pltpu.VMEM((n_z - 1,) + piece, jnp.float32),
            pltpu.VMEM((n_z - 1,) + piece, jnp.float32),
            pltpu.VMEM((n_z - 1,) + piece, jnp.float32),
            pltpu.VMEM((n_y,) + piece, jnp.float32),
            pltpu.VMEM(piece, jnp.float32),
            pltpu.SemaphoreType.DMA((2, 2 * n_z)),
            pltpu.SemaphoreType.DMA((2, n_z - 1, chunks)),
            pltpu.SemaphoreType.DMA((2, n_z - 1, chunks)),
            pltpu.SemaphoreType.DMA((2, chunks)),
        ] + ag_sems,
        compiler_params=pltpu.CompilerParams(collective_id=2 if last else 0, has_side_effects=True),
    )(pieces, scale, features)


def all_gather_kernel(n, feat_ref, scale_ref, adj_ref, out_ref, tiles_ref, src_ref, send_sem,
                      recv_sem):
    me = lax.axis_index("row")
    col = lax.axis_index("col")
    per_piece = src_ref.shape[0]
    src_ref[...] = (scale_ref[...] * feat_ref[...].astype(jnp.float32)).astype(src_ref.dtype)

    barrier = pltpu.get_barrier_semaphore()

    def greet(k, carry):
        peer = lax.rem(me + k, n)
        pl.semaphore_signal(barrier, inc=1, device_id=(peer, col), device_id_type=MESH)
        return carry

    lax.fori_loop(1, n, greet, 0)
    pl.semaphore_wait(barrier, n - 1)

    def copy(peer, slot):
        return pltpu.make_async_remote_copy(
            src_ref=src_ref,
            dst_ref=out_ref.at[pl.ds(slot * per_piece, per_piece)],
            send_sem=send_sem.at[peer],
            recv_sem=recv_sem.at[slot],
            device_id=(peer, col),
            device_id_type=MESH,
        )

    def start(k, carry):
        copy(lax.rem(me + k, n), me).start()
        return carry

    lax.fori_loop(1, n, start, 0)
    out_ref[pl.ds(me * per_piece, per_piece)] = src_ref[...]
    out_ref[n * per_piece] = jnp.zeros(out_ref.shape[1:], out_ref.dtype)

    rows = 32

    def shape_tiles(g, carry):
        at = pl.ds(pl.multiple_of(g * rows, rows), rows)
        tiles_ref[at] = adj_ref[at].reshape((rows,) + tiles_ref.shape[1:])
        return carry

    lax.fori_loop(0, adj_ref.shape[0] // rows, shape_tiles, 0)

    def finish(k, carry):
        sender = lax.rem(me + n - k, n)
        copy(sender, sender).wait_recv()
        copy(lax.rem(me + k, n), me).wait_send()
        return carry

    lax.fori_loop(1, n, finish, 0)


def row_all_gather(features, scale, adj_flat):
    n = lax.axis_size("row")
    nodes_dev, feat_width = features.shape[0] * TILE, features.shape[2]
    per_piece = nodes_dev // TILE
    vmem = pl.BlockSpec(memory_space=pltpu.VMEM)
    return pl.pallas_call(
        functools.partial(all_gather_kernel, n),
        out_shape=(
            jax.ShapeDtypeStruct((n * per_piece + 1, TILE, feat_width), jnp.bfloat16),
            jax.ShapeDtypeStruct((adj_flat.shape[0], TILE, TILE), adj_flat.dtype),
        ),
        in_specs=[vmem, vmem, vmem],
        out_specs=(vmem, vmem),
        scratch_shapes=[
            pltpu.VMEM((per_piece, TILE, feat_width), jnp.bfloat16),
            pltpu.SemaphoreType.DMA((n,)),
            pltpu.SemaphoreType.DMA((n,)),
        ],
        compiler_params=pltpu.CompilerParams(collective_id=1, has_side_effects=True),
    )(features, scale, adj_flat)


def block_product_kernel(group, rows_ref, cols_ref, adj_ref, panel_ref,
                         pieces_ref):
    pieces_ref[...] = jnp.zeros_like(pieces_ref)
    slots = adj_ref.shape[0]

    def body(g, carry):
        base = g * group
        prods = []
        for i in range(group):
            t = base + i
            p = jnp.dot(adj_ref[t], panel_ref[cols_ref[t]], preferred_element_type=jnp.float32)
            prods.append(p)
        for i in range(group):
            slot = rows_ref[base + i]
            pieces_ref[slot] += prods[i]
        return carry

    lax.fori_loop(0, slots // group, body, 0)


def block_product(row_ids, col_ids, dev_tiles, col_panel, row_tiles):
    slots = dev_tiles.shape[0]
    feat_width = col_panel.shape[2]
    group = 16 if slots % 16 == 0 else 1
    smem = pl.BlockSpec(memory_space=pltpu.SMEM)
    vmem = pl.BlockSpec(memory_space=pltpu.VMEM)
    return pl.pallas_call(
        functools.partial(block_product_kernel, group),
        out_shape=jax.ShapeDtypeStruct((row_tiles, TILE, feat_width), jnp.float32),
        in_specs=[smem, smem, vmem, vmem],
        out_specs=vmem,
        cost_estimate=pl.CostEstimate(
            flops=2 * slots * TILE * TILE * feat_width,
            bytes_accessed=slots * TILE * TILE * 2 + row_tiles * TILE * feat_width * 4,
            transcendentals=0,
        ),
    )(row_ids, col_ids, dev_tiles, col_panel)


def shards(features, degrees, adj_tiles, tile_rows, tile_cols, tile_counts):
    col_count = lax.axis_size("col")
    nodes_dev = features.shape[0]
    feat_width = features.shape[1]
    tile_slots = adj_tiles.shape[2]
    row_ids_all = tile_rows.reshape(tile_slots)
    live = jnp.arange(tile_slots, dtype=jnp.int32) < tile_counts.reshape(())
    panel_tiles = lax.axis_size("row") * (nodes_dev // TILE)
    col_ids_all = jnp.where(live, tile_cols.reshape(tile_slots), panel_tiles)
    row_tiles = nodes_dev * col_count // TILE
    norm_scale = jnp.sqrt(KNN / degrees.astype(jnp.float32))[:, None]
    scale = jnp.broadcast_to(norm_scale, features.shape).reshape(-1, TILE, feat_width)
    features = features.reshape(-1, TILE, feat_width)
    gathered, dev_tiles = row_all_gather(features, scale, adj_tiles.reshape(tile_slots, TILE * TILE))
    per_piece = nodes_dev // TILE
    n_y = col_count // (CORES * Z_RING)
    piece_j = row_ids_all // per_piece
    row_slots = (((piece_j % CORES) * Z_RING + (piece_j // CORES) % Z_RING) * n_y
                 + piece_j // (CORES * Z_RING)) * per_piece + row_ids_all % per_piece
    for repeat in range(STEPS):
        pieces = block_product(row_slots, col_ids_all, dev_tiles, gathered, row_tiles)
        gathered = col_reduce_scatter(
            pieces.reshape(CORES, Z_RING, -1, nodes_dev, feat_width),
            scale, features, repeat == STEPS - 1,
        )
    return gathered.astype(jnp.bfloat16)


def solution(mesh):
    return jax.shard_map(
        shards,
        mesh=mesh,
        in_specs=(
            P(("row", "col"), None),
            P(("row", "col")),
            P("row", "col", None, None),
            P("row", "col", None),
            P("row", "col", None),
            P("row", "col"),
        ),
        out_specs=P(("row", "col"), None),
        check_vma=False,
    )
```

```python
import functools

import jax
import jax.numpy as jnp
from jax import lax
from jax.experimental import pallas as pl
from jax.experimental.pallas import tpu as pltpu
from jax.sharding import PartitionSpec as P

TILE = 64
KNN = 32
STEPS = 2

MESH = pl.DeviceIdType.MESH

ALPHA = 0.1


CORES = 2
Z_RING = 8


def reduce_scatter_kernel(n_z, chunks, last, x_ref, scale_ref, feat_ref, out_ref, ra,
                          recv_cw, recv_ccw, send_cw, send_ccw, fin, y_recv,
                          a_sems, cw_sems, ccw_sems, y_sems, *ag_sems):
    c = lax.axis_index("col")
    row = lax.axis_index("row")
    core = lax.rem(c, CORES)
    z = lax.rem(c // CORES, n_z)
    yh = c // (CORES * n_z)

    def dev(yh_, z_, core_):
        return (row, (yh_ * n_z + z_) * CORES + core_)

    partner = dev(yh, z, 1 - core)
    right = dev(yh, lax.rem(z + 1, n_z), core)
    left = dev(yh, lax.rem(z + n_z - 1, n_z), core)
    y_partner = dev(1 - yh, z, core)

    n_row = lax.axis_size("row")
    barrier = pltpu.get_barrier_semaphore()
    for peer in (partner, right, left, y_partner):
        pl.semaphore_signal(barrier, inc=1, device_id=peer, device_id_type=MESH)
    if not last:
        def greet(k, carry):
            pl.semaphore_signal(barrier, inc=1, device_id=(lax.rem(row + k, n_row), c),
                                device_id_type=MESH)
            return carry

        lax.fori_loop(1, n_row, greet, 0)
    pl.semaphore_wait(barrier, 4 if last else 3 + n_row)

    def rcopy(src, dst, sems, idx, peer):
        return pltpu.make_async_remote_copy(
            src_ref=src, dst_ref=dst, send_sem=sems.at[(0,) + idx], recv_sem=sems.at[(1,) + idx],
            device_id=peer, device_id_type=MESH,
        )

    def first(d):
        return lax.rem(z + (n_z - 1 if d == 0 else 1), n_z)

    def got(d, s):
        return lax.rem(z + ((2 * n_z - s - 2) if d == 0 else (s + 2)), n_z)

    need = [(first(0), 0), (first(1), 1)]
    for s in range(n_z - 1):
        need += [(got(0, s), 0), (got(1, s), 1)]
    copies_a = []
    for k, (g, h) in enumerate(need):
        cp = rcopy(x_ref.at[1 - core, g, h], ra.at[g, h], a_sems, (k,), partner)
        cp.start()
        copies_a.append(cp)

    def ready(d, s):
        copies_a[d if s < 0 else 2 + 2 * s + d].wait_recv()

    size = x_ref.shape[3] // chunks
    recv = (recv_cw, recv_ccw)
    send = (send_cw, send_ccw)
    sems = (cw_sems, ccw_sems)
    to = (right, left)
    sends = list(copies_a)

    def ring_copy(d, s, i):
        part = pl.ds(i * size, size)
        return rcopy(send[d].at[s, part], recv[d].at[s, part], sems[d], (s, i), to[d])

    def y_copy(i):
        part = pl.ds(i * size, size)
        return rcopy(fin.at[1 - yh, part], y_recv.at[part], y_sems, (i,), y_partner)

    for d in range(2):
        ready(d, -1)
        g = first(d)
        send[d][0] = x_ref[core, g, d] + ra[g, d]
        for i in range(chunks):
            cp = ring_copy(d, 0, i)
            cp.start()
            sends.append(cp)
    for s in range(n_z - 1):
        for d in range(2):
            ready(d, s)
        for i in range(chunks):
            part = pl.ds(i * size, size)
            for d in range(2):
                g = got(d, s)
                ring_copy(d, s, i).wait_recv()
                val = recv[d][s, part] + x_ref[core, g, d, part] + ra[g, d, part]
                if s < n_z - 2:
                    send[d][s + 1, part] = val
                    cp = ring_copy(d, s + 1, i)
                    cp.start()
                    sends.append(cp)
                else:
                    fin[d, part] = val
            if s == n_z - 2:
                cp = y_copy(i)
                cp.start()
                sends.append(cp)

    if not last:
        ag_send, ag_recv = ag_sems

        def ag_copy(peer, slot, i):
            part = pl.ds(i * size, size)
            return pltpu.make_async_remote_copy(
                src_ref=out_ref.at[row * chunks + i], dst_ref=out_ref.at[slot * chunks + i],
                send_sem=ag_send.at[peer, i], recv_sem=ag_recv.at[slot, i],
                device_id=(peer, c), device_id_type=MESH,
            )

    for i in range(chunks):
        part = pl.ds(i * size, size)
        y_copy(i).wait_recv()
        own = fin[yh, part] + y_recv[part]
        current = ((1.0 - ALPHA) * scale_ref[i]) * own + ALPHA * feat_ref[i].astype(jnp.float32)
        if last:
            out_ref[part] = current.astype(out_ref.dtype)
        else:
            out_ref[row * chunks + i] = (scale_ref[i] * current).astype(out_ref.dtype)

            def ag_start(k, carry, i=i):
                ag_copy(lax.rem(row + k, n_row), row, i).start()
                return carry

            lax.fori_loop(1, n_row, ag_start, 0)
    if not last:
        out_ref[n_row * chunks] = jnp.zeros(out_ref.shape[1:], out_ref.dtype)

        def ag_finish(k, carry):
            for i in range(chunks):
                ag_copy(lax.rem(row + n_row - k, n_row), lax.rem(row + n_row - k, n_row), i).wait_recv()
                ag_copy(lax.rem(row + k, n_row), row, i).wait_send()
            return carry

        lax.fori_loop(1, n_row, ag_finish, 0)
    for cp in sends:
        cp.wait_send()


RS_CHUNKS = 4


def col_reduce_scatter(pieces, scale, features, last):
    cores, n_z, n_y, nodes_dev, feat_width = pieces.shape
    n_row = lax.axis_size("row")
    chunks = nodes_dev // TILE
    piece = (nodes_dev, feat_width)
    vmem = pl.BlockSpec(memory_space=pltpu.VMEM)
    out_shape = piece if last else (n_row * chunks + 1, TILE, feat_width)
    ag_sems = [] if last else [pltpu.SemaphoreType.DMA((n_row, chunks))] * 2
    return pl.pallas_call(
        functools.partial(reduce_scatter_kernel, n_z, chunks, last),
        out_shape=jax.ShapeDtypeStruct(out_shape, jnp.float32 if last else jnp.bfloat16),
        in_specs=[vmem] * 3,
        out_specs=vmem,
        scratch_shapes=[
            pltpu.VMEM((n_z, n_y) + piece, jnp.float32),
            pltpu.VMEM((n_z - 1,) + piece, jnp.float32),
            pltpu.VMEM((n_z - 1,) + piece, jnp.float32),
            pltpu.VMEM((n_z - 1,) + piece, jnp.float32),
            pltpu.VMEM((n_z - 1,) + piece, jnp.float32),
            pltpu.VMEM((n_y,) + piece, jnp.float32),
            pltpu.VMEM(piece, jnp.float32),
            pltpu.SemaphoreType.DMA((2, 2 * n_z)),
            pltpu.SemaphoreType.DMA((2, n_z - 1, chunks)),
            pltpu.SemaphoreType.DMA((2, n_z - 1, chunks)),
            pltpu.SemaphoreType.DMA((2, chunks)),
        ] + ag_sems,
        compiler_params=pltpu.CompilerParams(collective_id=2 if last else 0, has_side_effects=True),
    )(pieces, scale, features)


def all_gather_kernel(n, feat_ref, scale_ref, adj_ref, out_ref, tiles_ref, src_ref, send_sem,
                      recv_sem):
    me = lax.axis_index("row")
    col = lax.axis_index("col")
    per_piece = src_ref.shape[0]
    src_ref[...] = (scale_ref[...] * feat_ref[...].astype(jnp.float32)).astype(src_ref.dtype)

    barrier = pltpu.get_barrier_semaphore()

    def greet(k, carry):
        peer = lax.rem(me + k, n)
        pl.semaphore_signal(barrier, inc=1, device_id=(peer, col), device_id_type=MESH)
        return carry

    lax.fori_loop(1, n, greet, 0)
    pl.semaphore_wait(barrier, n - 1)

    def copy(peer, slot):
        return pltpu.make_async_remote_copy(
            src_ref=src_ref,
            dst_ref=out_ref.at[pl.ds(slot * per_piece, per_piece)],
            send_sem=send_sem.at[peer],
            recv_sem=recv_sem.at[slot],
            device_id=(peer, col),
            device_id_type=MESH,
        )

    def start(k, carry):
        copy(lax.rem(me + k, n), me).start()
        return carry

    lax.fori_loop(1, n, start, 0)
    out_ref[pl.ds(me * per_piece, per_piece)] = src_ref[...]
    out_ref[n * per_piece] = jnp.zeros(out_ref.shape[1:], out_ref.dtype)

    rows = 64

    def shape_tiles(g, carry):
        at = pl.ds(pl.multiple_of(g * rows, rows), rows)
        tiles_ref[at] = adj_ref[at].reshape((rows,) + tiles_ref.shape[1:])
        return carry

    lax.fori_loop(0, adj_ref.shape[0] // rows, shape_tiles, 0)

    def finish(k, carry):
        sender = lax.rem(me + n - k, n)
        copy(sender, sender).wait_recv()
        copy(lax.rem(me + k, n), me).wait_send()
        return carry

    lax.fori_loop(1, n, finish, 0)


def row_all_gather(features, scale, adj_flat):
    n = lax.axis_size("row")
    nodes_dev, feat_width = features.shape[0] * TILE, features.shape[2]
    per_piece = nodes_dev // TILE
    vmem = pl.BlockSpec(memory_space=pltpu.VMEM)
    return pl.pallas_call(
        functools.partial(all_gather_kernel, n),
        out_shape=(
            jax.ShapeDtypeStruct((n * per_piece + 1, TILE, feat_width), jnp.bfloat16),
            jax.ShapeDtypeStruct((adj_flat.shape[0], TILE, TILE), adj_flat.dtype),
        ),
        in_specs=[vmem, vmem, vmem],
        out_specs=(vmem, vmem),
        scratch_shapes=[
            pltpu.VMEM((per_piece, TILE, feat_width), jnp.bfloat16),
            pltpu.SemaphoreType.DMA((n,)),
            pltpu.SemaphoreType.DMA((n,)),
        ],
        compiler_params=pltpu.CompilerParams(collective_id=1, has_side_effects=True),
    )(features, scale, adj_flat)


def block_product_kernel(group, rows_ref, cols_ref, adj_ref, panel_ref,
                         pieces_ref):
    pieces_ref[...] = jnp.zeros_like(pieces_ref)
    slots = adj_ref.shape[0]

    def body(g, carry):
        base = g * group
        prods = []
        for i in range(group):
            t = base + i
            p = jnp.dot(adj_ref[t], panel_ref[cols_ref[t]], preferred_element_type=jnp.float32)
            prods.append(p)
        for i in range(group):
            slot = rows_ref[base + i]
            pieces_ref[slot] += prods[i]
        return carry

    lax.fori_loop(0, slots // group, body, 0)


def block_product(row_ids, col_ids, dev_tiles, col_panel, row_tiles):
    slots = dev_tiles.shape[0]
    feat_width = col_panel.shape[2]
    group = 16 if slots % 16 == 0 else 1
    smem = pl.BlockSpec(memory_space=pltpu.SMEM)
    vmem = pl.BlockSpec(memory_space=pltpu.VMEM)
    return pl.pallas_call(
        functools.partial(block_product_kernel, group),
        out_shape=jax.ShapeDtypeStruct((row_tiles, TILE, feat_width), jnp.float32),
        in_specs=[smem, smem, vmem, vmem],
        out_specs=vmem,
        cost_estimate=pl.CostEstimate(
            flops=2 * slots * TILE * TILE * feat_width,
            bytes_accessed=slots * TILE * TILE * 2 + row_tiles * TILE * feat_width * 4,
            transcendentals=0,
        ),
    )(row_ids, col_ids, dev_tiles, col_panel)


def shards(features, degrees, adj_tiles, tile_rows, tile_cols, tile_counts):
    col_count = lax.axis_size("col")
    nodes_dev = features.shape[0]
    feat_width = features.shape[1]
    tile_slots = adj_tiles.shape[2]
    row_ids_all = tile_rows.reshape(tile_slots)
    live = jnp.arange(tile_slots, dtype=jnp.int32) < tile_counts.reshape(())
    panel_tiles = lax.axis_size("row") * (nodes_dev // TILE)
    col_ids_all = jnp.where(live, tile_cols.reshape(tile_slots), panel_tiles)
    row_tiles = nodes_dev * col_count // TILE
    norm_scale = jnp.sqrt(KNN / degrees.astype(jnp.float32))[:, None]
    scale = jnp.broadcast_to(norm_scale, features.shape).reshape(-1, TILE, feat_width)
    features = features.reshape(-1, TILE, feat_width)
    gathered, dev_tiles = row_all_gather(features, scale, adj_tiles.reshape(tile_slots, TILE * TILE))
    per_piece = nodes_dev // TILE
    n_y = col_count // (CORES * Z_RING)
    piece_j = row_ids_all // per_piece
    row_slots = (((piece_j % CORES) * Z_RING + (piece_j // CORES) % Z_RING) * n_y
                 + piece_j // (CORES * Z_RING)) * per_piece + row_ids_all % per_piece
    for repeat in range(STEPS):
        pieces = block_product(row_slots, col_ids_all, dev_tiles, gathered, row_tiles)
        gathered = col_reduce_scatter(
            pieces.reshape(CORES, Z_RING, -1, nodes_dev, feat_width),
            scale, features, repeat == STEPS - 1,
        )
    return gathered.astype(jnp.bfloat16)


def solution(mesh):
    return jax.shard_map(
        shards,
        mesh=mesh,
        in_specs=(
            P(("row", "col"), None),
            P(("row", "col")),
            P("row", "col", None, None),
            P("row", "col", None),
            P("row", "col", None),
            P("row", "col"),
        ),
        out_specs=P(("row", "col"), None),
        check_vma=False,
    )
```

```python
import functools

import jax
import jax.numpy as jnp
from jax import lax
from jax.experimental import pallas as pl
from jax.experimental.pallas import tpu as pltpu
from jax.sharding import PartitionSpec as P

TILE = 64
KNN = 32
STEPS = 2

MESH = pl.DeviceIdType.MESH

ALPHA = 0.1


CORES = 2
Z_RING = 8


def reduce_scatter_kernel(n_z, chunks, last, x_ref, scale_ref, feat_ref, out_ref, ra,
                          recv_cw, recv_ccw, send_cw, send_ccw, fin, y_recv,
                          a_sems, cw_sems, ccw_sems, y_sems, *ag_sems):
    c = lax.axis_index("col")
    row = lax.axis_index("row")
    core = lax.rem(c, CORES)
    z = lax.rem(c // CORES, n_z)
    yh = c // (CORES * n_z)

    def dev(yh_, z_, core_):
        return (row, (yh_ * n_z + z_) * CORES + core_)

    partner = dev(yh, z, 1 - core)
    right = dev(yh, lax.rem(z + 1, n_z), core)
    left = dev(yh, lax.rem(z + n_z - 1, n_z), core)
    y_partner = dev(1 - yh, z, core)

    n_row = lax.axis_size("row")
    barrier = pltpu.get_barrier_semaphore()
    for peer in (partner, right, left, y_partner):
        pl.semaphore_signal(barrier, inc=1, device_id=peer, device_id_type=MESH)
    if not last:
        def greet(k, carry):
            pl.semaphore_signal(barrier, inc=1, device_id=(lax.rem(row + k, n_row), c),
                                device_id_type=MESH)
            return carry

        lax.fori_loop(1, n_row, greet, 0)
    pl.semaphore_wait(barrier, 4 if last else 3 + n_row)

    def rcopy(src, dst, sems, idx, peer):
        return pltpu.make_async_remote_copy(
            src_ref=src, dst_ref=dst, send_sem=sems.at[(0,) + idx], recv_sem=sems.at[(1,) + idx],
            device_id=peer, device_id_type=MESH,
        )

    def first(d):
        return lax.rem(z + (n_z - 1 if d == 0 else 1), n_z)

    def got(d, s):
        return lax.rem(z + ((2 * n_z - s - 2) if d == 0 else (s + 2)), n_z)

    need = [(first(0), 0), (first(1), 1)]
    for s in range(n_z - 1):
        need += [(got(0, s), 0), (got(1, s), 1)]
    copies_a = []
    for k, (g, h) in enumerate(need):
        cp = rcopy(x_ref.at[1 - core, g, h], ra.at[g, h], a_sems, (k,), partner)
        cp.start()
        copies_a.append(cp)

    def ready(d, s):
        copies_a[d if s < 0 else 2 + 2 * s + d].wait_recv()

    size = x_ref.shape[3] // chunks
    recv = (recv_cw, recv_ccw)
    send = (send_cw, send_ccw)
    sems = (cw_sems, ccw_sems)
    to = (right, left)
    sends = list(copies_a)

    def ring_copy(d, s, i):
        part = pl.ds(i * size, size)
        return rcopy(send[d].at[s, part], recv[d].at[s, part], sems[d], (s, i), to[d])

    def y_copy(i):
        part = pl.ds(i * size, size)
        return rcopy(fin.at[1 - yh, part], y_recv.at[part], y_sems, (i,), y_partner)

    for d in range(2):
        ready(d, -1)
        g = first(d)
        send[d][0] = x_ref[core, g, d] + ra[g, d]
        for i in range(chunks):
            cp = ring_copy(d, 0, i)
            cp.start()
            sends.append(cp)
    for s in range(n_z - 1):
        for d in range(2):
            ready(d, s)
        for i in range(chunks):
            part = pl.ds(i * size, size)
            for d in range(2):
                g = got(d, s)
                ring_copy(d, s, i).wait_recv()
                val = recv[d][s, part] + x_ref[core, g, d, part] + ra[g, d, part]
                if s < n_z - 2:
                    send[d][s + 1, part] = val
                    cp = ring_copy(d, s + 1, i)
                    cp.start()
                    sends.append(cp)
                else:
                    fin[d, part] = val
            if s == n_z - 2:
                cp = y_copy(i)
                cp.start()
                sends.append(cp)

    if not last:
        ag_send, ag_recv = ag_sems

        def ag_copy(peer, slot, i):
            part = pl.ds(i * size, size)
            return pltpu.make_async_remote_copy(
                src_ref=out_ref.at[row * chunks + i], dst_ref=out_ref.at[slot * chunks + i],
                send_sem=ag_send.at[peer, i], recv_sem=ag_recv.at[slot, i],
                device_id=(peer, c), device_id_type=MESH,
            )

    for i in range(chunks):
        part = pl.ds(i * size, size)
        y_copy(i).wait_recv()
        own = fin[yh, part] + y_recv[part]
        current = ((1.0 - ALPHA) * scale_ref[i]) * own + ALPHA * feat_ref[i].astype(jnp.float32)
        if last:
            out_ref[part] = current.astype(out_ref.dtype)
        else:
            out_ref[row * chunks + i] = (scale_ref[i] * current).astype(out_ref.dtype)

            def ag_start(k, carry, i=i):
                ag_copy(lax.rem(row + k, n_row), row, i).start()
                return carry

            lax.fori_loop(1, n_row, ag_start, 0)
    if not last:
        out_ref[n_row * chunks] = jnp.zeros(out_ref.shape[1:], out_ref.dtype)

        def ag_finish(k, carry):
            for i in range(chunks):
                ag_copy(lax.rem(row + n_row - k, n_row), lax.rem(row + n_row - k, n_row), i).wait_recv()
                ag_copy(lax.rem(row + k, n_row), row, i).wait_send()
            return carry

        lax.fori_loop(1, n_row, ag_finish, 0)
    for cp in sends:
        cp.wait_send()


RS_CHUNKS = 4


def col_reduce_scatter(pieces, scale, features, last):
    cores, n_z, n_y, nodes_dev, feat_width = pieces.shape
    n_row = lax.axis_size("row")
    chunks = nodes_dev // TILE
    piece = (nodes_dev, feat_width)
    vmem = pl.BlockSpec(memory_space=pltpu.VMEM)
    out_shape = piece if last else (n_row * chunks + 1, TILE, feat_width)
    ag_sems = [] if last else [pltpu.SemaphoreType.DMA((n_row, chunks))] * 2
    return pl.pallas_call(
        functools.partial(reduce_scatter_kernel, n_z, chunks, last),
        out_shape=jax.ShapeDtypeStruct(out_shape, jnp.float32 if last else jnp.bfloat16),
        in_specs=[vmem] * 3,
        out_specs=vmem,
        scratch_shapes=[
            pltpu.VMEM((n_z, n_y) + piece, jnp.float32),
            pltpu.VMEM((n_z - 1,) + piece, jnp.float32),
            pltpu.VMEM((n_z - 1,) + piece, jnp.float32),
            pltpu.VMEM((n_z - 1,) + piece, jnp.float32),
            pltpu.VMEM((n_z - 1,) + piece, jnp.float32),
            pltpu.VMEM((n_y,) + piece, jnp.float32),
            pltpu.VMEM(piece, jnp.float32),
            pltpu.SemaphoreType.DMA((2, 2 * n_z)),
            pltpu.SemaphoreType.DMA((2, n_z - 1, chunks)),
            pltpu.SemaphoreType.DMA((2, n_z - 1, chunks)),
            pltpu.SemaphoreType.DMA((2, chunks)),
        ] + ag_sems,
        compiler_params=pltpu.CompilerParams(collective_id=2 if last else 0, has_side_effects=True),
    )(pieces, scale, features)


def all_gather_kernel(n, feat_ref, scale_ref, adj_ref, out_ref, tiles_ref, src_ref, send_sem,
                      recv_sem):
    me = lax.axis_index("row")
    col = lax.axis_index("col")
    per_piece = src_ref.shape[0]
    src_ref[...] = (scale_ref[...] * feat_ref[...].astype(jnp.float32)).astype(src_ref.dtype)

    barrier = pltpu.get_barrier_semaphore()

    def greet(k, carry):
        peer = lax.rem(me + k, n)
        pl.semaphore_signal(barrier, inc=1, device_id=(peer, col), device_id_type=MESH)
        return carry

    lax.fori_loop(1, n, greet, 0)
    pl.semaphore_wait(barrier, n - 1)

    def copy(peer, slot):
        return pltpu.make_async_remote_copy(
            src_ref=src_ref,
            dst_ref=out_ref.at[pl.ds(slot * per_piece, per_piece)],
            send_sem=send_sem.at[peer],
            recv_sem=recv_sem.at[slot],
            device_id=(peer, col),
            device_id_type=MESH,
        )

    def start(k, carry):
        copy(lax.rem(me + k, n), me).start()
        return carry

    lax.fori_loop(1, n, start, 0)
    out_ref[pl.ds(me * per_piece, per_piece)] = src_ref[...]
    out_ref[n * per_piece] = jnp.zeros(out_ref.shape[1:], out_ref.dtype)

    rows = 128

    def shape_tiles(g, carry):
        at = pl.ds(pl.multiple_of(g * rows, rows), rows)
        tiles_ref[at] = adj_ref[at].reshape((rows,) + tiles_ref.shape[1:])
        return carry

    lax.fori_loop(0, adj_ref.shape[0] // rows, shape_tiles, 0)

    def finish(k, carry):
        sender = lax.rem(me + n - k, n)
        copy(sender, sender).wait_recv()
        copy(lax.rem(me + k, n), me).wait_send()
        return carry

    lax.fori_loop(1, n, finish, 0)


def row_all_gather(features, scale, adj_flat):
    n = lax.axis_size("row")
    nodes_dev, feat_width = features.shape[0] * TILE, features.shape[2]
    per_piece = nodes_dev // TILE
    vmem = pl.BlockSpec(memory_space=pltpu.VMEM)
    return pl.pallas_call(
        functools.partial(all_gather_kernel, n),
        out_shape=(
            jax.ShapeDtypeStruct((n * per_piece + 1, TILE, feat_width), jnp.bfloat16),
            jax.ShapeDtypeStruct((adj_flat.shape[0], TILE, TILE), adj_flat.dtype),
        ),
        in_specs=[vmem, vmem, vmem],
        out_specs=(vmem, vmem),
        scratch_shapes=[
            pltpu.VMEM((per_piece, TILE, feat_width), jnp.bfloat16),
            pltpu.SemaphoreType.DMA((n,)),
            pltpu.SemaphoreType.DMA((n,)),
        ],
        compiler_params=pltpu.CompilerParams(collective_id=1, has_side_effects=True),
    )(features, scale, adj_flat)


def block_product_kernel(group, rows_ref, cols_ref, adj_ref, panel_ref,
                         pieces_ref):
    pieces_ref[...] = jnp.zeros_like(pieces_ref)
    slots = adj_ref.shape[0]

    def body(g, carry):
        base = g * group
        prods = []
        for i in range(group):
            t = base + i
            p = jnp.dot(adj_ref[t], panel_ref[cols_ref[t]], preferred_element_type=jnp.float32)
            prods.append(p)
        for i in range(group):
            slot = rows_ref[base + i]
            pieces_ref[slot] += prods[i]
        return carry

    lax.fori_loop(0, slots // group, body, 0)


def block_product(row_ids, col_ids, dev_tiles, col_panel, row_tiles):
    slots = dev_tiles.shape[0]
    feat_width = col_panel.shape[2]
    group = 16 if slots % 16 == 0 else 1
    smem = pl.BlockSpec(memory_space=pltpu.SMEM)
    vmem = pl.BlockSpec(memory_space=pltpu.VMEM)
    return pl.pallas_call(
        functools.partial(block_product_kernel, group),
        out_shape=jax.ShapeDtypeStruct((row_tiles, TILE, feat_width), jnp.float32),
        in_specs=[smem, smem, vmem, vmem],
        out_specs=vmem,
        cost_estimate=pl.CostEstimate(
            flops=2 * slots * TILE * TILE * feat_width,
            bytes_accessed=slots * TILE * TILE * 2 + row_tiles * TILE * feat_width * 4,
            transcendentals=0,
        ),
    )(row_ids, col_ids, dev_tiles, col_panel)


def shards(features, degrees, adj_tiles, tile_rows, tile_cols, tile_counts):
    col_count = lax.axis_size("col")
    nodes_dev = features.shape[0]
    feat_width = features.shape[1]
    tile_slots = adj_tiles.shape[2]
    row_ids_all = tile_rows.reshape(tile_slots)
    live = jnp.arange(tile_slots, dtype=jnp.int32) < tile_counts.reshape(())
    panel_tiles = lax.axis_size("row") * (nodes_dev // TILE)
    col_ids_all = jnp.where(live, tile_cols.reshape(tile_slots), panel_tiles)
    row_tiles = nodes_dev * col_count // TILE
    norm_scale = jnp.sqrt(KNN / degrees.astype(jnp.float32))[:, None]
    scale = jnp.broadcast_to(norm_scale, features.shape).reshape(-1, TILE, feat_width)
    features = features.reshape(-1, TILE, feat_width)
    gathered, dev_tiles = row_all_gather(features, scale, adj_tiles.reshape(tile_slots, TILE * TILE))
    per_piece = nodes_dev // TILE
    n_y = col_count // (CORES * Z_RING)
    piece_j = row_ids_all // per_piece
    row_slots = (((piece_j % CORES) * Z_RING + (piece_j // CORES) % Z_RING) * n_y
                 + piece_j // (CORES * Z_RING)) * per_piece + row_ids_all % per_piece
    for repeat in range(STEPS):
        pieces = block_product(row_slots, col_ids_all, dev_tiles, gathered, row_tiles)
        gathered = col_reduce_scatter(
            pieces.reshape(CORES, Z_RING, -1, nodes_dev, feat_width),
            scale, features, repeat == STEPS - 1,
        )
    return gathered.astype(jnp.bfloat16)


def solution(mesh):
    return jax.shard_map(
        shards,
        mesh=mesh,
        in_specs=(
            P(("row", "col"), None),
            P(("row", "col")),
            P("row", "col", None, None),
            P("row", "col", None),
            P("row", "col", None),
            P("row", "col"),
        ),
        out_specs=P(("row", "col"), None),
        check_vma=False,
    )
```
